256 devices in a mesh: dp: 4 (over x), space: 64 (over y, z, core).
Axes of the slice: x: 4, y: 4, z: 8, core: 2. Of those that a mesh axis runs over, the one named last changes fastest.
Arguments:
- volume: bfloat16 [4, 128, 128, 16, 256], P('dp', None, 'space'), may hold values from -6 to 6
- w_first: bfloat16 [3, 3, 3, 128, 256], replicated, may hold values from -0.109375 to 0.109375
- w_second: bfloat16 [3, 3, 3, 256, 512], P(None, None, None, 'space'), may hold values from -0.078125 to 0.078125
- cotangent: bfloat16 [4, 512, 32, 256], P('dp', 'space'), may hold values from -6 to 6
Outputs:
- grad_second: float32 [3, 3, 3, 256, 512], P(None, None, None, 'space')
- pre_grad: bfloat16 [4, 256, 64, 4, 256], P('dp', None, 'space')
The draws below stay inside these ranges and needn't reach their ends.
All inputs are finite; a program needn't handle non-finite values.
Results may differ from the reference program's by a relative error of at most 0.0049.
Values may be sent and summed in bfloat16 or wider, within the bound.
No kernel may reach another device: no remote copies, remote signals or barrier semaphores. Data moves between devices by JAX's collectives and lax.ppermute only.
A program may use at most 128 MiB of HBM per device.

```python
import jax
import jax.numpy as jnp
from jax import lax

C1 = 128
C2 = 256
C3 = 512
HGT = 32
WID = 128
SAMPLES = 4
D1 = 128
N_SPACE = 64


def block_levels(own_key, dims, split, smallest, largest):
    def one(axis_at, blocks):
        draws = jax.random.uniform(jax.random.fold_in(jax.random.fold_in(own_key, 6), axis_at), (blocks,), jnp.float32, smallest / len(split), largest / len(split))
        return jnp.repeat(jnp.exp(draws), dims[axis_at] // blocks).reshape((-1,) + (1,) * (len(dims) - axis_at - 1))

    loudness = one(*split[0])
    for cut in split[1:]:
        loudness = loudness * one(*cut)
    return loudness


def centred(own_key, dims, scale, most, pieces=(), held_as=jnp.bfloat16):
    loudness = block_levels(own_key, dims, pieces, -0.22, 0.18) if pieces else 1.0
    entries = jax.random.normal(own_key, dims, jnp.float32) * scale * loudness
    return jnp.minimum(jnp.maximum(entries, -most), most).astype(held_as)


def setup_inputs(seed: int = 0) -> dict:
    seeds = jax.random.split(jax.random.key(seed), 5)
    volume = centred(seeds[0], (SAMPLES, C1, D1, 16, (HGT // 4) * (WID // 4)), 1.0, 6.0, ((0, 4), (2, 64)))
    w_first = centred(seeds[1], (3, 3, 3, C1, C2), (27 * C1) ** -0.5, 0.109375)
    w_second = centred(seeds[2], (3, 3, 3, C2, C3), (27 * C2) ** -0.5, 0.078125, ((3, 64),))
    cotangent = centred(seeds[3], (SAMPLES, C3, D1 // 4, (HGT // 4) * (WID // 4)), 1.0, 6.0, ((0, 4), (1, 64)))
    return {"volume": volume, "w_first": w_first, "w_second": w_second, "cotangent": cotangent}


leak_slope = 0.3

def activate(values):
    return leak_slope * values + (1.0 - leak_slope) * values * jax.nn.sigmoid(values)

def slope_of(values):
    sigmoid_value = jax.nn.sigmoid(values)
    return leak_slope + (1.0 - leak_slope) * (sigmoid_value + values * sigmoid_value * (1.0 - sigmoid_value))

def stride_taps(values, along_dim):
    length = values.shape[along_dim] // 2
    paired = values.reshape(values.shape[:along_dim] + (length, 2) + values.shape[along_dim + 1:])
    even_cells = lax.index_in_dim(paired, 0, along_dim + 1, keepdims=False)
    odd_cells = lax.index_in_dim(paired, 1, along_dim + 1, keepdims=False)
    before = jnp.concatenate([jnp.zeros_like(lax.slice_in_dim(odd_cells, 0, 1, axis=along_dim)), lax.slice_in_dim(odd_cells, 0, length - 1, axis=along_dim)], along_dim)
    return [before, even_cells, odd_cells]

def step_cells(values, by_row, by_col, row_len):
    cells = values.shape[-1]
    if by_row:
        filler = jnp.zeros(values.shape[:-1] + (row_len,), values.dtype)
        values = jnp.concatenate([filler, values[..., :cells - row_len]], -1)
    if by_col:
        filler = jnp.zeros(values.shape[:-1] + (1,), values.dtype)
        moved = jnp.concatenate([filler, values[..., :cells - 1]], -1)
        keeper = lax.iota(jnp.int32, cells) % row_len != 0
        values = jnp.where(keeper, moved, jnp.zeros_like(moved))
    return values

def plane_taps(values, row_len):
    phases = values.shape[-2]
    out_phases = phases // 2
    collected = []
    for row_tap in range(3):
        for col_tap in range(3):
            rows_out = []
            for row_phase in range(out_phases):
                cols_out = []
                for col_phase in range(out_phases):
                    row_at = 2 * row_phase + row_tap - 1
                    col_at = 2 * col_phase + col_tap - 1
                    part = values[..., row_at % phases, col_at % phases, :]
                    cols_out.append(step_cells(part, row_at < 0, col_at < 0, row_len))
                rows_out.append(jnp.stack(cols_out, -2))
            collected.append(jnp.stack(rows_out, -3))
    return collected

def all_taps(values, row_len):
    collected = []
    for depth_part in stride_taps(values, 1):
        collected.extend(plane_taps(depth_part, row_len))
    return collected

def contract_first(left_side, right_side):
    return lax.dot_general(left_side, right_side, (((0,), (0,)), ((), ())), preferred_element_type=jnp.float32)

def contract_last(left_side, right_side):
    return lax.dot_general(left_side, right_side, (((1,), (1,)), ((), ())), preferred_element_type=jnp.float32)

def reference(volume, w_first, w_second, cotangent):
    group_size = C2 // N_SPACE
    row_len = WID // 4
    cell_count = HGT // 4 * (WID // 4)

    def one_sample(inputs):
        volume_one, cot_one = inputs
        volume_cells = volume_one.reshape(C1, D1, 4, 4, cell_count)
        stacked = jnp.stack(all_taps(volume_cells, row_len), 0).reshape(27 * C1, -1)
        pre_act = contract_first(w_first.reshape(27 * C1, C2), stacked)
        hidden = activate(pre_act).astype(jnp.bfloat16).reshape(C2, D1 // 2, 2, 2, cell_count)
        cot_flat = cot_one.reshape(C3, -1)

        def per_group(group_index):
            block_cells = lax.dynamic_slice_in_dim(hidden, group_index * group_size, group_size, 0)
            block_taps = jnp.stack(all_taps(block_cells, row_len), 0).reshape(27 * group_size, -1)
            weight_grad = contract_last(block_taps, cot_flat)
            weight_rows = lax.dynamic_slice_in_dim(w_second, group_index * group_size, group_size, 3).reshape(27 * group_size, C3)
            tap_terms = jnp.dot(weight_rows, cot_flat, preferred_element_type=jnp.float32)

            def spread(field):
                return jnp.stack(all_taps(field, row_len), 0).reshape(27 * group_size, -1)
            unused, pull = jax.vjp(spread, jnp.zeros((group_size, D1 // 2, 2, 2, cell_count), jnp.float32))
            back_terms = pull(tap_terms)[0]
            return (weight_grad, back_terms)
        grad_blocks, back_blocks = lax.map(per_group, jnp.arange(N_SPACE, dtype=jnp.int32))
        grad_full = grad_blocks.reshape(N_SPACE, 3, 3, 3, group_size, C3).transpose(1, 2, 3, 0, 4, 5).reshape(3, 3, 3, C2, C3)
        hidden_grad = back_blocks.reshape(C2, D1 // 2, 4, cell_count).astype(jnp.bfloat16)
        hidden_grad = lax.optimization_barrier(hidden_grad)
        slopes = slope_of(pre_act.reshape(C2, D1 // 2, 4, cell_count))
        result = (hidden_grad.astype(jnp.float32) * slopes).astype(jnp.bfloat16)
        return (grad_full, result)
    grad_samples, pre_grad = lax.map(one_sample, (volume, cotangent))
    grad_second = lax.optimization_barrier(jnp.sum(grad_samples, 0))
    return (grad_second, pre_grad)
```

```python
import functools

import jax
import jax.numpy as jnp
from jax import lax
from jax.experimental import pallas as pl
from jax.experimental.pallas import tpu as pltpu
from jax.sharding import PartitionSpec as P

C3 = 512
WID = 128


leak_slope = 0.3


def from_behind(block, axis, distance):
    devices = range(lax.axis_size(axis))
    route = [(i - distance, i) for i in devices if i - distance in devices]
    return lax.ppermute(block, axis, route)


def from_side(block, axis, distance):
    size = lax.axis_size(axis)
    return lax.ppermute(block, axis, [(i, (i + distance) % size) for i in range(size)])


def activate(values):
    return leak_slope * values + (1.0 - leak_slope) * values * jax.nn.sigmoid(values)


def slope_of(values):
    sigmoid_value = jax.nn.sigmoid(values)
    return leak_slope + (1.0 - leak_slope) * (
        sigmoid_value + values * sigmoid_value * (1.0 - sigmoid_value)
    )


def shifted(block, by_row, by_col, row_len):
    moved = block.astype(jnp.float32)
    lane = lax.broadcasted_iota(jnp.int32, moved.shape, 1)
    moved = pltpu.roll(moved, by_row * row_len + by_col, 1)
    keep = None
    if by_row:
        keep = lane >= row_len
    if by_col:
        inner = lane % row_len != 0
        keep = inner if keep is None else jnp.logical_and(keep, inner)
    return jnp.where(keep, moved, 0.0).astype(block.dtype)


def conv_kernel(taps_of_plane, channels, row_len, w_ref, *refs):
    planes = refs[: len(taps_of_plane)]
    out_ref = refs[len(taps_of_plane)]
    cols_ref = refs[len(taps_of_plane) + 1]
    tap_rows = 9 * channels
    for at, plane in enumerate(planes):
        for row in range(-1, 4):
            for col in range(-1, 4):
                source = ((row % 4) * 4 + col % 4) * channels
                block = plane[source : source + channels, :]
                if row < 0 or col < 0:
                    block = shifted(block, int(row < 0), int(col < 0), row_len)
                for row_phase in range(2):
                    row_tap = row + 1 - 2 * row_phase
                    if not 0 <= row_tap <= 2:
                        continue
                    for col_phase in range(2):
                        col_tap = col + 1 - 2 * col_phase
                        if not 0 <= col_tap <= 2:
                            continue
                        start = at * tap_rows + (row_tap * 3 + col_tap) * channels
                        cols_ref[row_phase * 2 + col_phase, start : start + channels, :] = block
    for phase in range(4):
        out_ref[phase, :, :] = jnp.dot(
            w_ref[...], cols_ref[phase], preferred_element_type=jnp.float32
        ).astype(out_ref.dtype)


def conv(w_rows, planes, dtype, row_len):
    out_channels, depth = w_rows.shape
    count = len(planes)
    channels = depth // (9 * count)
    cells = planes[0].shape[1]
    return pl.pallas_call(
        functools.partial(conv_kernel, tuple(range(count)), channels, row_len),
        out_shape=jax.ShapeDtypeStruct((4, out_channels, cells), dtype),
        scratch_shapes=[pltpu.VMEM((4, depth, cells), jnp.bfloat16)],
        cost_estimate=pl.CostEstimate(
            flops=8 * out_channels * depth * cells, bytes_accessed=8 * depth * cells, transcendentals=0
        ),
    )(w_rows, *planes)


def spread(block, row_len):
    return jnp.concatenate(
        [block]
        + [shifted(block, by_row, by_col, row_len) for by_row, by_col in ((0, 1), (1, 0), (1, 1))],
        0,
    )


def gather_back(terms, row_len):
    rows = terms.shape[0] // 4
    lane = lax.broadcasted_iota(jnp.int32, (rows, terms.shape[1]), 1)
    cells = terms.shape[1]
    total = terms[:rows]
    for at, (by_row, by_col) in ((1, (0, 1)), (2, (1, 0)), (3, (1, 1))):
        moved = pltpu.roll(terms[at * rows : (at + 1) * rows], cells - by_row * row_len - by_col, 1)
        keep = lane < cells - row_len if by_row else None
        if by_col:
            inner = lane % row_len != row_len - 1
            keep = inner if keep is None else jnp.logical_and(keep, inner)
        total = total + jnp.where(keep, moved, 0.0)
    return total


def grad_kernel(row_len, hidden_ref, cot_ref, out_ref, rows_ref):
    planes, group, cells = hidden_ref.shape
    steps = planes // 2
    size = 4 * group
    rows_ref[0:size, 0:cells] = jnp.zeros((size, cells), rows_ref.dtype)

    def fill(s, carry):
        here = pl.ds(pl.multiple_of(s * cells, cells), cells)
        rows_ref[size : 2 * size, here] = spread(hidden_ref[2 * s], row_len)
        odd = spread(hidden_ref[2 * s + 1], row_len)
        rows_ref[2 * size : 3 * size, here] = odd

        @pl.when(s + 1 < steps)
        def _():
            rows_ref[0:size, pl.ds(pl.multiple_of((s + 1) * cells, cells), cells)] = odd

        return carry

    lax.fori_loop(0, steps, fill, 0)
    total = lax.dot_general(
        rows_ref[...], cot_ref[...], (((1,), (1,)), ((), ())), preferred_element_type=jnp.float32
    )
    own = group // 4
    for depth_tap in range(3):
        for row_tap in range(3):
            for col_tap in range(3):
                start = (
                    depth_tap * size
                    + (2 * int(row_tap == 0) + int(col_tap == 0)) * group
                    + (2 * int(row_tap != 1) + int(col_tap != 1)) * own
                )
                put = ((depth_tap * 3 + row_tap) * 3 + col_tap) * own
                out_ref[put : put + own, :] = total[start : start + own, :].astype(out_ref.dtype)


def grad(hidden, cot, dtype, row_len):
    planes, group, cells = hidden.shape
    outs = cot.shape[0]
    return pl.pallas_call(
        functools.partial(grad_kernel, row_len),
        out_shape=jax.ShapeDtypeStruct((27 * group // 4, outs), dtype),
        scratch_shapes=[pltpu.VMEM((12 * group, planes // 2 * cells), jnp.bfloat16)],
        cost_estimate=pl.CostEstimate(
            flops=12 * group * outs * planes * cells, bytes_accessed=2 * cot.size, transcendentals=0
        ),
    )(hidden, cot)


def back_kernel(row_len, w_ref, cot_ref, out_ref, terms_ref):
    planes, group, cells = out_ref.shape
    steps = planes // 2
    size = 4 * group

    def multiply(s, carry):
        here = pl.ds(pl.multiple_of(s * cells, cells), cells)
        terms_ref[:, here] = jnp.dot(
            w_ref[...], cot_ref[:, here], preferred_element_type=jnp.float32
        )
        return carry

    lax.fori_loop(0, steps, multiply, 0)

    def combine(s, carry):
        here = pl.ds(pl.multiple_of(s * cells, cells), cells)
        out_ref[2 * s] = gather_back(terms_ref[size : 2 * size, here], row_len).astype(out_ref.dtype)
        after = jnp.minimum(s + 1, steps - 1)
        next_one = pl.ds(pl.multiple_of(after * cells, cells), cells)
        extra = jnp.where(s + 1 < steps, terms_ref[0:size, next_one], 0.0)
        odd = terms_ref[2 * size : 3 * size, here] + extra
        out_ref[2 * s + 1] = gather_back(odd, row_len).astype(out_ref.dtype)
        return carry

    lax.fori_loop(0, steps, combine, 0)


def back(w_rows, cot, planes, row_len):
    rows, outs = w_rows.shape
    group = rows // 12
    cells = 2 * cot.shape[1] // planes
    return pl.pallas_call(
        functools.partial(back_kernel, row_len),
        out_shape=jax.ShapeDtypeStruct((planes, group, cells), jnp.bfloat16),
        scratch_shapes=[pltpu.VMEM((rows, cot.shape[1]), jnp.float32)],
        cost_estimate=pl.CostEstimate(
            flops=2 * rows * cot.size, bytes_accessed=2 * cot.size, transcendentals=0
        ),
    )(w_rows, cot)


def move_rows(w_second):
    nothing = jnp.zeros_like(w_second[:, 0])

    def halves(taps, gap):
        return [[taps[1], taps[2]], [gap, taps[0]]]

    by_row = halves([w_second[:, b] for b in range(3)], nothing)
    moved_rows = []
    for row in by_row:
        for_phase = []
        for part in row:
            by_col = halves([part[:, c] for c in range(3)], jnp.zeros_like(part[:, 0]))
            for_phase.append(jnp.stack([jnp.stack(col, 1) for col in by_col], 1))
        moved_rows.append(jnp.stack(for_phase, 2))
    rows = jnp.stack(moved_rows, 1)
    return rows.reshape(-1, w_second.shape[-1])


def per_device(volume, w_first, w_second, cotangent):
    channels = volume.shape[1]
    cell_count = volume.shape[4]
    out_channels = w_first.shape[4]
    row_len = WID // 4
    members = lax.axis_size("space")
    own_channels = out_channels // members
    planes = volume[0].reshape(channels, 2, 16, cell_count).transpose(1, 2, 0, 3)
    planes = planes.reshape(2, 16 * channels, cell_count)
    w_rows = w_first.reshape(27 * channels, out_channels)
    w_before = w_rows[: 9 * channels].T
    w_here = w_rows[9 * channels :].T
    ahead = conv(w_before, [planes[1]], jnp.bfloat16, row_len)
    behind = from_behind(ahead, "space", 1)
    gathered = lax.all_gather(cotangent[0], "space", axis=0, tiled=True)
    cot_flat = gathered.reshape(C3, -1)
    pre_act = conv(w_here, [planes[0], planes[1]], jnp.float32, row_len)
    pre_act = pre_act + behind.astype(jnp.float32)
    hidden = activate(pre_act).astype(jnp.bfloat16)
    blocks = hidden.reshape(4, members, own_channels, cell_count).transpose(1, 0, 2, 3)
    blocks = blocks.reshape(members, 4 * own_channels, cell_count)
    by_plane = lax.all_to_all(blocks, "space", split_axis=0, concat_axis=0, tiled=True)
    back_terms = back(move_rows(w_second), cot_flat, members, row_len)
    hidden_grad = lax.all_to_all(back_terms, "space", split_axis=0, concat_axis=0, tiled=True)
    partial = grad(by_plane, cot_flat, jnp.bfloat16, row_len)
    sides = [from_side(partial, "dp", distance) for distance in (1, 2, 3)]
    left, opposite, right = [side.astype(jnp.float32) for side in sides]
    grad_second = (partial.astype(jnp.float32) + opposite) + (left + right)
    grad_second = grad_second.reshape(3, 3, 3, own_channels, C3)
    hidden_grad = hidden_grad.reshape(members, 4, own_channels, cell_count).transpose(0, 2, 1, 3)
    hidden_grad = hidden_grad.reshape(out_channels, 4, cell_count).astype(jnp.float32)
    slopes = slope_of(pre_act.transpose(1, 0, 2))
    pre_grad = (hidden_grad * slopes).astype(jnp.bfloat16)
    return (grad_second, pre_grad[None, :, None])


def solution(mesh):
    in_specs = (
        P("dp", None, "space", None, None),
        P(),
        P(None, None, None, "space", None),
        P("dp", "space", None, None),
    )
    out_specs = (P(None, None, None, "space", None), P("dp", None, "space", None, None))
    return jax.shard_map(
        per_device, mesh=mesh, in_specs=in_specs, out_specs=out_specs, check_vma=False
    )
```

```python
import functools

import jax
import jax.numpy as jnp
from jax import lax
from jax.experimental import pallas as pl
from jax.experimental.pallas import tpu as pltpu
from jax.sharding import PartitionSpec as P

C3 = 512
WID = 128


leak_slope = 0.3


def from_behind(block, axis, distance):
    devices = range(lax.axis_size(axis))
    route = [(i - distance, i) for i in devices if i - distance in devices]
    return lax.ppermute(block, axis, route)


def from_side(block, axis, distance):
    size = lax.axis_size(axis)
    return lax.ppermute(block, axis, [(i, (i + distance) % size) for i in range(size)])


def activate(values):
    return leak_slope * values + (1.0 - leak_slope) * values * jax.nn.sigmoid(values)


def slope_of(values):
    sigmoid_value = jax.nn.sigmoid(values)
    return leak_slope + (1.0 - leak_slope) * (
        sigmoid_value + values * sigmoid_value * (1.0 - sigmoid_value)
    )


def shifted(block, by_row, by_col, row_len):
    moved = block.astype(jnp.float32)
    lane = lax.broadcasted_iota(jnp.int32, moved.shape, 1)
    moved = pltpu.roll(moved, by_row * row_len + by_col, 1)
    keep = None
    if by_row:
        keep = lane >= row_len
    if by_col:
        inner = lane % row_len != 0
        keep = inner if keep is None else jnp.logical_and(keep, inner)
    return jnp.where(keep, moved, 0.0).astype(block.dtype)


def conv_kernel(taps_of_plane, channels, row_len, w_ref, *refs):
    planes = refs[: len(taps_of_plane)]
    out_ref = refs[len(taps_of_plane)]
    cols_ref = refs[len(taps_of_plane) + 1]
    tap_rows = 9 * channels
    for at, plane in enumerate(planes):
        for row in range(-1, 4):
            for col in range(-1, 4):
                source = ((row % 4) * 4 + col % 4) * channels
                block = plane[source : source + channels, :]
                if row < 0 or col < 0:
                    block = shifted(block, int(row < 0), int(col < 0), row_len)
                for row_phase in range(2):
                    row_tap = row + 1 - 2 * row_phase
                    if not 0 <= row_tap <= 2:
                        continue
                    for col_phase in range(2):
                        col_tap = col + 1 - 2 * col_phase
                        if not 0 <= col_tap <= 2:
                            continue
                        start = at * tap_rows + (row_tap * 3 + col_tap) * channels
                        cols_ref[row_phase * 2 + col_phase, start : start + channels, :] = block
    for phase in range(4):
        out_ref[phase, :, :] = jnp.dot(
            w_ref[...], cols_ref[phase], preferred_element_type=jnp.float32
        ).astype(out_ref.dtype)


def conv(w_rows, planes, dtype, row_len):
    out_channels, depth = w_rows.shape
    count = len(planes)
    channels = depth // (9 * count)
    cells = planes[0].shape[1]
    return pl.pallas_call(
        functools.partial(conv_kernel, tuple(range(count)), channels, row_len),
        out_shape=jax.ShapeDtypeStruct((4, out_channels, cells), dtype),
        scratch_shapes=[pltpu.VMEM((4, depth, cells), jnp.bfloat16)],
        cost_estimate=pl.CostEstimate(
            flops=8 * out_channels * depth * cells, bytes_accessed=8 * depth * cells, transcendentals=0
        ),
    )(w_rows, *planes)


def spread(block, row_len):
    return jnp.concatenate(
        [block]
        + [shifted(block, by_row, by_col, row_len) for by_row, by_col in ((0, 1), (1, 0), (1, 1))],
        0,
    )


def gather_back(terms, row_len):
    rows = terms.shape[0] // 4
    lane = lax.broadcasted_iota(jnp.int32, (rows, terms.shape[1]), 1)
    cells = terms.shape[1]
    total = terms[:rows]
    for at, (by_row, by_col) in ((1, (0, 1)), (2, (1, 0)), (3, (1, 1))):
        moved = pltpu.roll(terms[at * rows : (at + 1) * rows], cells - by_row * row_len - by_col, 1)
        keep = lane < cells - row_len if by_row else None
        if by_col:
            inner = lane % row_len != row_len - 1
            keep = inner if keep is None else jnp.logical_and(keep, inner)
        total = total + jnp.where(keep, moved, 0.0)
    return total


def grad_kernel(row_len, hidden_ref, cot_ref, out_ref, even_ref, odd_ref):
    planes, group, cells = hidden_ref.shape
    steps = planes // 2
    own = group // 4
    for s in range(steps):
        here = slice(s * cells, (s + 1) * cells)
        even_ref[:, here] = spread(hidden_ref[2 * s], row_len)
        odd_ref[:, here] = spread(hidden_ref[2 * s + 1], row_len)
    over_cells = (((1,), (1,)), ((), ()))
    sources = ((odd_ref, cells), (even_ref, 0), (odd_ref, 0))
    for depth_tap, (rows_ref, start) in enumerate(sources):
        total = lax.dot_general(
            rows_ref[...],
            cot_ref[:, start : start + steps * cells],
            over_cells,
            preferred_element_type=jnp.float32,
        )
        for row_tap in range(3):
            for col_tap in range(3):
                at = (2 * int(row_tap == 0) + int(col_tap == 0)) * group
                at += (2 * int(row_tap != 1) + int(col_tap != 1)) * own
                put = (depth_tap * 3 + row_tap) * 3 + col_tap
                out_ref[put] = total[at : at + own, :].astype(out_ref.dtype)


def grad(hidden, cot, dtype, row_len):
    planes, group, cells = hidden.shape
    outs = cot.shape[0]
    rows = pltpu.VMEM((4 * group, planes // 2 * cells), jnp.bfloat16)
    return pl.pallas_call(
        functools.partial(grad_kernel, row_len),
        out_shape=jax.ShapeDtypeStruct((27, group // 4, outs), dtype),
        scratch_shapes=[rows, rows],
        cost_estimate=pl.CostEstimate(
            flops=12 * group * outs * planes * cells, bytes_accessed=2 * cot.size, transcendentals=0
        ),
    )(hidden, cot)


def back_kernel(row_len, place_ref, w_ref, mine_ref, theirs_ref, out_ref, cot_ref):
    planes, group, cells = out_ref.shape
    ring, rows_y, unit, half = mine_ref.shape
    z, core = place_ref[0], place_ref[1]
    here = pl.ds(pl.multiple_of(core * half, 128), half)
    there = pl.ds(pl.multiple_of((1 - core) * half, 128), half)
    for k in range(ring):
        for y in range(rows_y):
            row = y * ring * unit + lax.rem(z + k, ring) * unit
            rows = pl.ds(pl.multiple_of(row, unit), unit)
            cot_ref[rows, here] = mine_ref[k, y]
            cot_ref[rows, there] = theirs_ref[k, y]
    size = 4 * group

    def one(at, start):
        return jnp.dot(
            w_ref[at * size : (at + 1) * size, :],
            cot_ref[:, start : start + cells],
            preferred_element_type=jnp.float32,
        )

    for s in range(planes // 2):
        start = s * cells
        out_ref[2 * s] = gather_back(one(1, start), row_len).astype(out_ref.dtype)
        odd = one(2, start) + one(0, start + cells)
        out_ref[2 * s + 1] = gather_back(odd, row_len).astype(out_ref.dtype)


def back(place, w_rows, mine, theirs, planes, row_len):
    rows, outs = w_rows.shape
    group = rows // 12
    width = 2 * mine.shape[3]
    cells = width // (planes // 2 + 1)
    vmem = pl.BlockSpec(memory_space=pltpu.VMEM)
    return pl.pallas_call(
        functools.partial(back_kernel, row_len),
        out_shape=(
            jax.ShapeDtypeStruct((planes, group, cells), jnp.bfloat16),
            jax.ShapeDtypeStruct((outs, width), jnp.bfloat16),
        ),
        in_specs=[pl.BlockSpec(memory_space=pltpu.SMEM), vmem, vmem, vmem],
        out_specs=(vmem, vmem),
        cost_estimate=pl.CostEstimate(
            flops=rows * outs * planes * cells, bytes_accessed=4 * outs * width, transcendentals=0
        ),
    )(place, w_rows, mine, theirs)


def move_rows(w_second):
    nothing = jnp.zeros_like(w_second[:, 0])

    def halves(taps, gap):
        return [[taps[1], taps[2]], [gap, taps[0]]]

    by_row = halves([w_second[:, b] for b in range(3)], nothing)
    moved_rows = []
    for row in by_row:
        for_phase = []
        for part in row:
            by_col = halves([part[:, c] for c in range(3)], jnp.zeros_like(part[:, 0]))
            for_phase.append(jnp.stack([jnp.stack(col, 1) for col in by_col], 1))
        moved_rows.append(jnp.stack(for_phase, 2))
    rows = jnp.stack(moved_rows, 1)
    return rows.reshape(-1, w_second.shape[-1])


ROWS, RING, CORES = 4, 8, 2


def on_space(block, y_by=0, z_by=0, core_by=0):
    route = []
    for y in range(ROWS):
        for z in range(RING):
            for core in range(CORES):
                to = ((y + y_by) % ROWS, (z + z_by) % RING, (core + core_by) % CORES)
                route.append(((y * RING + z) * CORES + core, (to[0] * RING + to[1]) * CORES + to[2]))
    return lax.ppermute(block, "space", route)


COLUMNS = [[y * RING * CORES + g for y in range(ROWS)] for g in range(RING * CORES)]
SLABS = [[y * RING * CORES + g for g in range(RING * CORES)] for y in range(ROWS)]


def exchange(blocks, groups):
    return lax.all_to_all(
        blocks, "space", split_axis=0, concat_axis=0, axis_index_groups=groups, tiled=True
    )


def per_device(volume, w_first, w_second, cotangent):
    channels = volume.shape[1]
    cells = volume.shape[4]
    out_channels = w_first.shape[4]
    own = w_second.shape[3]
    row_len = WID // 4
    me = lax.axis_index("space")
    core, z = me % CORES, me // CORES % RING
    group = RING * CORES

    depth = cotangent.shape[2]
    share = depth // ROWS
    local = jnp.pad(cotangent[0], ((0, 0), (0, 1), (0, 0)))
    parts = jnp.stack([local[:, y * share : (y + 1) * share + 1] for y in range(ROWS)])
    parts = parts.reshape(ROWS, -1, (share + 1) * cells)
    half = (share + 1) * cells // 2
    low, high = parts[:, :, :half], parts[:, :, half:]
    kept = jnp.where(core == 0, low, high)
    other = on_space(jnp.where(core == 0, high, low), core_by=1)
    unit = jnp.concatenate(
        [jnp.where(core == 0, kept, other), jnp.where(core == 0, other, kept)], 1
    )
    first = exchange(unit, COLUMNS)
    up, down = [first], [first]
    for _ in range(3):
        up.append(on_space(up[-1], z_by=1))
        down.append(on_space(down[-1], z_by=-1))
    far = jnp.concatenate(
        [on_space(up[3][: ROWS // 2], z_by=1), on_space(down[3][ROWS // 2 :], z_by=-1)], 0
    )
    mine = jnp.stack(down + [far] + up[:0:-1])
    theirs = on_space(mine, core_by=1)

    w_all = exchange(jnp.broadcast_to(w_second, (ROWS,) + w_second.shape), COLUMNS)
    w_group = w_all.transpose(1, 2, 3, 0, 4, 5).reshape(3, 3, 3, ROWS * own, C3)

    planes = volume[0].reshape(channels, 2, 16, cells).transpose(1, 2, 0, 3)
    planes = planes.reshape(2, 16 * channels, cells)
    w_rows = w_first.reshape(27 * channels, out_channels)
    w_before = w_rows[: 9 * channels].T
    w_here = w_rows[9 * channels :].T
    ahead = conv(w_before, [planes[1]], jnp.bfloat16, row_len)
    behind = from_behind(ahead, "space", 1)
    pre_act = conv(w_here, [planes[0], planes[1]], jnp.float32, row_len)
    pre_act = pre_act + behind.astype(jnp.float32)
    hidden = activate(pre_act).astype(jnp.bfloat16)
    blocks = hidden.reshape(4, ROWS, group, own, cells).transpose(2, 0, 1, 3, 4)
    by_plane = exchange(blocks.reshape(group, 4 * ROWS * own, cells), SLABS)

    place = jnp.stack([z, core]).astype(jnp.int32)
    back_terms, cot_row = back(place, move_rows(w_group), mine, theirs, group, row_len)
    hidden_grad = exchange(back_terms, SLABS)

    partial = grad(by_plane, cot_row, jnp.bfloat16, row_len)
    partial = partial.reshape(27, ROWS, own, C3).transpose(1, 0, 2, 3).reshape(ROWS, 27 * own, C3)
    partial = jnp.sum(exchange(partial, COLUMNS).astype(jnp.float32), 0).astype(jnp.bfloat16)
    sides = [from_side(partial, "dp", distance) for distance in (1, 2, 3)]
    left, opposite, right = [side.astype(jnp.float32) for side in sides]
    grad_second = (partial.astype(jnp.float32) + opposite) + (left + right)
    grad_second = grad_second.reshape(3, 3, 3, own, C3)

    hidden_grad = hidden_grad.reshape(group, 4, ROWS, own, cells).transpose(2, 0, 3, 1, 4)
    hidden_grad = hidden_grad.reshape(out_channels, 4, cells).astype(jnp.float32)
    slopes = slope_of(pre_act.transpose(1, 0, 2))
    pre_grad = (hidden_grad * slopes).astype(jnp.bfloat16)
    return (grad_second, pre_grad[None, :, None])


def solution(mesh):
    in_specs = (
        P("dp", None, "space", None, None),
        P(),
        P(None, None, None, "space", None),
        P("dp", "space", None, None),
    )
    out_specs = (P(None, None, None, "space", None), P("dp", None, "space", None, None))
    return jax.shard_map(
        per_device, mesh=mesh, in_specs=in_specs, out_specs=out_specs, check_vma=False
    )
```

```python
import functools

import jax
import jax.numpy as jnp
from jax import lax
from jax.experimental import pallas as pl
from jax.experimental.pallas import tpu as pltpu
from jax.sharding import PartitionSpec as P


C3 = 512
WID = 128


leak_slope = 0.3


def from_behind(block, axis, distance):
    devices = range(lax.axis_size(axis))
    route = [(i - distance, i) for i in devices if i - distance in devices]
    return lax.ppermute(block, axis, route)


def from_side(block, axis, distance):
    size = lax.axis_size(axis)
    return lax.ppermute(block, axis, [(i, (i + distance) % size) for i in range(size)])


def shifted(block, by_row, by_col, row_len):
    moved = block.astype(jnp.float32)
    lane = lax.broadcasted_iota(jnp.int32, moved.shape, 1)
    moved = pltpu.roll(moved, by_row * row_len + by_col, 1)
    keep = None
    if by_row:
        keep = lane >= row_len
    if by_col:
        inner = lane % row_len != 0
        keep = inner if keep is None else jnp.logical_and(keep, inner)
    return jnp.where(keep, moved, 0.0).astype(block.dtype)


def conv_kernel(use, channels, row_len, w_ref, planes_ref, out_ref, cols_ref):
    tap_rows = 9 * channels
    for at, (_, plane) in enumerate(use):
        for row in range(-1, 4):
            for col in range(-1, 4):
                source = ((row % 4) * 4 + col % 4) * channels
                block = planes_ref[plane, source : source + channels, :]
                if row < 0 or col < 0:
                    block = shifted(block, int(row < 0), int(col < 0), row_len)
                for row_phase in range(2):
                    row_tap = row + 1 - 2 * row_phase
                    if not 0 <= row_tap <= 2:
                        continue
                    for col_phase in range(2):
                        col_tap = col + 1 - 2 * col_phase
                        if not 0 <= col_tap <= 2:
                            continue
                        start = at * tap_rows + (row_tap * 3 + col_tap) * channels
                        cols_ref[row_phase * 2 + col_phase, start : start + channels, :] = block
    first = use[0][0] * tap_rows
    weights = w_ref[:, first : first + len(use) * tap_rows]
    for phase in range(4):
        out_ref[phase, :, :] = jnp.dot(
            weights, cols_ref[phase], preferred_element_type=jnp.float32
        ).astype(out_ref.dtype)


def conv(w_rows, planes, use, dtype, row_len):
    outs, depth = w_rows.shape
    channels = depth // 27
    cells = planes.shape[2]
    depth = 9 * channels * len(use)
    return pl.pallas_call(
        functools.partial(conv_kernel, use, channels, row_len),
        out_shape=jax.ShapeDtypeStruct((4, outs, cells), dtype),
        scratch_shapes=[pltpu.VMEM((4, depth, cells), jnp.bfloat16)],
        cost_estimate=pl.CostEstimate(
            flops=8 * outs * depth * cells, bytes_accessed=4 * depth * cells, transcendentals=0
        ),
    )(w_rows, planes)


def act_kernel(part_ref, behind_ref, hidden_ref, slope_ref):
    groups, rows, _ = hidden_ref.shape
    unit = rows // 4
    for phase in range(4):
        for at in range(groups):
            here = slice(at * unit, (at + 1) * unit)
            values = part_ref[phase, here, :] + behind_ref[phase, here, :].astype(jnp.float32)
            gate = jax.nn.sigmoid(values)
            there = slice(phase * unit, (phase + 1) * unit)
            gated = (1.0 - leak_slope) * gate
            hidden_ref[at, there, :] = (leak_slope * values + gated * values).astype(
                hidden_ref.dtype
            )
            slope_ref[at, there, :] = leak_slope + gated * (1.0 + values * (1.0 - gate))


def act(part, behind, groups):
    phases, outs, cells = part.shape
    shape = (groups, phases * outs // groups, cells)
    return pl.pallas_call(
        act_kernel,
        out_shape=(
            jax.ShapeDtypeStruct(shape, jnp.bfloat16),
            jax.ShapeDtypeStruct(shape, jnp.float32),
        ),
        cost_estimate=pl.CostEstimate(
            flops=10 * part.size, bytes_accessed=12 * part.size, transcendentals=part.size
        ),
    )(part, behind)


def pile_kernel(*refs):
    for at, ref in enumerate(refs[:-1]):
        refs[-1][at] = ref[...]


def pile(blocks):
    shape = (len(blocks),) + blocks[0].shape
    return pl.pallas_call(
        pile_kernel,
        out_shape=jax.ShapeDtypeStruct(shape, blocks[0].dtype),
        cost_estimate=pl.CostEstimate(
            flops=0, bytes_accessed=4 * len(blocks) * blocks[0].size, transcendentals=0
        ),
    )(*blocks)


def spread(block, row_len):
    return jnp.concatenate(
        [block]
        + [shifted(block, by_row, by_col, row_len) for by_row, by_col in ((0, 1), (1, 0), (1, 1))],
        0,
    )


def gather_back(terms, row_len):
    rows = terms.shape[0] // 4
    lane = lax.broadcasted_iota(jnp.int32, (rows, terms.shape[1]), 1)
    cells = terms.shape[1]
    total = terms[:rows]
    for at, (by_row, by_col) in ((1, (0, 1)), (2, (1, 0)), (3, (1, 1))):
        moved = pltpu.roll(terms[at * rows : (at + 1) * rows], cells - by_row * row_len - by_col, 1)
        keep = lane < cells - row_len if by_row else None
        if by_col:
            inner = lane % row_len != row_len - 1
            keep = inner if keep is None else jnp.logical_and(keep, inner)
        total = total + jnp.where(keep, moved, 0.0)
    return total


def grad_kernel(row_len, place_ref, hidden_ref, cot_ref, *refs):
    outs_refs, (even_ref, odd_ref, sum_ref) = refs[:-3], refs[-3:]
    planes, group, cells = hidden_ref.shape
    steps = planes // 2
    own = group // 4
    unit = own // len(outs_refs)
    for s in range(steps):
        here = slice(s * cells, (s + 1) * cells)
        even_ref[:, here] = spread(hidden_ref[2 * s], row_len)
        odd_ref[:, here] = spread(hidden_ref[2 * s + 1], row_len)
    over_cells = (((1,), (1,)), ((), ()))
    sources = ((odd_ref, cells), (even_ref, 0), (odd_ref, 0))
    for depth_tap, (rows_ref, start) in enumerate(sources):
        total = lax.dot_general(
            rows_ref[...],
            cot_ref[:, start : start + steps * cells],
            over_cells,
            preferred_element_type=jnp.float32,
        )
        for row_tap in range(3):
            for col_tap in range(3):
                at = (2 * int(row_tap == 0) + int(col_tap == 0)) * group
                at += (2 * int(row_tap != 1) + int(col_tap != 1)) * own
                put = ((depth_tap * 3 + row_tap) * 3 + col_tap) * unit
                for y in range(len(outs_refs)):
                    first = at + y * unit
                    sum_ref[y, put : put + unit, :] = total[first : first + unit, :]
    for away, out_ref in enumerate(outs_refs):
        y = lax.rem(place_ref[0] + away, len(outs_refs))
        out_ref[...] = sum_ref[y].astype(out_ref.dtype)


def grad(place, hidden, cot, row_count, row_len):
    planes, group, cells = hidden.shape
    outs = cot.shape[0]
    rows = pltpu.VMEM((4 * group, planes // 2 * cells), jnp.bfloat16)
    size = 27 * group // (4 * row_count)
    vmem = pl.BlockSpec(memory_space=pltpu.VMEM)
    return pl.pallas_call(
        functools.partial(grad_kernel, row_len),
        out_shape=[
            jax.ShapeDtypeStruct((size, outs), jnp.bfloat16 if away else jnp.float32)
            for away in range(row_count)
        ],
        in_specs=[pl.BlockSpec(memory_space=pltpu.SMEM), vmem, vmem],
        out_specs=[vmem] * row_count,
        scratch_shapes=[rows, rows, pltpu.VMEM((row_count, size, outs), jnp.float32)],
        cost_estimate=pl.CostEstimate(
            flops=12 * group * outs * planes * cells, bytes_accessed=2 * cot.size, transcendentals=0
        ),
    )(place, hidden, cot)


def back_kernel(row_len, place_ref, w_ref, mine_ref, theirs_ref, out_ref, cot_ref):
    planes, group, cells = out_ref.shape
    ring, rows_y, unit, half = mine_ref.shape
    z, core = place_ref[1], place_ref[2]
    here = pl.ds(pl.multiple_of(core * half, 128), half)
    there = pl.ds(pl.multiple_of((1 - core) * half, 128), half)
    for k in range(ring):
        for y in range(rows_y):
            row = y * ring * unit + lax.rem(z + k, ring) * unit
            rows = pl.ds(pl.multiple_of(row, unit), unit)
            cot_ref[rows, here] = mine_ref[k, y]
            cot_ref[rows, there] = theirs_ref[k, y]
    size = 4 * group

    def one(at, start):
        return jnp.dot(
            w_ref[at * size : (at + 1) * size, :],
            cot_ref[:, start : start + cells],
            preferred_element_type=jnp.float32,
        )

    for s in range(planes // 2):
        start = s * cells
        out_ref[2 * s] = gather_back(one(1, start), row_len).astype(out_ref.dtype)
        odd = one(2, start) + one(0, start + cells)
        out_ref[2 * s + 1] = gather_back(odd, row_len).astype(out_ref.dtype)


def back(place, w_rows, mine, theirs, planes, row_len):
    rows, outs = w_rows.shape
    group = rows // 12
    width = 2 * mine.shape[3]
    cells = width // (planes // 2 + 1)
    vmem = pl.BlockSpec(memory_space=pltpu.VMEM)
    return pl.pallas_call(
        functools.partial(back_kernel, row_len),
        out_shape=(
            jax.ShapeDtypeStruct((planes, group, cells), jnp.bfloat16),
            jax.ShapeDtypeStruct((outs, width), jnp.bfloat16),
        ),
        in_specs=[pl.BlockSpec(memory_space=pltpu.SMEM), vmem, vmem, vmem],
        out_specs=(vmem, vmem),
        cost_estimate=pl.CostEstimate(
            flops=rows * outs * planes * cells, bytes_accessed=4 * outs * width, transcendentals=0
        ),
    )(place, w_rows, mine, theirs)


def move_rows(w_second):
    nothing = jnp.zeros_like(w_second[:, 0])

    def halves(taps, gap):
        return [[taps[1], taps[2]], [gap, taps[0]]]

    by_row = halves([w_second[:, b] for b in range(3)], nothing)
    moved_rows = []
    for row in by_row:
        for_phase = []
        for part in row:
            by_col = halves([part[:, c] for c in range(3)], jnp.zeros_like(part[:, 0]))
            for_phase.append(jnp.stack([jnp.stack(col, 1) for col in by_col], 1))
        moved_rows.append(jnp.stack(for_phase, 2))
    rows = jnp.stack(moved_rows, 1)
    return rows.reshape(-1, w_second.shape[-1])


ROWS, RING, CORES = 4, 8, 2


def on_space(block, y_by=0, z_by=0, core_by=0):
    route = []
    for y in range(ROWS):
        for z in range(RING):
            for core in range(CORES):
                to = ((y + y_by) % ROWS, (z + z_by) % RING, (core + core_by) % CORES)
                route.append(((y * RING + z) * CORES + core, (to[0] * RING + to[1]) * CORES + to[2]))
    return lax.ppermute(block, "space", route)


CHIPS = [(y, z) for y in range(ROWS) for z in range(RING)]


def members(pick):
    groups = {}
    for y, z in CHIPS:
        for core in range(CORES):
            groups.setdefault(pick(y, z, core), []).append((y * RING + z) * CORES + core)
    return list(groups.values())


COLUMNS = members(lambda y, z, core: (z, core))
PILLARS = members(lambda y, z, core: z)
SLABS = members(lambda y, z, core: y)


def exchange(blocks, groups):
    return lax.all_to_all(
        blocks, "space", split_axis=0, concat_axis=0, axis_index_groups=groups, tiled=True
    )


def section(volume, w_first, w_second, cotangent):
    channels = volume.shape[1]
    cells = volume.shape[4]
    outs = w_first.shape[4]
    own = w_second.shape[3]
    row_len = WID // 4
    me = lax.axis_index("space")
    y, z, core = me // (RING * CORES), me // CORES % RING, me % CORES
    place = jnp.stack([y, z, core]).astype(jnp.int32)
    group = RING * CORES

    share = cotangent.shape[2] // ROWS
    local = jnp.pad(cotangent[0], ((0, 0), (0, 1), (0, 0)))
    parts = jnp.stack([local[:, at * share : (at + 1) * share + 1] for at in range(ROWS)])
    parts = parts.reshape(ROWS, -1, CORES, (share + 1) * cells // CORES).transpose(0, 2, 1, 3)
    first = exchange(parts.reshape((ROWS * CORES,) + parts.shape[2:]), PILLARS)
    first = first.reshape(ROWS, -1, first.shape[2])
    up, down = [first], [first]
    for _ in range(3):
        up.append(on_space(up[-1], z_by=1))
        down.append(on_space(down[-1], z_by=-1))
    far = on_space(up[3], z_by=1)
    mine = pile(down + [far] + up[:0:-1])
    theirs = on_space(mine, core_by=1)

    w_rel = [w_second]
    for step in range(1, ROWS):
        w_rel.append(on_space(w_second, y_by=-step))
    w_rel = jnp.stack(w_rel + w_rel, 3)
    w_group = lax.dynamic_slice_in_dim(w_rel, (ROWS - y) % ROWS, ROWS, 3)
    w_group = w_group.reshape(3, 3, 3, ROWS * own, C3)

    planes = volume[0].transpose(1, 2, 0, 3).reshape(2, 16 * channels, cells)
    w_rows = w_first.reshape(27 * channels, ROWS, group, own).transpose(2, 1, 3, 0)
    w_rows = w_rows.reshape(outs, 27 * channels)
    ahead = conv(w_rows, planes, ((0, 1),), jnp.bfloat16, row_len)
    behind = from_behind(ahead, "space", 1)
    part = conv(w_rows, planes, ((1, 0), (2, 1)), jnp.float32, row_len)
    hidden, slopes = act(part, behind, group)
    by_plane = exchange(hidden, SLABS)

    back_terms, cot_row = back(place, move_rows(w_group), mine, theirs, group, row_len)
    hidden_grad = exchange(back_terms, SLABS)

    partial, *others = grad(place, by_plane, cot_row, ROWS, row_len)
    for step, block in enumerate(others, 1):
        partial = partial + on_space(block, y_by=step).astype(jnp.float32)
    partial = partial.astype(jnp.bfloat16)
    sides = []
    for distance in (1, 2, 3):
        sides.append(from_side(partial, "dp", distance).astype(jnp.float32))
    grad_second = (partial.astype(jnp.float32) + sides[1]) + (sides[0] + sides[2])
    grad_second = grad_second.reshape(3, 3, 3, own, C3)

    pre_grad = (hidden_grad.astype(jnp.float32) * slopes).astype(jnp.bfloat16)
    pre_grad = pre_grad.reshape(group, 4, ROWS, own, cells).transpose(2, 0, 3, 1, 4)
    return (grad_second, pre_grad.reshape(1, outs, 1, 4, cells))


def solution(mesh):
    in_specs = (
        P("dp", None, "space", None, None),
        P(),
        P(None, None, None, "space", None),
        P("dp", "space", None, None),
    )
    out_specs = (P(None, None, None, "space", None), P("dp", None, "space", None, None))
    return jax.shard_map(
        section, mesh=mesh, in_specs=in_specs, out_specs=out_specs, check_vma=False
    )
```

```python
import functools

import jax
import jax.numpy as jnp
from jax import lax
from jax.experimental import pallas as pl
from jax.experimental.pallas import tpu as pltpu
from jax.sharding import PartitionSpec as P


C3 = 512
WID = 128


leak_slope = 0.3


def from_behind(block, axis, distance):
    devices = range(lax.axis_size(axis))
    route = [(i - distance, i) for i in devices if i - distance in devices]
    return lax.ppermute(block, axis, route)


def from_side(block, axis, distance):
    size = lax.axis_size(axis)
    return lax.ppermute(block, axis, [(i, (i + distance) % size) for i in range(size)])


ROWS, RING, CORES = 4, 8, 2
IN_VMEM = pl.BlockSpec(memory_space=pltpu.VMEM)


def shifted(block, by_row, by_col, row_len):
    moved = block.astype(jnp.float32)
    lane = lax.broadcasted_iota(jnp.int32, moved.shape, 1)
    moved = pltpu.roll(moved, by_row * row_len + by_col, 1)
    keep = None
    if by_row:
        keep = lane >= row_len
    if by_col:
        inner = lane % row_len != 0
        keep = inner if keep is None else jnp.logical_and(keep, inner)
    return jnp.where(keep, moved, 0.0).astype(block.dtype)


def conv_kernel(use, channels, row_len, w_ref, planes_ref, out_ref, cols_ref):
    tap_rows = 9 * channels
    for at, (_, plane) in enumerate(use):
        for row in range(-1, 4):
            for col in range(-1, 4):
                source = ((row % 4) * 4 + col % 4) * channels
                block = planes_ref[plane, source : source + channels, :]
                if row < 0 or col < 0:
                    block = shifted(block, int(row < 0), int(col < 0), row_len)
                for row_phase in range(2):
                    row_tap = row + 1 - 2 * row_phase
                    if not 0 <= row_tap <= 2:
                        continue
                    for col_phase in range(2):
                        col_tap = col + 1 - 2 * col_phase
                        if not 0 <= col_tap <= 2:
                            continue
                        start = at * tap_rows + (row_tap * 3 + col_tap) * channels
                        cols_ref[row_phase * 2 + col_phase, start : start + channels, :] = block
    first = use[0][0] * tap_rows
    weights = w_ref[:, first : first + len(use) * tap_rows]
    for phase in range(4):
        out_ref[phase, :, :] = jnp.dot(
            weights, cols_ref[phase], preferred_element_type=jnp.float32
        ).astype(out_ref.dtype)


def conv(w_rows, planes, use, dtype, row_len):
    outs, depth = w_rows.shape
    channels = depth // 27
    cells = planes.shape[2]
    depth = 9 * channels * len(use)
    return pl.pallas_call(
        functools.partial(conv_kernel, use, channels, row_len),
        out_shape=jax.ShapeDtypeStruct((4, outs, cells), dtype),
        in_specs=[IN_VMEM] * 2,
        out_specs=IN_VMEM,
        scratch_shapes=[pltpu.VMEM((4, depth, cells), jnp.bfloat16)],
        cost_estimate=pl.CostEstimate(
            flops=8 * outs * depth * cells, bytes_accessed=4 * depth * cells, transcendentals=0
        ),
    )(w_rows, planes)


def act_kernel(part_ref, behind_ref, hidden_ref, slope_ref):
    groups, rows, _ = hidden_ref.shape
    unit = rows // 4
    outs = part_ref.shape[1]
    own = unit // ROWS
    for phase in range(4):
        values = part_ref[phase] + behind_ref[phase].astype(jnp.float32)
        gate = jax.nn.sigmoid(values)
        gated = (1.0 - leak_slope) * gate
        active = leak_slope * values + gated * values
        slope = leak_slope + gated * (1.0 + values * (1.0 - gate))
        there = slice(phase * unit, (phase + 1) * unit)
        for at in range(groups):
            picks = [slice(first, first + own) for first in range(at * own, outs, outs // ROWS)]
            block = jnp.concatenate([active[pick] for pick in picks], 0)
            hidden_ref[at, there, :] = block.astype(hidden_ref.dtype)
            slope_ref[at, there, :] = jnp.concatenate([slope[pick] for pick in picks], 0)


def act(part, behind, groups):
    phases, outs, cells = part.shape
    shape = (groups, phases * outs // groups, cells)
    return pl.pallas_call(
        act_kernel,
        out_shape=(
            jax.ShapeDtypeStruct(shape, jnp.bfloat16),
            jax.ShapeDtypeStruct(shape, jnp.float32),
        ),
        in_specs=[IN_VMEM] * 2,
        out_specs=(IN_VMEM,) * 2,
        cost_estimate=pl.CostEstimate(
            flops=10 * part.size, bytes_accessed=12 * part.size, transcendentals=part.size
        ),
    )(part, behind)


def pile_kernel(*refs):
    for at, ref in enumerate(refs[:-1]):
        refs[-1][at] = ref[...]


def pile(blocks):
    shape = (len(blocks),) + blocks[0].shape
    return pl.pallas_call(
        pile_kernel,
        out_shape=jax.ShapeDtypeStruct(shape, blocks[0].dtype),
        in_specs=[IN_VMEM] * len(blocks),
        out_specs=IN_VMEM,
        cost_estimate=pl.CostEstimate(
            flops=0, bytes_accessed=4 * len(blocks) * blocks[0].size, transcendentals=0
        ),
    )(*blocks)


def spread(block, row_len):
    return jnp.concatenate(
        [block]
        + [shifted(block, by_row, by_col, row_len) for by_row, by_col in ((0, 1), (1, 0), (1, 1))],
        0,
    )


def gather_back(terms, row_len):
    rows = terms.shape[0] // 4
    lane = lax.broadcasted_iota(jnp.int32, (rows, terms.shape[1]), 1)
    cells = terms.shape[1]
    total = terms[:rows]
    for at, (by_row, by_col) in ((1, (0, 1)), (2, (1, 0)), (3, (1, 1))):
        moved = pltpu.roll(terms[at * rows : (at + 1) * rows], cells - by_row * row_len - by_col, 1)
        keep = lane < cells - row_len if by_row else None
        if by_col:
            inner = lane % row_len != row_len - 1
            keep = inner if keep is None else jnp.logical_and(keep, inner)
        total = total + jnp.where(keep, moved, 0.0)
    return total


def grad_kernel(row_len, place_ref, hidden_ref, cot_ref, *refs):
    outs_refs, (even_ref, odd_ref, sum_ref) = refs[:-3], refs[-3:]
    planes, group, cells = hidden_ref.shape
    steps = planes // 2
    own = group // 4
    unit = own // len(outs_refs)
    for s in range(steps):
        here = slice(s * cells, (s + 1) * cells)
        even_ref[:, here] = spread(hidden_ref[2 * s], row_len)
        odd_ref[:, here] = spread(hidden_ref[2 * s + 1], row_len)
    over_cells = (((1,), (1,)), ((), ()))
    sources = ((odd_ref, cells), (even_ref, 0), (odd_ref, 0))
    for depth_tap, (rows_ref, start) in enumerate(sources):
        total = lax.dot_general(
            rows_ref[...],
            cot_ref[:, start : start + steps * cells],
            over_cells,
            preferred_element_type=jnp.float32,
        )
        for row_tap in range(3):
            for col_tap in range(3):
                at = (2 * int(row_tap == 0) + int(col_tap == 0)) * group
                at += (2 * int(row_tap != 1) + int(col_tap != 1)) * own
                put = ((depth_tap * 3 + row_tap) * 3 + col_tap) * unit
                for y in range(len(outs_refs)):
                    first = at + y * unit
                    sum_ref[y, put : put + unit, :] = total[first : first + unit, :]
    for away, out_ref in enumerate(outs_refs):
        y = lax.rem(place_ref[0] + away, len(outs_refs))
        out_ref[...] = sum_ref[y].astype(out_ref.dtype)


def grad(place, hidden, cot, row_count, row_len):
    planes, group, cells = hidden.shape
    outs = cot.shape[0]
    rows = pltpu.VMEM((4 * group, planes // 2 * cells), jnp.bfloat16)
    size = 27 * group // (4 * row_count)
    return pl.pallas_call(
        functools.partial(grad_kernel, row_len),
        out_shape=[
            jax.ShapeDtypeStruct((size, outs), jnp.bfloat16 if away else jnp.float32)
            for away in range(row_count)
        ],
        in_specs=[pl.BlockSpec(memory_space=pltpu.SMEM), IN_VMEM, IN_VMEM],
        out_specs=[IN_VMEM] * row_count,
        scratch_shapes=[rows, rows, pltpu.VMEM((row_count, size, outs), jnp.float32)],
        cost_estimate=pl.CostEstimate(
            flops=12 * group * outs * planes * cells, bytes_accessed=2 * cot.size, transcendentals=0
        ),
    )(place, hidden, cot)


def back_kernel(row_len, place_ref, *refs):
    w_refs, (mine_ref, theirs_ref, out_ref, cot_ref, rows_ref, moves_ref) = refs[:-6], refs[-6:]
    planes, group, cells = out_ref.shape
    ring, row_count, unit, half = mine_ref.shape
    y, z, core = place_ref[0], place_ref[1], place_ref[2]
    here = pl.ds(pl.multiple_of(core * half, 128), half)
    there = pl.ds(pl.multiple_of((1 - core) * half, 128), half)
    for k in range(ring):
        for row in range(row_count):
            first = row * ring * unit + lax.rem(z + k, ring) * unit
            rows = pl.ds(pl.multiple_of(first, unit), unit)
            cot_ref[rows, here] = mine_ref[k, row]
            cot_ref[rows, there] = theirs_ref[k, row]

    for away, w_ref in enumerate(w_refs):
        rows_ref[lax.rem(y + away, row_count)] = w_ref[...].astype(jnp.float32)
    block = group // 4
    own = block // row_count
    size = 4 * group
    moves_ref[...] = jnp.zeros_like(moves_ref)
    for tap in range(27):
        depth_tap, row_tap, col_tap = tap // 9, tap // 3 % 3, tap % 3
        at = depth_tap * size + (2 * int(row_tap == 0) + int(col_tap == 0)) * group
        at += (2 * int(row_tap != 1) + int(col_tap != 1)) * block
        pieces = [rows_ref[row, tap * own : (tap + 1) * own, :] for row in range(row_count)]
        moves_ref[at : at + block, :] = jnp.concatenate(pieces, 0).astype(moves_ref.dtype)

    def one(at, start):
        return jnp.dot(
            moves_ref[at * size : (at + 1) * size, :],
            cot_ref[:, start : start + cells],
            preferred_element_type=jnp.float32,
        )

    for s in range(planes // 2):
        start = s * cells
        out_ref[2 * s] = gather_back(one(1, start), row_len).astype(out_ref.dtype)
        odd = one(2, start) + one(0, start + cells)
        out_ref[2 * s + 1] = gather_back(odd, row_len).astype(out_ref.dtype)


def back(place, w_rel, mine, theirs, planes, row_len):
    size, outs = w_rel[0].shape
    row_count = len(w_rel)
    group = 4 * row_count * size // 27
    width = 2 * mine.shape[3]
    cells = width // (planes // 2 + 1)
    return pl.pallas_call(
        functools.partial(back_kernel, row_len),
        out_shape=(
            jax.ShapeDtypeStruct((planes, group, cells), jnp.bfloat16),
            jax.ShapeDtypeStruct((outs, width), jnp.bfloat16),
        ),
        in_specs=[pl.BlockSpec(memory_space=pltpu.SMEM)] + [IN_VMEM] * (row_count + 2),
        out_specs=(IN_VMEM,) * 2,
        scratch_shapes=[
            pltpu.VMEM((row_count, size, outs), jnp.float32),
            pltpu.VMEM((12 * group, outs), jnp.bfloat16),
        ],
        cost_estimate=pl.CostEstimate(
            flops=12 * group * outs * planes * cells, bytes_accessed=4 * outs * width, transcendentals=0
        ),
    )(place, *w_rel, mine, theirs)


def on_space(block, y_by=0, z_by=0, core_by=0):
    route = []
    for y in range(ROWS):
        for z in range(RING):
            for core in range(CORES):
                to = ((y + y_by) % ROWS, (z + z_by) % RING, (core + core_by) % CORES)
                route.append(((y * RING + z) * CORES + core, (to[0] * RING + to[1]) * CORES + to[2]))
    return lax.ppermute(block, "space", route)


CHIPS = [(y, z) for y in range(ROWS) for z in range(RING)]


def members(pick):
    groups = {}
    for y, z in CHIPS:
        for core in range(CORES):
            groups.setdefault(pick(y, z, core), []).append((y * RING + z) * CORES + core)
    return list(groups.values())


COLUMNS = members(lambda y, z, core: (z, core))
PILLARS = members(lambda y, z, core: z)
SLABS = members(lambda y, z, core: y)


def exchange(blocks, groups):
    return lax.all_to_all(
        blocks, "space", split_axis=0, concat_axis=0, axis_index_groups=groups, tiled=True
    )


def section(volume, w_first, w_second, cotangent):
    channels = volume.shape[1]
    cells = volume.shape[4]
    outs = w_first.shape[4]
    own = w_second.shape[3]
    row_len = WID // 4
    me = lax.axis_index("space")
    y, z, core = me // (RING * CORES), me // CORES % RING, me % CORES
    place = jnp.stack([y, z, core]).astype(jnp.int32)
    group = RING * CORES

    share = cotangent.shape[2] // ROWS
    local = jnp.pad(cotangent[0], ((0, 0), (0, 1), (0, 0)))
    parts = jnp.stack([local[:, at * share : (at + 1) * share + 1] for at in range(ROWS)])
    parts = parts.reshape(ROWS, -1, CORES, (share + 1) * cells // CORES).transpose(0, 2, 1, 3)
    first = exchange(parts.reshape((ROWS * CORES,) + parts.shape[2:]), PILLARS)
    first = first.reshape(ROWS, -1, first.shape[2])
    up, down = [first], [first]
    for _ in range(3):
        up.append(on_space(up[-1], z_by=1))
        down.append(on_space(down[-1], z_by=-1))
    far = on_space(up[3], z_by=1)
    mine = pile(down + [far] + up[:0:-1])
    theirs = on_space(mine, core_by=1)

    w_rel = [w_second.reshape(27 * own, C3)]
    for step in range(1, ROWS):
        w_rel.append(on_space(w_rel[0], y_by=-step))

    planes = volume[0].transpose(1, 2, 0, 3).reshape(2, 16 * channels, cells)
    w_rows = w_first.reshape(27 * channels, outs).T
    ahead = conv(w_rows, planes, ((0, 1),), jnp.bfloat16, row_len)
    behind = from_behind(ahead, "space", 1)
    part = conv(w_rows, planes, ((1, 0), (2, 1)), jnp.float32, row_len)
    hidden, slopes = act(part, behind, group)
    by_plane = exchange(hidden, SLABS)

    back_terms, cot_row = back(place, w_rel, mine, theirs, group, row_len)
    hidden_grad = exchange(back_terms, SLABS)

    partial, *others = grad(place, by_plane, cot_row, ROWS, row_len)
    for step, block in enumerate(others, 1):
        partial = partial + on_space(block, y_by=step).astype(jnp.float32)
    partial = partial.astype(jnp.bfloat16)
    sides = []
    for distance in (1, 2, 3):
        sides.append(from_side(partial, "dp", distance).astype(jnp.float32))
    grad_second = (partial.astype(jnp.float32) + sides[1]) + (sides[0] + sides[2])
    grad_second = grad_second.reshape(3, 3, 3, own, C3)

    pre_grad = (hidden_grad.astype(jnp.float32) * slopes).astype(jnp.bfloat16)
    pre_grad = pre_grad.reshape(group, 4, ROWS, own, cells).transpose(2, 0, 3, 1, 4)
    return (grad_second, pre_grad.reshape(1, outs, 1, 4, cells))


def solution(mesh):
    in_specs = (
        P("dp", None, "space", None, None),
        P(),
        P(None, None, None, "space", None),
        P("dp", "space", None, None),
    )
    out_specs = (P(None, None, None, "space", None), P("dp", None, "space", None, None))
    return jax.shard_map(
        section, mesh=mesh, in_specs=in_specs, out_specs=out_specs, check_vma=False
    )
```

```python
import functools

import jax
import jax.numpy as jnp
from jax import lax
from jax.experimental import pallas as pl
from jax.experimental.pallas import tpu as pltpu
from jax.sharding import PartitionSpec as P


C3 = 512
WID = 128


leak_slope = 0.3


def from_behind(block, axis, distance):
    devices = range(lax.axis_size(axis))
    route = [(i - distance, i) for i in devices if i - distance in devices]
    return lax.ppermute(block, axis, route)


def from_side(block, axis, distance):
    size = lax.axis_size(axis)
    return lax.ppermute(block, axis, [(i, (i + distance) % size) for i in range(size)])


ROWS, RING, CORES = 4, 8, 2
IN_VMEM = pl.BlockSpec(memory_space=pltpu.VMEM)


def shifted(block, by_row, by_col, row_len):
    moved = block.astype(jnp.float32)
    lane = lax.broadcasted_iota(jnp.int32, moved.shape, 1)
    moved = pltpu.roll(moved, by_row * row_len + by_col, 1)
    keep = None
    if by_row:
        keep = lane >= row_len
    if by_col:
        inner = lane % row_len != 0
        keep = inner if keep is None else jnp.logical_and(keep, inner)
    return jnp.where(keep, moved, 0.0).astype(block.dtype)


def conv_kernel(use, channels, row_len, w_ref, planes_ref, out_ref, cols_ref):
    tap_rows = 9 * channels
    cells = planes_ref.shape[2]
    for at, (_, plane) in enumerate(use):
        for row in range(-1, 4):
            for col in range(-1, 4):
                source = ((row % 4) * 4 + col % 4) * channels
                block = planes_ref[plane, source : source + channels, :]
                if row < 0 or col < 0:
                    block = shifted(block, int(row < 0), int(col < 0), row_len)
                for row_phase in range(2):
                    row_tap = row + 1 - 2 * row_phase
                    if not 0 <= row_tap <= 2:
                        continue
                    for col_phase in range(2):
                        col_tap = col + 1 - 2 * col_phase
                        if not 0 <= col_tap <= 2:
                            continue
                        start = at * tap_rows + (row_tap * 3 + col_tap) * channels
                        phase = row_phase * 2 + col_phase
                        put = slice(phase * cells, (phase + 1) * cells)
                        cols_ref[start : start + channels, put] = block
    first = use[0][0] * tap_rows
    total = lax.dot_general(
        w_ref[first : first + len(use) * tap_rows, :],
        cols_ref[...],
        (((0,), (0,)), ((), ())),
        preferred_element_type=jnp.float32,
    )
    for phase in range(4):
        out_ref[phase] = total[:, phase * cells : (phase + 1) * cells].astype(out_ref.dtype)


def conv(w_rows, planes, use, dtype, row_len):
    depth, outs = w_rows.shape
    channels = depth // 27
    cells = planes.shape[2]
    depth = 9 * channels * len(use)
    return pl.pallas_call(
        functools.partial(conv_kernel, use, channels, row_len),
        out_shape=jax.ShapeDtypeStruct((4, outs, cells), dtype),
        in_specs=[IN_VMEM] * 2,
        out_specs=IN_VMEM,
        scratch_shapes=[pltpu.VMEM((depth, 4 * cells), jnp.bfloat16)],
        cost_estimate=pl.CostEstimate(
            flops=8 * outs * depth * cells, bytes_accessed=4 * depth * cells, transcendentals=0
        ),
    )(w_rows, planes)


def act_kernel(part_ref, behind_ref, hidden_ref, slope_ref):
    groups, rows, _ = hidden_ref.shape
    unit = rows // 4
    outs = part_ref.shape[1]
    own = unit // ROWS
    for phase in range(4):
        values = part_ref[phase] + behind_ref[phase].astype(jnp.float32)
        gate = jax.nn.sigmoid(values)
        gated = (1.0 - leak_slope) * gate
        active = leak_slope * values + gated * values
        slope = leak_slope + gated * (1.0 + values * (1.0 - gate))
        there = slice(phase * unit, (phase + 1) * unit)
        for at in range(groups):
            picks = [slice(first, first + own) for first in range(at * own, outs, outs // ROWS)]
            block = jnp.concatenate([active[pick] for pick in picks], 0)
            hidden_ref[at, there, :] = block.astype(hidden_ref.dtype)
            slope_ref[at, there, :] = jnp.concatenate([slope[pick] for pick in picks], 0)


def act(part, behind, groups):
    phases, outs, cells = part.shape
    shape = (groups, phases * outs // groups, cells)
    return pl.pallas_call(
        act_kernel,
        out_shape=(
            jax.ShapeDtypeStruct(shape, jnp.bfloat16),
            jax.ShapeDtypeStruct(shape, jnp.float32),
        ),
        in_specs=[IN_VMEM] * 2,
        out_specs=(IN_VMEM,) * 2,
        cost_estimate=pl.CostEstimate(
            flops=10 * part.size, bytes_accessed=12 * part.size, transcendentals=part.size
        ),
    )(part, behind)


def pile_kernel(*refs):
    for at, ref in enumerate(refs[:-1]):
        refs[-1][at] = ref[...]


def pile(blocks):
    shape = (len(blocks),) + blocks[0].shape
    return pl.pallas_call(
        pile_kernel,
        out_shape=jax.ShapeDtypeStruct(shape, blocks[0].dtype),
        in_specs=[IN_VMEM] * len(blocks),
        out_specs=IN_VMEM,
        cost_estimate=pl.CostEstimate(
            flops=0, bytes_accessed=4 * len(blocks) * blocks[0].size, transcendentals=0
        ),
    )(*blocks)


def spread(block, row_len):
    return jnp.concatenate(
        [block]
        + [shifted(block, by_row, by_col, row_len) for by_row, by_col in ((0, 1), (1, 0), (1, 1))],
        0,
    )


def gather_back(terms, row_len):
    rows = terms.shape[0] // 4
    lane = lax.broadcasted_iota(jnp.int32, (rows, terms.shape[1]), 1)
    cells = terms.shape[1]
    total = terms[:rows]
    for at, (by_row, by_col) in ((1, (0, 1)), (2, (1, 0)), (3, (1, 1))):
        moved = pltpu.roll(terms[at * rows : (at + 1) * rows], cells - by_row * row_len - by_col, 1)
        keep = lane < cells - row_len if by_row else None
        if by_col:
            inner = lane % row_len != row_len - 1
            keep = inner if keep is None else jnp.logical_and(keep, inner)
        total = total + jnp.where(keep, moved, 0.0)
    return total


def grad_kernel(row_len, place_ref, hidden_ref, cot_ref, *refs):
    outs_refs, (even_ref, odd_ref, sum_ref) = refs[:-3], refs[-3:]
    planes, group, cells = hidden_ref.shape
    steps = planes // 2
    own = group // 4
    unit = own // len(outs_refs)
    for s in range(steps):
        here = slice(s * cells, (s + 1) * cells)
        even_ref[:, here] = spread(hidden_ref[2 * s], row_len)
        odd_ref[:, here] = spread(hidden_ref[2 * s + 1], row_len)
    over_cells = (((1,), (1,)), ((), ()))
    sources = ((odd_ref, cells), (even_ref, 0), (odd_ref, 0))
    for depth_tap, (rows_ref, start) in enumerate(sources):
        total = lax.dot_general(
            rows_ref[...],
            cot_ref[:, start : start + steps * cells],
            over_cells,
            preferred_element_type=jnp.float32,
        )
        for row_tap in range(3):
            for col_tap in range(3):
                at = (2 * int(row_tap == 0) + int(col_tap == 0)) * group
                at += (2 * int(row_tap != 1) + int(col_tap != 1)) * own
                put = ((depth_tap * 3 + row_tap) * 3 + col_tap) * unit
                for y in range(len(outs_refs)):
                    first = at + y * unit
                    sum_ref[y, put : put + unit, :] = total[first : first + unit, :]
    for away, out_ref in enumerate(outs_refs):
        y = lax.rem(place_ref[0] + away, len(outs_refs))
        out_ref[...] = sum_ref[y].astype(out_ref.dtype)


def grad(place, hidden, cot, row_count, row_len):
    planes, group, cells = hidden.shape
    outs = cot.shape[0]
    rows = pltpu.VMEM((4 * group, planes // 2 * cells), jnp.bfloat16)
    size = 27 * group // (4 * row_count)
    return pl.pallas_call(
        functools.partial(grad_kernel, row_len),
        out_shape=[
            jax.ShapeDtypeStruct((size, outs), jnp.bfloat16 if away else jnp.float32)
            for away in range(row_count)
        ],
        in_specs=[pl.BlockSpec(memory_space=pltpu.SMEM), IN_VMEM, IN_VMEM],
        out_specs=[IN_VMEM] * row_count,
        scratch_shapes=[rows, rows, pltpu.VMEM((row_count, size, outs), jnp.float32)],
        cost_estimate=pl.CostEstimate(
            flops=12 * group * outs * planes * cells, bytes_accessed=2 * cot.size, transcendentals=0
        ),
    )(place, hidden, cot)


def back_kernel(row_len, place_ref, *refs):
    w_refs, (mine_ref, theirs_ref, out_ref, cot_ref, rows_ref, moves_ref) = refs[:-6], refs[-6:]
    planes, group, cells = out_ref.shape
    ring, row_count, unit, half = mine_ref.shape
    y, z, core = place_ref[0], place_ref[1], place_ref[2]
    here = pl.ds(pl.multiple_of(core * half, 128), half)
    there = pl.ds(pl.multiple_of((1 - core) * half, 128), half)
    for k in range(ring):
        for row in range(row_count):
            first = row * ring * unit + lax.rem(z + k, ring) * unit
            rows = pl.ds(pl.multiple_of(first, unit), unit)
            cot_ref[rows, here] = mine_ref[k, row]
            cot_ref[rows, there] = theirs_ref[k, row]

    for away, w_ref in enumerate(w_refs):
        rows_ref[lax.rem(y + away, row_count)] = w_ref[...].astype(jnp.float32)
    block = group // 4
    own = block // row_count
    size = 4 * group
    moves_ref[...] = jnp.zeros_like(moves_ref)
    for tap in range(27):
        depth_tap, row_tap, col_tap = tap // 9, tap // 3 % 3, tap % 3
        at = depth_tap * size + (2 * int(row_tap == 0) + int(col_tap == 0)) * group
        at += (2 * int(row_tap != 1) + int(col_tap != 1)) * block
        pieces = [rows_ref[row, tap * own : (tap + 1) * own, :] for row in range(row_count)]
        moves_ref[at : at + block, :] = jnp.concatenate(pieces, 0).astype(moves_ref.dtype)

    def one(at, start):
        return jnp.dot(
            moves_ref[at * size : (at + 1) * size, :],
            cot_ref[:, start : start + cells],
            preferred_element_type=jnp.float32,
        )

    for s in range(planes // 2):
        start = s * cells
        out_ref[2 * s] = gather_back(one(1, start), row_len).astype(out_ref.dtype)
        odd = one(2, start) + one(0, start + cells)
        out_ref[2 * s + 1] = gather_back(odd, row_len).astype(out_ref.dtype)


def back(place, w_rel, mine, theirs, planes, row_len):
    size, outs = w_rel[0].shape
    row_count = len(w_rel)
    group = 4 * row_count * size // 27
    width = 2 * mine.shape[3]
    cells = width // (planes // 2 + 1)
    return pl.pallas_call(
        functools.partial(back_kernel, row_len),
        out_shape=(
            jax.ShapeDtypeStruct((planes, group, cells), jnp.bfloat16),
            jax.ShapeDtypeStruct((outs, width), jnp.bfloat16),
        ),
        in_specs=[pl.BlockSpec(memory_space=pltpu.SMEM)] + [IN_VMEM] * (row_count + 2),
        out_specs=(IN_VMEM,) * 2,
        scratch_shapes=[
            pltpu.VMEM((row_count, size, outs), jnp.float32),
            pltpu.VMEM((12 * group, outs), jnp.bfloat16),
        ],
        cost_estimate=pl.CostEstimate(
            flops=12 * group * outs * planes * cells, bytes_accessed=4 * outs * width, transcendentals=0
        ),
    )(place, *w_rel, mine, theirs)


def on_space(block, y_by=0, z_by=0, core_by=0):
    route = []
    for y in range(ROWS):
        for z in range(RING):
            for core in range(CORES):
                to = ((y + y_by) % ROWS, (z + z_by) % RING, (core + core_by) % CORES)
                route.append(((y * RING + z) * CORES + core, (to[0] * RING + to[1]) * CORES + to[2]))
    return lax.ppermute(block, "space", route)


CHIPS = [(y, z) for y in range(ROWS) for z in range(RING)]


def members(pick):
    groups = {}
    for y, z in CHIPS:
        for core in range(CORES):
            groups.setdefault(pick(y, z, core), []).append((y * RING + z) * CORES + core)
    return list(groups.values())


COLUMNS = members(lambda y, z, core: (z, core))
PILLARS = members(lambda y, z, core: z)
SLABS = members(lambda y, z, core: y)


def exchange(blocks, groups):
    return lax.all_to_all(
        blocks, "space", split_axis=0, concat_axis=0, axis_index_groups=groups, tiled=True
    )


def section(volume, w_first, w_second, cotangent):
    channels = volume.shape[1]
    cells = volume.shape[4]
    outs = w_first.shape[4]
    own = w_second.shape[3]
    row_len = WID // 4
    me = lax.axis_index("space")
    y, z, core = me // (RING * CORES), me // CORES % RING, me % CORES
    place = jnp.stack([y, z, core]).astype(jnp.int32)
    group = RING * CORES

    share = cotangent.shape[2] // ROWS
    local = jnp.pad(cotangent[0], ((0, 0), (0, 1), (0, 0)))
    parts = jnp.stack([local[:, at * share : (at + 1) * share + 1] for at in range(ROWS)])
    parts = parts.reshape(ROWS, -1, CORES, (share + 1) * cells // CORES).transpose(0, 2, 1, 3)
    first = exchange(parts.reshape((ROWS * CORES,) + parts.shape[2:]), PILLARS)
    first = first.reshape(ROWS, -1, first.shape[2])
    hops = {0: first}
    for step in (1, -1, 2, -2):
        hops[step] = on_space(first, z_by=-step)
    for step, come in ((3, 2), (-3, -2), (4, 2)):
        hops[step] = on_space(hops[come], z_by=come - step)
    mine = pile([hops[step] for step in (0, 1, 2, 3, 4, -3, -2, -1)])
    theirs = on_space(mine, core_by=1)

    w_rel = [w_second.reshape(27 * own, C3)]
    for step in range(1, ROWS):
        w_rel.append(on_space(w_rel[0], y_by=-step))

    planes = volume[0].transpose(1, 2, 0, 3).reshape(2, 16 * channels, cells)
    w_rows = w_first.reshape(27 * channels, outs)
    ahead = conv(w_rows, planes, ((0, 1),), jnp.bfloat16, row_len)
    behind = from_behind(ahead, "space", 1)
    part = conv(w_rows, planes, ((1, 0), (2, 1)), jnp.float32, row_len)
    hidden, slopes = act(part, behind, group)
    by_plane = exchange(hidden, SLABS)

    back_terms, cot_row = back(place, w_rel, mine, theirs, group, row_len)
    hidden_grad = exchange(back_terms, SLABS)

    partial, *others = grad(place, by_plane, cot_row, ROWS, row_len)
    for step, block in enumerate(others, 1):
        partial = partial + on_space(block, y_by=step).astype(jnp.float32)
    partial = partial.astype(jnp.bfloat16)
    sides = []
    for distance in (1, 2, 3):
        sides.append(from_side(partial, "dp", distance).astype(jnp.float32))
    grad_second = (partial.astype(jnp.float32) + sides[1]) + (sides[0] + sides[2])
    grad_second = grad_second.reshape(3, 3, 3, own, C3)

    pre_grad = (hidden_grad.astype(jnp.float32) * slopes).astype(jnp.bfloat16)
    pre_grad = pre_grad.reshape(group, 4, ROWS, own, cells).transpose(2, 0, 3, 1, 4)
    return (grad_second, pre_grad.reshape(1, outs, 1, 4, cells))


def solution(mesh):
    in_specs = (
        P("dp", None, "space", None, None),
        P(),
        P(None, None, None, "space", None),
        P("dp", "space", None, None),
    )
    out_specs = (P(None, None, None, "space", None), P("dp", None, "space", None, None))
    return jax.shard_map(
        section, mesh=mesh, in_specs=in_specs, out_specs=out_specs, check_vma=False
    )
```

```python
import functools

import jax
import jax.numpy as jnp
from jax import lax
from jax.experimental import pallas as pl
from jax.experimental.pallas import tpu as pltpu
from jax.sharding import PartitionSpec as P


C3 = 512
WID = 128


leak_slope = 0.3


def from_behind(block, axis, distance):
    devices = range(lax.axis_size(axis))
    route = [(i - distance, i) for i in devices if i - distance in devices]
    return lax.ppermute(block, axis, route)


def from_side(block, axis, distance):
    size = lax.axis_size(axis)
    return lax.ppermute(block, axis, [(i, (i + distance) % size) for i in range(size)])


def activate(values):
    return leak_slope * values + (1.0 - leak_slope) * values * jax.nn.sigmoid(values)


def slope_of(values):
    sigmoid_value = jax.nn.sigmoid(values)
    return leak_slope + (1.0 - leak_slope) * (
        sigmoid_value + values * sigmoid_value * (1.0 - sigmoid_value)
    )


ROWS, RING, CORES = 4, 8, 2
IN_VMEM = pl.BlockSpec(memory_space=pltpu.VMEM)
GRANT = pltpu.CompilerParams(vmem_limit_bytes=16 * 2**20)


def shifted(block, by_row, by_col, row_len):
    moved = block.astype(jnp.float32)
    lane = lax.broadcasted_iota(jnp.int32, moved.shape, 1)
    moved = pltpu.roll(moved, by_row * row_len + by_col, 1)
    keep = None
    if by_row:
        keep = lane >= row_len
    if by_col:
        inner = lane % row_len != 0
        keep = inner if keep is None else jnp.logical_and(keep, inner)
    return jnp.where(keep, moved, 0.0).astype(block.dtype)


def conv_kernel(use, channels, row_len, w_ref, planes_ref, out_ref, cols_ref):
    tap_rows = 9 * channels
    cells = planes_ref.shape[2]
    for at, (_, plane) in enumerate(use):
        for row in range(-1, 4):
            for col in range(-1, 4):
                source = ((row % 4) * 4 + col % 4) * channels
                block = planes_ref[plane, source : source + channels, :]
                if row < 0 or col < 0:
                    block = shifted(block, int(row < 0), int(col < 0), row_len)
                for row_phase in range(2):
                    row_tap = row + 1 - 2 * row_phase
                    if not 0 <= row_tap <= 2:
                        continue
                    for col_phase in range(2):
                        col_tap = col + 1 - 2 * col_phase
                        if not 0 <= col_tap <= 2:
                            continue
                        start = at * tap_rows + (row_tap * 3 + col_tap) * channels
                        phase = row_phase * 2 + col_phase
                        put = slice(phase * cells, (phase + 1) * cells)
                        cols_ref[start : start + channels, put] = block
    first = use[0][0] * tap_rows
    total = lax.dot_general(
        w_ref[first : first + len(use) * tap_rows, :],
        cols_ref[...],
        (((0,), (0,)), ((), ())),
        preferred_element_type=jnp.float32,
    )
    for phase in range(4):
        out_ref[phase] = total[:, phase * cells : (phase + 1) * cells].astype(out_ref.dtype)


def conv(w_rows, planes, use, dtype, row_len):
    depth, outs = w_rows.shape
    channels = depth // 27
    cells = planes.shape[2]
    depth = 9 * channels * len(use)
    return pl.pallas_call(
        functools.partial(conv_kernel, use, channels, row_len),
        out_shape=jax.ShapeDtypeStruct((4, outs, cells), dtype),
        in_specs=[IN_VMEM] * 2,
        out_specs=IN_VMEM,
        scratch_shapes=[pltpu.VMEM((depth, 4 * cells), jnp.bfloat16)],
        compiler_params=GRANT,
        cost_estimate=pl.CostEstimate(
            flops=8 * outs * depth * cells, bytes_accessed=4 * depth * cells, transcendentals=0
        ),
    )(w_rows, planes)


def regrouped(values, own, at):
    outs = values.shape[0]
    starts = range(at * own, outs, outs // ROWS)
    return jnp.concatenate([values[start : start + own] for start in starts], 0)


def pointwise_kernel(rule, part_ref, behind_ref, result_ref):
    groups, rows, _ = result_ref.shape
    unit = rows // 4
    for phase in range(4):
        values = rule(part_ref[phase] + behind_ref[phase].astype(jnp.float32))
        for at in range(groups):
            block = regrouped(values, unit // ROWS, at)
            result_ref[at, phase * unit : (phase + 1) * unit, :] = block.astype(result_ref.dtype)


def pointwise(rule, part, behind, groups, dtype):
    phases, outs, cells = part.shape
    return pl.pallas_call(
        functools.partial(pointwise_kernel, rule),
        out_shape=jax.ShapeDtypeStruct((groups, phases * outs // groups, cells), dtype),
        in_specs=[IN_VMEM] * 2,
        out_specs=IN_VMEM,
        compiler_params=GRANT,
        cost_estimate=pl.CostEstimate(
            flops=10 * part.size, bytes_accessed=8 * part.size, transcendentals=part.size
        ),
    )(part, behind)


def pile_kernel(*refs):
    for at, ref in enumerate(refs[:-1]):
        refs[-1][at] = ref[...]


def pile(blocks):
    shape = (len(blocks),) + blocks[0].shape
    return pl.pallas_call(
        pile_kernel,
        out_shape=jax.ShapeDtypeStruct(shape, blocks[0].dtype),
        in_specs=[IN_VMEM] * len(blocks),
        out_specs=IN_VMEM,
        compiler_params=GRANT,
        cost_estimate=pl.CostEstimate(
            flops=0, bytes_accessed=4 * len(blocks) * blocks[0].size, transcendentals=0
        ),
    )(*blocks)


def spread(block, row_len):
    return jnp.concatenate(
        [block]
        + [shifted(block, by_row, by_col, row_len) for by_row, by_col in ((0, 1), (1, 0), (1, 1))],
        0,
    )


def gather_back(terms, row_len):
    rows = terms.shape[0] // 4
    lane = lax.broadcasted_iota(jnp.int32, (rows, terms.shape[1]), 1)
    cells = terms.shape[1]
    total = terms[:rows]
    for at, (by_row, by_col) in ((1, (0, 1)), (2, (1, 0)), (3, (1, 1))):
        moved = pltpu.roll(terms[at * rows : (at + 1) * rows], cells - by_row * row_len - by_col, 1)
        keep = lane < cells - row_len if by_row else None
        if by_col:
            inner = lane % row_len != row_len - 1
            keep = inner if keep is None else jnp.logical_and(keep, inner)
        total = total + jnp.where(keep, moved, 0.0)
    return total


def grad_kernel(row_len, place_ref, hidden_ref, cot_ref, *refs):
    outs_refs, (even_ref, odd_ref, sum_ref) = refs[:-3], refs[-3:]
    planes, group, cells = hidden_ref.shape
    steps = planes // 2
    own = group // 4
    unit = own // len(outs_refs)
    for s in range(steps):
        here = slice(s * cells, (s + 1) * cells)
        even_ref[:, here] = spread(hidden_ref[2 * s], row_len)
        odd_ref[:, here] = spread(hidden_ref[2 * s + 1], row_len)
    over_cells = (((1,), (1,)), ((), ()))
    sources = ((odd_ref, cells), (even_ref, 0), (odd_ref, 0))
    for depth_tap, (rows_ref, start) in enumerate(sources):
        total = lax.dot_general(
            rows_ref[...],
            cot_ref[:, start : start + steps * cells],
            over_cells,
            preferred_element_type=jnp.float32,
        )
        for row_tap in range(3):
            for col_tap in range(3):
                at = (2 * int(row_tap == 0) + int(col_tap == 0)) * group
                at += (2 * int(row_tap != 1) + int(col_tap != 1)) * own
                put = ((depth_tap * 3 + row_tap) * 3 + col_tap) * unit
                for y in range(len(outs_refs)):
                    first = at + y * unit
                    sum_ref[y, put : put + unit, :] = total[first : first + unit, :]
    for away, out_ref in enumerate(outs_refs):
        y = lax.rem(place_ref[0] + away, len(outs_refs))
        out_ref[...] = sum_ref[y].astype(out_ref.dtype)


def grad(place, hidden, cot, row_count, row_len):
    planes, group, cells = hidden.shape
    outs = cot.shape[0]
    rows = pltpu.VMEM((4 * group, planes // 2 * cells), jnp.bfloat16)
    size = 27 * group // (4 * row_count)
    return pl.pallas_call(
        functools.partial(grad_kernel, row_len),
        out_shape=[
            jax.ShapeDtypeStruct((size, outs), jnp.bfloat16 if away else jnp.float32)
            for away in range(row_count)
        ],
        in_specs=[pl.BlockSpec(memory_space=pltpu.SMEM), IN_VMEM, IN_VMEM],
        out_specs=[IN_VMEM] * row_count,
        scratch_shapes=[rows, rows, pltpu.VMEM((row_count, size, outs), jnp.float32)],
        compiler_params=GRANT,
        cost_estimate=pl.CostEstimate(
            flops=12 * group * outs * planes * cells, bytes_accessed=2 * cot.size, transcendentals=0
        ),
    )(place, hidden, cot)


def back_kernel(row_len, place_ref, *refs):
    w_refs, (mine_ref, theirs_ref, out_ref, cot_ref, rows_ref, moves_ref) = refs[:-6], refs[-6:]
    planes, group, cells = out_ref.shape
    ring, row_count, unit, half = mine_ref.shape
    y, z, core = place_ref[0], place_ref[1], place_ref[2]
    here = pl.ds(pl.multiple_of(core * half, 128), half)
    there = pl.ds(pl.multiple_of((1 - core) * half, 128), half)
    for k in range(ring):
        for row in range(row_count):
            first = row * ring * unit + lax.rem(z + k, ring) * unit
            rows = pl.ds(pl.multiple_of(first, unit), unit)
            cot_ref[rows, here] = mine_ref[k, row]
            cot_ref[rows, there] = theirs_ref[k, row]

    for away, w_ref in enumerate(w_refs):
        rows_ref[lax.rem(y + away, row_count)] = w_ref[...].astype(jnp.float32)
    block = group // 4
    own = block // row_count
    size = 4 * group
    moves_ref[...] = jnp.zeros_like(moves_ref)
    for tap in range(27):
        depth_tap, row_tap, col_tap = tap // 9, tap // 3 % 3, tap % 3
        at = depth_tap * size + (2 * int(row_tap == 0) + int(col_tap == 0)) * group
        at += (2 * int(row_tap != 1) + int(col_tap != 1)) * block
        pieces = [rows_ref[row, tap * own : (tap + 1) * own, :] for row in range(row_count)]
        moves_ref[at : at + block, :] = jnp.concatenate(pieces, 0).astype(moves_ref.dtype)

    def one(at, start):
        return jnp.dot(
            moves_ref[at * size : (at + 1) * size, :],
            cot_ref[:, start : start + cells],
            preferred_element_type=jnp.float32,
        )

    for s in range(planes // 2):
        start = s * cells
        out_ref[2 * s] = gather_back(one(1, start), row_len).astype(out_ref.dtype)
        odd = one(2, start) + one(0, start + cells)
        out_ref[2 * s + 1] = gather_back(odd, row_len).astype(out_ref.dtype)


def back(place, w_rel, mine, theirs, planes, row_len):
    size, outs = w_rel[0].shape
    row_count = len(w_rel)
    group = 4 * row_count * size // 27
    width = 2 * mine.shape[3]
    cells = width // (planes // 2 + 1)
    return pl.pallas_call(
        functools.partial(back_kernel, row_len),
        out_shape=(
            jax.ShapeDtypeStruct((planes, group, cells), jnp.bfloat16),
            jax.ShapeDtypeStruct((outs, width), jnp.bfloat16),
        ),
        in_specs=[pl.BlockSpec(memory_space=pltpu.SMEM)] + [IN_VMEM] * (row_count + 2),
        out_specs=(IN_VMEM,) * 2,
        scratch_shapes=[
            pltpu.VMEM((row_count, size, outs), jnp.float32),
            pltpu.VMEM((12 * group, outs), jnp.bfloat16),
        ],
        compiler_params=GRANT,
        cost_estimate=pl.CostEstimate(
            flops=12 * group * outs * planes * cells, bytes_accessed=4 * outs * width, transcendentals=0
        ),
    )(place, *w_rel, mine, theirs)


def on_space(block, y_by=0, z_by=0, core_by=0):
    route = []
    for y in range(ROWS):
        for z in range(RING):
            for core in range(CORES):
                to = ((y + y_by) % ROWS, (z + z_by) % RING, (core + core_by) % CORES)
                route.append(((y * RING + z) * CORES + core, (to[0] * RING + to[1]) * CORES + to[2]))
    return lax.ppermute(block, "space", route)


CHIPS = [(y, z) for y in range(ROWS) for z in range(RING)]


def members(pick):
    groups = {}
    for y, z in CHIPS:
        for core in range(CORES):
            groups.setdefault(pick(y, z, core), []).append((y * RING + z) * CORES + core)
    return list(groups.values())


COLUMNS = members(lambda y, z, core: (z, core))
PILLARS = members(lambda y, z, core: z)
SLABS = members(lambda y, z, core: y)


def exchange(blocks, groups):
    return lax.all_to_all(
        blocks, "space", split_axis=0, concat_axis=0, axis_index_groups=groups, tiled=True
    )


def section(volume, w_first, w_second, cotangent):
    channels = volume.shape[1]
    cells = volume.shape[4]
    outs = w_first.shape[4]
    own = w_second.shape[3]
    row_len = WID // 4
    me = lax.axis_index("space")
    y, z, core = me // (RING * CORES), me // CORES % RING, me % CORES
    place = jnp.stack([y, z, core]).astype(jnp.int32)
    group = RING * CORES

    share = cotangent.shape[2] // ROWS
    local = jnp.pad(cotangent[0], ((0, 0), (0, 1), (0, 0)))
    parts = jnp.stack([local[:, at * share : (at + 1) * share + 1] for at in range(ROWS)])
    parts = parts.reshape(ROWS, -1, CORES, (share + 1) * cells // CORES).transpose(0, 2, 1, 3)
    first = exchange(parts.reshape((ROWS * CORES,) + parts.shape[2:]), PILLARS)
    first = first.reshape(ROWS, -1, first.shape[2])
    hops = {0: first}
    for step in (1, -1, 2, -2):
        hops[step] = on_space(first, z_by=-step)
    for step, come in ((3, 2), (-3, -2), (4, 2)):
        hops[step] = on_space(hops[come], z_by=come - step)
    mine = pile([hops[step] for step in (0, 1, 2, 3, 4, -3, -2, -1)])
    theirs = on_space(mine, core_by=1)

    w_rel = [w_second.reshape(27 * own, C3)]
    for step in range(1, ROWS):
        w_rel.append(on_space(w_rel[0], y_by=-step))

    planes = volume[0].transpose(1, 2, 0, 3).reshape(2, 16 * channels, cells)
    w_rows = w_first.reshape(27 * channels, outs)
    ahead = conv(w_rows, planes, ((0, 1),), jnp.bfloat16, row_len)
    behind = from_behind(ahead, "space", 1)
    part = conv(w_rows, planes, ((1, 0), (2, 1)), jnp.float32, row_len)
    hidden = pointwise(activate, part, behind, group, jnp.bfloat16)
    slopes = pointwise(slope_of, part, behind, group, jnp.float32)
    by_plane = exchange(hidden, SLABS)

    back_terms, cot_row = back(place, w_rel, mine, theirs, group, row_len)
    hidden_grad = exchange(back_terms, SLABS)

    partial, *others = grad(place, by_plane, cot_row, ROWS, row_len)
    for step, block in enumerate(others, 1):
        partial = partial + on_space(block, y_by=step).astype(jnp.float32)
    partial = partial.astype(jnp.bfloat16)
    sides = []
    for distance in (1, 2, 3):
        sides.append(from_side(partial, "dp", distance).astype(jnp.float32))
    grad_second = (partial.astype(jnp.float32) + sides[1]) + (sides[0] + sides[2])
    grad_second = grad_second.reshape(3, 3, 3, own, C3)

    pre_grad = (hidden_grad.astype(jnp.float32) * slopes).astype(jnp.bfloat16)
    pre_grad = pre_grad.reshape(group, 4, ROWS, own, cells).transpose(2, 0, 3, 1, 4)
    return (grad_second, pre_grad.reshape(1, outs, 1, 4, cells))


def solution(mesh):
    in_specs = (
        P("dp", None, "space", None, None),
        P(),
        P(None, None, None, "space", None),
        P("dp", "space", None, None),
    )
    out_specs = (P(None, None, None, "space", None), P("dp", None, "space", None, None))
    return jax.shard_map(
        section, mesh=mesh, in_specs=in_specs, out_specs=out_specs, check_vma=False
    )
```

```python
import functools

import jax
import jax.numpy as jnp
from jax import lax
from jax.experimental import pallas as pl
from jax.experimental.pallas import tpu as pltpu
from jax.sharding import PartitionSpec as P


C3 = 512
WID = 128


leak_slope = 0.3


def from_behind(block, axis, distance):
    devices = range(lax.axis_size(axis))
    route = [(i - distance, i) for i in devices if i - distance in devices]
    return lax.ppermute(block, axis, route)


def from_side(block, axis, distance):
    size = lax.axis_size(axis)
    return lax.ppermute(block, axis, [(i, (i + distance) % size) for i in range(size)])


def activate(values):
    return leak_slope * values + (1.0 - leak_slope) * values * jax.nn.sigmoid(values)


def slope_of(values):
    sigmoid_value = jax.nn.sigmoid(values)
    return leak_slope + (1.0 - leak_slope) * (
        sigmoid_value + values * sigmoid_value * (1.0 - sigmoid_value)
    )


ROWS, RING, CORES = 4, 8, 2
IN_VMEM = pl.BlockSpec(memory_space=pltpu.VMEM)
ANYWHERE = pl.BlockSpec(memory_space=pl.ANY)
GRANT = pltpu.CompilerParams(vmem_limit_bytes=16 * 2**20)


def shifted(block, by_row, by_col, row_len):
    moved = block.astype(jnp.float32)
    lane = lax.broadcasted_iota(jnp.int32, moved.shape, 1)
    moved = pltpu.roll(moved, by_row * row_len + by_col, 1)
    keep = None
    if by_row:
        keep = lane >= row_len
    if by_col:
        inner = lane % row_len != 0
        keep = inner if keep is None else jnp.logical_and(keep, inner)
    return jnp.where(keep, moved, 0.0).astype(block.dtype)


def conv_kernel(row_len, w_from, planes_from, ahead_ref, part_ref, *scratch):
    cols_ref, w_ref, planes_ref, sems = scratch
    copies = [
        pltpu.make_async_copy(planes_from.at[0], planes_ref.at[0], sems.at[0]),
        pltpu.make_async_copy(planes_from.at[1], planes_ref.at[1], sems.at[1]),
        pltpu.make_async_copy(w_from, w_ref, sems.at[2]),
    ]
    for copy in copies:
        copy.start()
    cells = planes_ref.shape[2]
    channels = planes_ref.shape[1] // 16
    tap_rows = 9 * channels
    for plane in range(2):
        copies[plane].wait()
        for row in range(-1, 4):
            for col in range(-1, 4):
                source = ((row % 4) * 4 + col % 4) * channels
                block = planes_ref[plane, source : source + channels, :]
                if row < 0 or col < 0:
                    block = shifted(block, int(row < 0), int(col < 0), row_len)
                for row_phase in range(2):
                    row_tap = row + 1 - 2 * row_phase
                    if not 0 <= row_tap <= 2:
                        continue
                    for col_phase in range(2):
                        col_tap = col + 1 - 2 * col_phase
                        if not 0 <= col_tap <= 2:
                            continue
                        start = plane * tap_rows + (row_tap * 3 + col_tap) * channels
                        phase = row_phase * 2 + col_phase
                        put = slice(phase * cells, (phase + 1) * cells)
                        cols_ref[start : start + channels, put] = block
    copies[2].wait()
    over_rows = (((0,), (0,)), ((), ()))
    for out_ref, weights, cols in (
        (ahead_ref, w_ref[:tap_rows, :], cols_ref[tap_rows:, :]),
        (part_ref, w_ref[tap_rows:, :], cols_ref[...]),
    ):
        total = lax.dot_general(weights, cols, over_rows, preferred_element_type=jnp.float32)
        for phase in range(4):
            out_ref[phase] = total[:, phase * cells : (phase + 1) * cells].astype(out_ref.dtype)


def conv(w_rows, planes, row_len):
    depth, outs = w_rows.shape
    cells = planes.shape[2]
    return pl.pallas_call(
        functools.partial(conv_kernel, row_len),
        out_shape=(
            jax.ShapeDtypeStruct((4, outs, cells), jnp.bfloat16),
            jax.ShapeDtypeStruct((4, outs, cells), jnp.float32),
        ),
        in_specs=[ANYWHERE] * 2,
        out_specs=(IN_VMEM,) * 2,
        scratch_shapes=[
            pltpu.VMEM((2 * depth // 3, 4 * cells), jnp.bfloat16),
            pltpu.VMEM(w_rows.shape, jnp.bfloat16),
            pltpu.VMEM(planes.shape, jnp.bfloat16),
            pltpu.SemaphoreType.DMA((3,)),
        ],
        compiler_params=GRANT,
        cost_estimate=pl.CostEstimate(
            flops=8 * outs * depth * cells, bytes_accessed=4 * depth * cells, transcendentals=0
        ),
    )(w_rows, planes)


def regrouped(values, own, at):
    outs = values.shape[0]
    starts = range(at * own, outs, outs // ROWS)
    return jnp.concatenate([values[start : start + own] for start in starts], 0)


def pointwise_kernel(rule, part_ref, behind_ref, result_ref):
    groups, rows, _ = result_ref.shape
    unit = rows // 4
    for phase in range(4):
        values = rule(part_ref[phase] + behind_ref[phase].astype(jnp.float32))
        for at in range(groups):
            block = regrouped(values, unit // ROWS, at)
            result_ref[at, phase * unit : (phase + 1) * unit, :] = block.astype(result_ref.dtype)


def pointwise(rule, part, behind, groups, dtype):
    phases, outs, cells = part.shape
    return pl.pallas_call(
        functools.partial(pointwise_kernel, rule),
        out_shape=jax.ShapeDtypeStruct((groups, phases * outs // groups, cells), dtype),
        in_specs=[IN_VMEM] * 2,
        out_specs=IN_VMEM,
        compiler_params=GRANT,
        cost_estimate=pl.CostEstimate(
            flops=10 * part.size, bytes_accessed=8 * part.size, transcendentals=part.size
        ),
    )(part, behind)


def pile_kernel(*refs):
    blocks, out_ref, sems = refs[:-2], refs[-2], refs[-1]
    copies = [
        pltpu.make_async_copy(block, out_ref.at[at], sems.at[at]) for at, block in enumerate(blocks)
    ]
    for copy in copies:
        copy.start()
    for copy in copies:
        copy.wait()


def pile(blocks):
    shape = (len(blocks),) + blocks[0].shape
    return pl.pallas_call(
        pile_kernel,
        out_shape=jax.ShapeDtypeStruct(shape, blocks[0].dtype),
        in_specs=[ANYWHERE] * len(blocks),
        out_specs=IN_VMEM,
        scratch_shapes=[pltpu.SemaphoreType.DMA((len(blocks),))],
        compiler_params=GRANT,
        cost_estimate=pl.CostEstimate(
            flops=0, bytes_accessed=4 * len(blocks) * blocks[0].size, transcendentals=0
        ),
    )(*blocks)


def spread(block, row_len):
    return jnp.concatenate(
        [block]
        + [shifted(block, by_row, by_col, row_len) for by_row, by_col in ((0, 1), (1, 0), (1, 1))],
        0,
    )


def gather_back(terms, row_len):
    rows = terms.shape[0] // 4
    lane = lax.broadcasted_iota(jnp.int32, (rows, terms.shape[1]), 1)
    cells = terms.shape[1]
    total = terms[:rows]
    for at, (by_row, by_col) in ((1, (0, 1)), (2, (1, 0)), (3, (1, 1))):
        moved = pltpu.roll(terms[at * rows : (at + 1) * rows], cells - by_row * row_len - by_col, 1)
        keep = lane < cells - row_len if by_row else None
        if by_col:
            inner = lane % row_len != row_len - 1
            keep = inner if keep is None else jnp.logical_and(keep, inner)
        total = total + jnp.where(keep, moved, 0.0)
    return total


def cot_copies(place_ref, mine, theirs_ref, cot_ref, sems):
    ring = len(mine)
    half = cot_ref.shape[3] // 2
    z, core = place_ref[1], place_ref[2]
    here = pl.ds(pl.multiple_of(core * half, 128), half)
    there = pl.ds(pl.multiple_of((1 - core) * half, 128), half)
    copies = []
    for k in range(ring):
        to = lax.rem(z + k, ring)
        for side, (source, part) in enumerate(((mine[k], here), (theirs_ref.at[k], there))):
            copies.append(
                pltpu.make_async_copy(source, cot_ref.at[:, to, :, part], sems.at[2 * k + side])
            )
    return copies


def grad_kernel(row_len, place_ref, hidden_ref, *refs):
    mine, theirs_ref, refs = refs[:RING], refs[RING], refs[RING + 1 :]
    outs_refs, (cot_ref, sems, even_ref, odd_ref, sum_ref) = refs[:-5], refs[-5:]
    copies = cot_copies(place_ref, mine, theirs_ref, cot_ref, sems)
    for copy in copies:
        copy.start()
    planes, group, cells = hidden_ref.shape
    steps = planes // 2
    own = group // 4
    unit = own // len(outs_refs)
    for s in range(steps):
        here = slice(s * cells, (s + 1) * cells)
        even_ref[:, here] = spread(hidden_ref[2 * s], row_len)
        odd_ref[:, here] = spread(hidden_ref[2 * s + 1], row_len)
    for copy in copies:
        copy.wait()
    over_cells = (((1,), (1,)), ((), ()))
    sources = ((odd_ref, cells), (even_ref, 0), (odd_ref, 0))
    for depth_tap, (rows_ref, start) in enumerate(sources):
        total = lax.dot_general(
            rows_ref[...],
            cot_ref[:, :, :, start : start + steps * cells].reshape(-1, steps * cells),
            over_cells,
            preferred_element_type=jnp.float32,
        )
        for row_tap in range(3):
            for col_tap in range(3):
                at = (2 * int(row_tap == 0) + int(col_tap == 0)) * group
                at += (2 * int(row_tap != 1) + int(col_tap != 1)) * own
                put = ((depth_tap * 3 + row_tap) * 3 + col_tap) * unit
                for y in range(len(outs_refs)):
                    first = at + y * unit
                    sum_ref[y, put : put + unit, :] = total[first : first + unit, :]
    for away, out_ref in enumerate(outs_refs):
        y = lax.rem(place_ref[0] + away, len(outs_refs))
        out_ref[...] = sum_ref[y].astype(out_ref.dtype)


def grad(place, hidden, mine, theirs, row_len):
    planes, group, cells = hidden.shape
    cot_shape = mine[0].shape[:1] + (RING,) + mine[0].shape[1:2] + (2 * mine[0].shape[2],)
    outs = cot_shape[0] * cot_shape[1] * cot_shape[2]
    rows = pltpu.VMEM((4 * group, planes // 2 * cells), jnp.bfloat16)
    size = 27 * group // (4 * ROWS)
    return pl.pallas_call(
        functools.partial(grad_kernel, row_len),
        out_shape=[
            jax.ShapeDtypeStruct((size, outs), jnp.bfloat16 if away else jnp.float32)
            for away in range(ROWS)
        ],
        in_specs=[pl.BlockSpec(memory_space=pltpu.SMEM), IN_VMEM] + [ANYWHERE] * (RING + 1),
        out_specs=[IN_VMEM] * ROWS,
        scratch_shapes=[
            pltpu.VMEM(cot_shape, jnp.bfloat16),
            pltpu.SemaphoreType.DMA((2 * RING,)),
            rows,
            rows,
            pltpu.VMEM((ROWS, size, outs), jnp.float32),
        ],
        compiler_params=GRANT,
        cost_estimate=pl.CostEstimate(
            flops=12 * group * outs * planes * cells, bytes_accessed=2**22, transcendentals=0
        ),
    )(place, hidden, *mine, theirs)


def back_kernel(row_len, place_ref, *refs):
    w_refs, mine, theirs_ref = refs[:ROWS], refs[ROWS : ROWS + RING], refs[ROWS + RING]
    out_ref, cot_ref, sems, rows_ref, moves_ref = refs[ROWS + RING + 1 :]
    planes, group, cells = out_ref.shape
    row_count = ROWS
    y = place_ref[0]
    copies = cot_copies(place_ref, mine, theirs_ref, cot_ref, sems)
    for copy in copies:
        copy.start()

    for away, w_ref in enumerate(w_refs):
        rows_ref[lax.rem(y + away, row_count)] = w_ref[...].astype(jnp.float32)
    block = group // 4
    own = block // row_count
    size = 4 * group
    moves_ref[...] = jnp.zeros_like(moves_ref)
    for tap in range(27):
        depth_tap, row_tap, col_tap = tap // 9, tap // 3 % 3, tap % 3
        at = depth_tap * size + (2 * int(row_tap == 0) + int(col_tap == 0)) * group
        at += (2 * int(row_tap != 1) + int(col_tap != 1)) * block
        pieces = [rows_ref[row, tap * own : (tap + 1) * own, :] for row in range(row_count)]
        moves_ref[at : at + block, :] = jnp.concatenate(pieces, 0).astype(moves_ref.dtype)

    for copy in copies:
        copy.wait()

    def one(at, start):
        return jnp.dot(
            moves_ref[at * size : (at + 1) * size, :],
            cot_ref[:, :, :, start : start + cells].reshape(-1, cells),
            preferred_element_type=jnp.float32,
        )

    for s in range(planes // 2):
        start = s * cells
        out_ref[2 * s] = gather_back(one(1, start), row_len).astype(out_ref.dtype)
        odd = one(2, start) + one(0, start + cells)
        out_ref[2 * s + 1] = gather_back(odd, row_len).astype(out_ref.dtype)


def back(place, w_rel, mine, theirs, planes, row_len):
    size, outs = w_rel[0].shape
    group = 4 * ROWS * size // 27
    cot_shape = mine[0].shape[:1] + (RING,) + mine[0].shape[1:2] + (2 * mine[0].shape[2],)
    cells = cot_shape[3] // (planes // 2 + 1)
    return pl.pallas_call(
        functools.partial(back_kernel, row_len),
        out_shape=jax.ShapeDtypeStruct((planes, group, cells), jnp.bfloat16),
        in_specs=[pl.BlockSpec(memory_space=pltpu.SMEM)] + [IN_VMEM] * ROWS + [ANYWHERE] * (RING + 1),
        out_specs=IN_VMEM,
        scratch_shapes=[
            pltpu.VMEM(cot_shape, jnp.bfloat16),
            pltpu.SemaphoreType.DMA((2 * RING,)),
            pltpu.VMEM((ROWS, size, outs), jnp.float32),
            pltpu.VMEM((12 * group, outs), jnp.bfloat16),
        ],
        compiler_params=GRANT,
        cost_estimate=pl.CostEstimate(
            flops=12 * group * outs * planes * cells, bytes_accessed=2**22, transcendentals=0
        ),
    )(place, *w_rel, *mine, theirs)


def on_space(block, y_by=0, z_by=0, core_by=0):
    route = []
    for y in range(ROWS):
        for z in range(RING):
            for core in range(CORES):
                to = ((y + y_by) % ROWS, (z + z_by) % RING, (core + core_by) % CORES)
                route.append(((y * RING + z) * CORES + core, (to[0] * RING + to[1]) * CORES + to[2]))
    return lax.ppermute(block, "space", route)


CHIPS = [(y, z) for y in range(ROWS) for z in range(RING)]


def members(pick):
    groups = {}
    for y, z in CHIPS:
        for core in range(CORES):
            groups.setdefault(pick(y, z, core), []).append((y * RING + z) * CORES + core)
    return list(groups.values())


COLUMNS = members(lambda y, z, core: (z, core))
PILLARS = members(lambda y, z, core: z)
SLABS = members(lambda y, z, core: y)


def exchange(blocks, groups):
    return lax.all_to_all(
        blocks, "space", split_axis=0, concat_axis=0, axis_index_groups=groups, tiled=True
    )


def section(volume, w_first, w_second, cotangent):
    channels = volume.shape[1]
    cells = volume.shape[4]
    outs = w_first.shape[4]
    own = w_second.shape[3]
    row_len = WID // 4
    me = lax.axis_index("space")
    y, z, core = me // (RING * CORES), me // CORES % RING, me % CORES
    place = jnp.stack([y, z, core]).astype(jnp.int32)
    group = RING * CORES

    share = cotangent.shape[2] // ROWS
    local = jnp.pad(cotangent[0], ((0, 0), (0, 1), (0, 0)))
    parts = jnp.stack([local[:, at * share : (at + 1) * share + 1] for at in range(ROWS)])
    parts = parts.reshape(ROWS, -1, CORES, (share + 1) * cells // CORES).transpose(0, 2, 1, 3)
    first = exchange(parts.reshape((ROWS * CORES,) + parts.shape[2:]), PILLARS)
    first = first.reshape(ROWS, -1, first.shape[2])
    up, down = [first], [first]
    for _ in range(3):
        up.append(on_space(up[-1], z_by=1))
        down.append(on_space(down[-1], z_by=-1))
    far = on_space(up[3], z_by=1)
    mine = down + [far] + up[:0:-1]
    piled = pile(mine)
    theirs = on_space(piled, core_by=1)

    w_rel = [w_second.reshape(27 * own, C3)]
    for step in range(1, ROWS):
        w_rel.append(on_space(w_rel[0], y_by=-step))

    planes = volume[0].transpose(1, 2, 0, 3).reshape(2, 16 * channels, cells)
    w_rows = w_first.reshape(27 * channels, outs)
    ahead, part = conv(w_rows, planes, row_len)
    behind = from_behind(ahead, "space", 1)
    hidden = pointwise(activate, part, behind, group, jnp.bfloat16)
    slopes = pointwise(slope_of, part, behind, group, jnp.float32)
    by_plane = exchange(hidden, SLABS)

    back_terms = back(place, w_rel, mine, theirs, group, row_len)
    hidden_grad = exchange(back_terms, SLABS)

    partial, *others = grad(place, by_plane, mine, theirs, row_len)
    for step, block in enumerate(others, 1):
        partial = partial + on_space(block, y_by=step).astype(jnp.float32)
    partial = partial.astype(jnp.bfloat16)
    sides = []
    for distance in (1, 2, 3):
        sides.append(from_side(partial, "dp", distance).astype(jnp.float32))
    grad_second = (partial.astype(jnp.float32) + sides[1]) + (sides[0] + sides[2])
    grad_second = grad_second.reshape(3, 3, 3, own, C3)

    pre_grad = (hidden_grad.astype(jnp.float32) * slopes).astype(jnp.bfloat16)
    pre_grad = pre_grad.reshape(group, 4, ROWS, own, cells).transpose(2, 0, 3, 1, 4)
    return (grad_second, pre_grad.reshape(1, outs, 1, 4, cells))


def solution(mesh):
    in_specs = (
        P("dp", None, "space", None, None),
        P(),
        P(None, None, None, "space", None),
        P("dp", "space", None, None),
    )
    out_specs = (P(None, None, None, "space", None), P("dp", None, "space", None, None))
    return jax.shard_map(
        section, mesh=mesh, in_specs=in_specs, out_specs=out_specs, check_vma=False
    )
```

```python
import functools

import jax
import jax.numpy as jnp
from jax import lax
from jax.experimental import pallas as pl
from jax.experimental.pallas import tpu as pltpu
from jax.sharding import PartitionSpec as P


C3 = 512
WID = 128


leak_slope = 0.3


def from_behind(block, axis, distance):
    devices = range(lax.axis_size(axis))
    route = [(i - distance, i) for i in devices if i - distance in devices]
    return lax.ppermute(block, axis, route)


def from_side(block, axis, distance):
    size = lax.axis_size(axis)
    return lax.ppermute(block, axis, [(i, (i + distance) % size) for i in range(size)])


def activate(values):
    return leak_slope * values + (1.0 - leak_slope) * values * jax.nn.sigmoid(values)


def slope_of(values):
    sigmoid_value = jax.nn.sigmoid(values)
    return leak_slope + (1.0 - leak_slope) * (
        sigmoid_value + values * sigmoid_value * (1.0 - sigmoid_value)
    )


ROWS, RING, CORES = 4, 8, 2
IN_VMEM = pl.BlockSpec(memory_space=pltpu.VMEM)
IN_HBM = pl.BlockSpec(memory_space=pltpu.HBM)
GRANT = pltpu.CompilerParams(vmem_limit_bytes=16 * 2**20)


def shifted(block, by_row, by_col, row_len):
    moved = block.astype(jnp.float32)
    lane = lax.broadcasted_iota(jnp.int32, moved.shape, 1)
    moved = pltpu.roll(moved, by_row * row_len + by_col, 1)
    keep = None
    if by_row:
        keep = lane >= row_len
    if by_col:
        inner = lane % row_len != 0
        keep = inner if keep is None else jnp.logical_and(keep, inner)
    return jnp.where(keep, moved, 0.0).astype(block.dtype)


def conv_kernel(row_len, w_from, planes_ref, ahead_ref, part_ref, cols_ref, w_ref, sem):
    copy = pltpu.make_async_copy(w_from, w_ref, sem)
    copy.start()
    cells = planes_ref.shape[2]
    channels = planes_ref.shape[1] // 16
    tap_rows = 9 * channels
    for plane in range(2):
        for row in range(-1, 4):
            for col in range(-1, 4):
                source = ((row % 4) * 4 + col % 4) * channels
                block = planes_ref[plane, source : source + channels, :]
                if row < 0 or col < 0:
                    block = shifted(block, int(row < 0), int(col < 0), row_len)
                for row_phase in range(2):
                    row_tap = row + 1 - 2 * row_phase
                    if not 0 <= row_tap <= 2:
                        continue
                    for col_phase in range(2):
                        col_tap = col + 1 - 2 * col_phase
                        if not 0 <= col_tap <= 2:
                            continue
                        start = plane * tap_rows + (row_tap * 3 + col_tap) * channels
                        phase = row_phase * 2 + col_phase
                        put = slice(phase * cells, (phase + 1) * cells)
                        cols_ref[start : start + channels, put] = block
    copy.wait()
    over_rows = (((0,), (0,)), ((), ()))
    for out_ref, weights, cols in (
        (ahead_ref, w_ref[:tap_rows, :], cols_ref[tap_rows:, :]),
        (part_ref, w_ref[tap_rows:, :], cols_ref[...]),
    ):
        total = lax.dot_general(weights, cols, over_rows, preferred_element_type=jnp.float32)
        for phase in range(4):
            out_ref[phase] = total[:, phase * cells : (phase + 1) * cells].astype(out_ref.dtype)


def conv(w_rows, planes, row_len):
    depth, outs = w_rows.shape
    cells = planes.shape[2]
    return pl.pallas_call(
        functools.partial(conv_kernel, row_len),
        out_shape=(
            jax.ShapeDtypeStruct((4, outs, cells), jnp.bfloat16),
            jax.ShapeDtypeStruct((4, outs, cells), jnp.float32),
        ),
        in_specs=[IN_HBM, IN_VMEM],
        out_specs=(IN_VMEM,) * 2,
        scratch_shapes=[
            pltpu.VMEM((2 * depth // 3, 4 * cells), jnp.bfloat16),
            pltpu.VMEM(w_rows.shape, jnp.bfloat16),
            pltpu.SemaphoreType.DMA(()),
        ],
        compiler_params=GRANT,
        cost_estimate=pl.CostEstimate(
            flops=8 * outs * depth * cells, bytes_accessed=4 * depth * cells, transcendentals=0
        ),
    )(w_rows, planes)


def regrouped(values, own, at):
    outs = values.shape[0]
    starts = range(at * own, outs, outs // ROWS)
    return jnp.concatenate([values[start : start + own] for start in starts], 0)


def pointwise_kernel(rule, part_ref, behind_ref, result_ref):
    groups, rows, _ = result_ref.shape
    unit = rows // 4
    for phase in range(4):
        values = rule(part_ref[phase] + behind_ref[phase].astype(jnp.float32))
        for at in range(groups):
            block = regrouped(values, unit // ROWS, at)
            result_ref[at, phase * unit : (phase + 1) * unit, :] = block.astype(result_ref.dtype)


def pointwise(rule, part, behind, groups, dtype):
    phases, outs, cells = part.shape
    return pl.pallas_call(
        functools.partial(pointwise_kernel, rule),
        out_shape=jax.ShapeDtypeStruct((groups, phases * outs // groups, cells), dtype),
        in_specs=[IN_VMEM] * 2,
        out_specs=IN_VMEM,
        compiler_params=GRANT,
        cost_estimate=pl.CostEstimate(
            flops=10 * part.size, bytes_accessed=8 * part.size, transcendentals=part.size
        ),
    )(part, behind)


def pile_kernel(*refs):
    blocks, out_ref, sems = refs[:-2], refs[-2], refs[-1]
    copies = [
        pltpu.make_async_copy(block, out_ref.at[at], sems.at[at]) for at, block in enumerate(blocks)
    ]
    for copy in copies:
        copy.start()
    for copy in copies:
        copy.wait()


def pile(blocks):
    shape = (len(blocks),) + blocks[0].shape
    return pl.pallas_call(
        pile_kernel,
        out_shape=jax.ShapeDtypeStruct(shape, blocks[0].dtype),
        in_specs=[IN_HBM] * len(blocks),
        out_specs=IN_VMEM,
        scratch_shapes=[pltpu.SemaphoreType.DMA((len(blocks),))],
        compiler_params=GRANT,
        cost_estimate=pl.CostEstimate(
            flops=0, bytes_accessed=4 * len(blocks) * blocks[0].size, transcendentals=0
        ),
    )(*blocks)


def spread(block, row_len):
    return jnp.concatenate(
        [block]
        + [shifted(block, by_row, by_col, row_len) for by_row, by_col in ((0, 1), (1, 0), (1, 1))],
        0,
    )


def gather_back(terms, row_len):
    rows = terms.shape[0] // 4
    lane = lax.broadcasted_iota(jnp.int32, (rows, terms.shape[1]), 1)
    cells = terms.shape[1]
    total = terms[:rows]
    for at, (by_row, by_col) in ((1, (0, 1)), (2, (1, 0)), (3, (1, 1))):
        moved = pltpu.roll(terms[at * rows : (at + 1) * rows], cells - by_row * row_len - by_col, 1)
        keep = lane < cells - row_len if by_row else None
        if by_col:
            inner = lane % row_len != row_len - 1
            keep = inner if keep is None else jnp.logical_and(keep, inner)
        total = total + jnp.where(keep, moved, 0.0)
    return total


def cot_copies(place_ref, mine, theirs_ref, cot_ref, sems):
    ring = len(mine)
    half = cot_ref.shape[3] // 2
    z, core = place_ref[1], place_ref[2]
    here = pl.ds(pl.multiple_of(core * half, 128), half)
    there = pl.ds(pl.multiple_of((1 - core) * half, 128), half)
    copies = []
    for k in range(ring):
        to = lax.rem(z + k, ring)
        for side, (source, part) in enumerate(((mine[k], here), (theirs_ref.at[k], there))):
            copies.append(
                pltpu.make_async_copy(source, cot_ref.at[:, to, :, part], sems.at[2 * k + side])
            )
    return copies


def grad_kernel(row_len, place_ref, hidden_ref, *refs):
    mine, theirs_ref, refs = refs[:RING], refs[RING], refs[RING + 1 :]
    outs_refs, (cot_ref, sems, even_ref, odd_ref, sum_ref) = refs[:-5], refs[-5:]
    copies = cot_copies(place_ref, mine, theirs_ref, cot_ref, sems)
    for copy in copies:
        copy.start()
    planes, group, cells = hidden_ref.shape
    steps = planes // 2
    own = group // 4
    unit = own // len(outs_refs)
    for s in range(steps):
        here = slice(s * cells, (s + 1) * cells)
        even_ref[:, here] = spread(hidden_ref[2 * s], row_len)
        odd_ref[:, here] = spread(hidden_ref[2 * s + 1], row_len)
    for copy in copies:
        copy.wait()
    over_cells = (((1,), (1,)), ((), ()))
    sources = ((odd_ref, cells), (even_ref, 0), (odd_ref, 0))
    for depth_tap, (rows_ref, start) in enumerate(sources):
        total = lax.dot_general(
            rows_ref[...],
            cot_ref[:, :, :, start : start + steps * cells].reshape(-1, steps * cells),
            over_cells,
            preferred_element_type=jnp.float32,
        )
        for row_tap in range(3):
            for col_tap in range(3):
                at = (2 * int(row_tap == 0) + int(col_tap == 0)) * group
                at += (2 * int(row_tap != 1) + int(col_tap != 1)) * own
                put = ((depth_tap * 3 + row_tap) * 3 + col_tap) * unit
                for y in range(len(outs_refs)):
                    first = at + y * unit
                    sum_ref[y, put : put + unit, :] = total[first : first + unit, :]
    for away, out_ref in enumerate(outs_refs):
        y = lax.rem(place_ref[0] + away, len(outs_refs))
        out_ref[...] = sum_ref[y].astype(out_ref.dtype)


def grad(place, hidden, mine, theirs, row_len):
    planes, group, cells = hidden.shape
    cot_shape = mine[0].shape[:1] + (RING,) + mine[0].shape[1:2] + (2 * mine[0].shape[2],)
    outs = cot_shape[0] * cot_shape[1] * cot_shape[2]
    rows = pltpu.VMEM((4 * group, planes // 2 * cells), jnp.bfloat16)
    size = 27 * group // (4 * ROWS)
    return pl.pallas_call(
        functools.partial(grad_kernel, row_len),
        out_shape=[
            jax.ShapeDtypeStruct((size, outs), jnp.bfloat16 if away else jnp.float32)
            for away in range(ROWS)
        ],
        in_specs=[pl.BlockSpec(memory_space=pltpu.SMEM), IN_VMEM] + [IN_HBM] * (RING + 1),
        out_specs=[IN_VMEM] * ROWS,
        scratch_shapes=[
            pltpu.VMEM(cot_shape, jnp.bfloat16),
            pltpu.SemaphoreType.DMA((2 * RING,)),
            rows,
            rows,
            pltpu.VMEM((ROWS, size, outs), jnp.float32),
        ],
        compiler_params=GRANT,
        cost_estimate=pl.CostEstimate(
            flops=12 * group * outs * planes * cells, bytes_accessed=2**22, transcendentals=0
        ),
    )(place, hidden, *mine, theirs)


def back_kernel(row_len, place_ref, *refs):
    w_refs, mine, theirs_ref = refs[:ROWS], refs[ROWS : ROWS + RING], refs[ROWS + RING]
    out_ref, cot_ref, sems, rows_ref, moves_ref = refs[ROWS + RING + 1 :]
    planes, group, cells = out_ref.shape
    row_count = ROWS
    y = place_ref[0]
    copies = cot_copies(place_ref, mine, theirs_ref, cot_ref, sems)
    for copy in copies:
        copy.start()

    for away, w_ref in enumerate(w_refs):
        rows_ref[lax.rem(y + away, row_count)] = w_ref[...].astype(jnp.float32)
    block = group // 4
    own = block // row_count
    size = 4 * group
    moves_ref[...] = jnp.zeros_like(moves_ref)
    for tap in range(27):
        depth_tap, row_tap, col_tap = tap // 9, tap // 3 % 3, tap % 3
        at = depth_tap * size + (2 * int(row_tap == 0) + int(col_tap == 0)) * group
        at += (2 * int(row_tap != 1) + int(col_tap != 1)) * block
        pieces = [rows_ref[row, tap * own : (tap + 1) * own, :] for row in range(row_count)]
        moves_ref[at : at + block, :] = jnp.concatenate(pieces, 0).astype(moves_ref.dtype)

    for copy in copies:
        copy.wait()

    def one(at, start):
        return jnp.dot(
            moves_ref[at * size : (at + 1) * size, :],
            cot_ref[:, :, :, start : start + cells].reshape(-1, cells),
            preferred_element_type=jnp.float32,
        )

    for s in range(planes // 2):
        start = s * cells
        out_ref[2 * s] = gather_back(one(1, start), row_len).astype(out_ref.dtype)
        odd = one(2, start) + one(0, start + cells)
        out_ref[2 * s + 1] = gather_back(odd, row_len).astype(out_ref.dtype)


def back(place, w_rel, mine, theirs, planes, row_len):
    size, outs = w_rel[0].shape
    group = 4 * ROWS * size // 27
    cot_shape = mine[0].shape[:1] + (RING,) + mine[0].shape[1:2] + (2 * mine[0].shape[2],)
    cells = cot_shape[3] // (planes // 2 + 1)
    return pl.pallas_call(
        functools.partial(back_kernel, row_len),
        out_shape=jax.ShapeDtypeStruct((planes, group, cells), jnp.bfloat16),
        in_specs=[pl.BlockSpec(memory_space=pltpu.SMEM)] + [IN_VMEM] * ROWS + [IN_HBM] * (RING + 1),
        out_specs=IN_VMEM,
        scratch_shapes=[
            pltpu.VMEM(cot_shape, jnp.bfloat16),
            pltpu.SemaphoreType.DMA((2 * RING,)),
            pltpu.VMEM((ROWS, size, outs), jnp.float32),
            pltpu.VMEM((12 * group, outs), jnp.bfloat16),
        ],
        compiler_params=GRANT,
        cost_estimate=pl.CostEstimate(
            flops=12 * group * outs * planes * cells, bytes_accessed=2**22, transcendentals=0
        ),
    )(place, *w_rel, *mine, theirs)


def on_space(block, y_by=0, z_by=0, core_by=0):
    route = []
    for y in range(ROWS):
        for z in range(RING):
            for core in range(CORES):
                to = ((y + y_by) % ROWS, (z + z_by) % RING, (core + core_by) % CORES)
                route.append(((y * RING + z) * CORES + core, (to[0] * RING + to[1]) * CORES + to[2]))
    return lax.ppermute(block, "space", route)


CHIPS = [(y, z) for y in range(ROWS) for z in range(RING)]


def members(pick):
    groups = {}
    for y, z in CHIPS:
        for core in range(CORES):
            groups.setdefault(pick(y, z, core), []).append((y * RING + z) * CORES + core)
    return list(groups.values())


COLUMNS = members(lambda y, z, core: (z, core))
PILLARS = members(lambda y, z, core: z)
SLABS = members(lambda y, z, core: y)


def exchange(blocks, groups):
    return lax.all_to_all(
        blocks, "space", split_axis=0, concat_axis=0, axis_index_groups=groups, tiled=True
    )


def section(volume, w_first, w_second, cotangent):
    channels = volume.shape[1]
    cells = volume.shape[4]
    outs = w_first.shape[4]
    own = w_second.shape[3]
    row_len = WID // 4
    me = lax.axis_index("space")
    y, z, core = me // (RING * CORES), me // CORES % RING, me % CORES
    place = jnp.stack([y, z, core]).astype(jnp.int32)
    group = RING * CORES

    share = cotangent.shape[2] // ROWS
    local = jnp.pad(cotangent[0], ((0, 0), (0, 1), (0, 0)))
    parts = jnp.stack([local[:, at * share : (at + 1) * share + 1] for at in range(ROWS)])
    parts = parts.reshape(ROWS, -1, CORES, (share + 1) * cells // CORES).transpose(0, 2, 1, 3)
    first = exchange(parts.reshape((ROWS * CORES,) + parts.shape[2:]), PILLARS)
    first = first.reshape(ROWS, -1, first.shape[2])
    hops = {0: first}
    for step in (1, -1, 2, -2):
        hops[step] = on_space(first, z_by=-step)
    for step, come in ((3, 2), (-3, -2), (4, 2)):
        hops[step] = on_space(hops[come], z_by=come - step)
    mine = [hops[step] for step in (0, 1, 2, 3, 4, -3, -2, -1)]
    piled = pile(mine)
    theirs = on_space(piled, core_by=1)

    w_rel = [w_second.reshape(27 * own, C3)]
    for step in range(1, ROWS):
        w_rel.append(on_space(w_rel[0], y_by=-step))

    planes = volume[0].transpose(1, 2, 0, 3).reshape(2, 16 * channels, cells)
    w_rows = w_first.reshape(27 * channels, outs)
    ahead, part = conv(w_rows, planes, row_len)
    behind = from_behind(ahead, "space", 1)
    hidden = pointwise(activate, part, behind, group, jnp.bfloat16)
    slopes = pointwise(slope_of, part, behind, group, jnp.float32)
    by_plane = exchange(hidden, SLABS)

    back_terms = back(place, w_rel, mine, theirs, group, row_len)
    hidden_grad = exchange(back_terms, SLABS)

    partial, *others = grad(place, by_plane, mine, theirs, row_len)
    for step, block in enumerate(others, 1):
        partial = partial + on_space(block, y_by=step).astype(jnp.float32)
    partial = partial.astype(jnp.bfloat16)
    sides = []
    for distance in (1, 2, 3):
        sides.append(from_side(partial, "dp", distance).astype(jnp.float32))
    grad_second = (partial.astype(jnp.float32) + sides[1]) + (sides[0] + sides[2])
    grad_second = grad_second.reshape(3, 3, 3, own, C3)

    pre_grad = (hidden_grad.astype(jnp.float32) * slopes).astype(jnp.bfloat16)
    pre_grad = pre_grad.reshape(group, 4, ROWS, own, cells).transpose(2, 0, 3, 1, 4)
    return (grad_second, pre_grad.reshape(1, outs, 1, 4, cells))


def solution(mesh):
    in_specs = (
        P("dp", None, "space", None, None),
        P(),
        P(None, None, None, "space", None),
        P("dp", "space", None, None),
    )
    out_specs = (P(None, None, None, "space", None), P("dp", None, "space", None, None))
    return jax.shard_map(
        section, mesh=mesh, in_specs=in_specs, out_specs=out_specs, check_vma=False
    )
```

```python
import functools

import jax
import jax.numpy as jnp
from jax import lax
from jax.experimental import pallas as pl
from jax.experimental.pallas import tpu as pltpu
from jax.sharding import PartitionSpec as P


C3 = 512
WID = 128


leak_slope = 0.3


def from_behind(block, axis, distance):
    devices = range(lax.axis_size(axis))
    route = [(i - distance, i) for i in devices if i - distance in devices]
    return lax.ppermute(block, axis, route)


def from_side(block, axis, distance):
    size = lax.axis_size(axis)
    return lax.ppermute(block, axis, [(i, (i + distance) % size) for i in range(size)])


def activate(values):
    return leak_slope * values + (1.0 - leak_slope) * values * jax.nn.sigmoid(values)


def slope_of(values):
    sigmoid_value = jax.nn.sigmoid(values)
    return leak_slope + (1.0 - leak_slope) * (
        sigmoid_value + values * sigmoid_value * (1.0 - sigmoid_value)
    )


ROWS, RING, CORES = 4, 8, 2
IN_VMEM = pl.BlockSpec(memory_space=pltpu.VMEM)
IN_HBM = pl.BlockSpec(memory_space=pltpu.HBM)
GRANT = pltpu.CompilerParams(vmem_limit_bytes=16 * 2**20)


def shifted(block, by_row, by_col, row_len):
    moved = block.astype(jnp.float32)
    lane = lax.broadcasted_iota(jnp.int32, moved.shape, 1)
    moved = pltpu.roll(moved, by_row * row_len + by_col, 1)
    keep = None
    if by_row:
        keep = lane >= row_len
    if by_col:
        inner = lane % row_len != 0
        keep = inner if keep is None else jnp.logical_and(keep, inner)
    return jnp.where(keep, moved, 0.0).astype(block.dtype)


def conv_kernel(row_len, w_from, planes_ref, ahead_ref, part_ref, cols_ref, w_ref, sem):
    copy = pltpu.make_async_copy(w_from, w_ref, sem)
    copy.start()
    cells = planes_ref.shape[2]
    channels = planes_ref.shape[1] // 16
    tap_rows = 9 * channels
    for plane in range(2):
        for row in range(-1, 4):
            for col in range(-1, 4):
                source = ((row % 4) * 4 + col % 4) * channels
                block = planes_ref[plane, source : source + channels, :]
                if row < 0 or col < 0:
                    block = shifted(block, int(row < 0), int(col < 0), row_len)
                for row_phase in range(2):
                    row_tap = row + 1 - 2 * row_phase
                    if not 0 <= row_tap <= 2:
                        continue
                    for col_phase in range(2):
                        col_tap = col + 1 - 2 * col_phase
                        if not 0 <= col_tap <= 2:
                            continue
                        start = plane * tap_rows + (row_tap * 3 + col_tap) * channels
                        phase = row_phase * 2 + col_phase
                        put = slice(phase * cells, (phase + 1) * cells)
                        cols_ref[start : start + channels, put] = block
    copy.wait()
    over_rows = (((0,), (0,)), ((), ()))
    for out_ref, weights, cols in (
        (ahead_ref, w_ref[:tap_rows, :], cols_ref[tap_rows:, :]),
        (part_ref, w_ref[tap_rows:, :], cols_ref[...]),
    ):
        total = lax.dot_general(weights, cols, over_rows, preferred_element_type=jnp.float32)
        for phase in range(4):
            out_ref[phase] = total[:, phase * cells : (phase + 1) * cells].astype(out_ref.dtype)


def conv(w_rows, planes, row_len):
    depth, outs = w_rows.shape
    cells = planes.shape[2]
    return pl.pallas_call(
        functools.partial(conv_kernel, row_len),
        out_shape=(
            jax.ShapeDtypeStruct((4, outs, cells), jnp.bfloat16),
            jax.ShapeDtypeStruct((4, outs, cells), jnp.float32),
        ),
        in_specs=[IN_HBM, IN_VMEM],
        out_specs=(IN_VMEM,) * 2,
        scratch_shapes=[
            pltpu.VMEM((2 * depth // 3, 4 * cells), jnp.bfloat16),
            pltpu.VMEM(w_rows.shape, jnp.bfloat16),
            pltpu.SemaphoreType.DMA(()),
        ],
        compiler_params=GRANT,
        cost_estimate=pl.CostEstimate(
            flops=8 * outs * depth * cells, bytes_accessed=4 * depth * cells, transcendentals=0
        ),
    )(w_rows, planes)


def regrouped(values, own, at):
    outs = values.shape[0]
    starts = range(at * own, outs, outs // ROWS)
    return jnp.concatenate([values[start : start + own] for start in starts], 0)


def pointwise_kernel(rule, part_ref, behind_ref, result_ref):
    groups, rows, _ = result_ref.shape
    unit = rows // 4
    for phase in range(4):
        values = rule(part_ref[phase] + behind_ref[phase].astype(jnp.float32))
        for at in range(groups):
            block = regrouped(values, unit // ROWS, at)
            result_ref[at, phase * unit : (phase + 1) * unit, :] = block.astype(result_ref.dtype)


def pointwise(rule, part, behind, groups, dtype):
    phases, outs, cells = part.shape
    return pl.pallas_call(
        functools.partial(pointwise_kernel, rule),
        out_shape=jax.ShapeDtypeStruct((groups, phases * outs // groups, cells), dtype),
        in_specs=[IN_VMEM] * 2,
        out_specs=IN_VMEM,
        compiler_params=GRANT,
        cost_estimate=pl.CostEstimate(
            flops=10 * part.size, bytes_accessed=8 * part.size, transcendentals=part.size
        ),
    )(part, behind)


def pile_kernel(*refs):
    blocks, out_ref, sems = refs[:-2], refs[-2], refs[-1]
    copies = [
        pltpu.make_async_copy(block, out_ref.at[at], sems.at[at]) for at, block in enumerate(blocks)
    ]
    for copy in copies:
        copy.start()
    for copy in copies:
        copy.wait()


def pile(blocks):
    shape = (len(blocks),) + blocks[0].shape
    return pl.pallas_call(
        pile_kernel,
        out_shape=jax.ShapeDtypeStruct(shape, blocks[0].dtype),
        in_specs=[IN_HBM] * len(blocks),
        out_specs=IN_VMEM,
        scratch_shapes=[pltpu.SemaphoreType.DMA((len(blocks),))],
        compiler_params=GRANT,
        cost_estimate=pl.CostEstimate(
            flops=0, bytes_accessed=4 * len(blocks) * blocks[0].size, transcendentals=0
        ),
    )(*blocks)


def spread(block, row_len):
    return jnp.concatenate(
        [block]
        + [shifted(block, by_row, by_col, row_len) for by_row, by_col in ((0, 1), (1, 0), (1, 1))],
        0,
    )


def gather_back(terms, row_len):
    rows = terms.shape[0] // 4
    lane = lax.broadcasted_iota(jnp.int32, (rows, terms.shape[1]), 1)
    cells = terms.shape[1]
    total = terms[:rows]
    for at, (by_row, by_col) in ((1, (0, 1)), (2, (1, 0)), (3, (1, 1))):
        moved = pltpu.roll(terms[at * rows : (at + 1) * rows], cells - by_row * row_len - by_col, 1)
        keep = lane < cells - row_len if by_row else None
        if by_col:
            inner = lane % row_len != row_len - 1
            keep = inner if keep is None else jnp.logical_and(keep, inner)
        total = total + jnp.where(keep, moved, 0.0)
    return total


def cot_copies(place_ref, mine, theirs_ref, cot_ref, sems):
    ring = len(mine)
    half = cot_ref.shape[3] // 2
    z, core = place_ref[1], place_ref[2]
    here = pl.ds(pl.multiple_of(core * half, 128), half)
    there = pl.ds(pl.multiple_of((1 - core) * half, 128), half)
    copies = []
    for k in range(ring):
        to = lax.rem(z + k, ring)
        for side, (source, part) in enumerate(((mine[k], here), (theirs_ref.at[k], there))):
            copies.append(
                pltpu.make_async_copy(source, cot_ref.at[:, to, :, part], sems.at[2 * k + side])
            )
    return copies


def grad_kernel(row_len, place_ref, hidden_ref, *refs):
    mine, theirs_ref, refs = refs[:RING], refs[RING], refs[RING + 1 :]
    outs_refs, (cot_ref, sems, even_ref, odd_ref, sum_ref) = refs[:-5], refs[-5:]
    copies = cot_copies(place_ref, mine, theirs_ref, cot_ref, sems)
    for copy in copies:
        copy.start()
    planes, group, cells = hidden_ref.shape
    steps = planes // 2
    own = group // 4
    unit = own // len(outs_refs)
    for s in range(steps):
        here = slice(s * cells, (s + 1) * cells)
        even_ref[:, here] = spread(hidden_ref[2 * s], row_len)
        odd_ref[:, here] = spread(hidden_ref[2 * s + 1], row_len)
    for copy in copies:
        copy.wait()
    over_cells = (((1,), (1,)), ((), ()))
    sources = ((odd_ref, cells), (even_ref, 0), (odd_ref, 0))
    for depth_tap, (rows_ref, start) in enumerate(sources):
        total = lax.dot_general(
            rows_ref[...],
            cot_ref[:, :, :, start : start + steps * cells].reshape(-1, steps * cells),
            over_cells,
            preferred_element_type=jnp.float32,
        )
        for row_tap in range(3):
            for col_tap in range(3):
                at = (2 * int(row_tap == 0) + int(col_tap == 0)) * group
                at += (2 * int(row_tap != 1) + int(col_tap != 1)) * own
                put = ((depth_tap * 3 + row_tap) * 3 + col_tap) * unit
                for y in range(len(outs_refs)):
                    first = at + y * unit
                    sum_ref[y, put : put + unit, :] = total[first : first + unit, :]
    for away, out_ref in enumerate(outs_refs):
        y = lax.rem(place_ref[0] + away, len(outs_refs))
        out_ref[...] = sum_ref[y].astype(out_ref.dtype)


def grad(place, hidden, mine, theirs, row_len):
    planes, group, cells = hidden.shape
    cot_shape = mine[0].shape[:1] + (RING,) + mine[0].shape[1:2] + (2 * mine[0].shape[2],)
    outs = cot_shape[0] * cot_shape[1] * cot_shape[2]
    rows = pltpu.VMEM((4 * group, planes // 2 * cells), jnp.bfloat16)
    size = 27 * group // (4 * ROWS)
    return pl.pallas_call(
        functools.partial(grad_kernel, row_len),
        out_shape=[
            jax.ShapeDtypeStruct((size, outs), jnp.bfloat16 if away else jnp.float32)
            for away in range(ROWS)
        ],
        in_specs=[pl.BlockSpec(memory_space=pltpu.SMEM), IN_VMEM] + [IN_HBM] * (RING + 1),
        out_specs=[IN_VMEM] * ROWS,
        scratch_shapes=[
            pltpu.VMEM(cot_shape, jnp.bfloat16),
            pltpu.SemaphoreType.DMA((2 * RING,)),
            rows,
            rows,
            pltpu.VMEM((ROWS, size, outs), jnp.float32),
        ],
        compiler_params=GRANT,
        cost_estimate=pl.CostEstimate(
            flops=12 * group * outs * planes * cells, bytes_accessed=2**22, transcendentals=0
        ),
    )(place, hidden, *mine, theirs)


def moves_kernel(place_ref, *refs):
    w_refs, (moves_ref, rows_ref) = refs[:-2], refs[-2:]
    for away, w_ref in enumerate(w_refs):
        rows_ref[lax.rem(place_ref[0] + away, ROWS)] = w_ref[...].astype(jnp.float32)
    own = w_refs[0].shape[0] // 27
    block = ROWS * own
    group = 4 * block
    moves_ref[...] = jnp.zeros_like(moves_ref)
    for tap in range(27):
        depth_tap, row_tap, col_tap = tap // 9, tap // 3 % 3, tap % 3
        at = (4 * depth_tap + 2 * int(row_tap == 0) + int(col_tap == 0)) * group
        at += (2 * int(row_tap != 1) + int(col_tap != 1)) * block
        pieces = [rows_ref[row, tap * own : (tap + 1) * own, :] for row in range(ROWS)]
        moves_ref[at : at + block, :] = jnp.concatenate(pieces, 0).astype(moves_ref.dtype)


def moves_of(place, w_rel):
    size, outs = w_rel[0].shape
    return pl.pallas_call(
        moves_kernel,
        out_shape=jax.ShapeDtypeStruct((48 * ROWS * size // 27, outs), jnp.bfloat16),
        in_specs=[pl.BlockSpec(memory_space=pltpu.SMEM)] + [IN_VMEM] * ROWS,
        out_specs=IN_VMEM,
        scratch_shapes=[pltpu.VMEM((ROWS, size, outs), jnp.float32)],
        compiler_params=GRANT,
        cost_estimate=pl.CostEstimate(flops=0, bytes_accessed=2**20, transcendentals=0),
    )(place, *w_rel)


def back_kernel(row_len, place_ref, moves_ref, *refs):
    mine, theirs_ref, (out_ref, cot_ref, sems) = refs[:RING], refs[RING], refs[RING + 1 :]
    planes, group, cells = out_ref.shape
    size = 4 * group
    copies = cot_copies(place_ref, mine, theirs_ref, cot_ref, sems)
    for copy in copies:
        copy.start()
    for copy in copies:
        copy.wait()

    def one(at, start):
        return jnp.dot(
            moves_ref[at * size : (at + 1) * size, :],
            cot_ref[:, :, :, start : start + cells].reshape(-1, cells),
            preferred_element_type=jnp.float32,
        )

    for s in range(planes // 2):
        start = s * cells
        out_ref[2 * s] = gather_back(one(1, start), row_len).astype(out_ref.dtype)
        odd = one(2, start) + one(0, start + cells)
        out_ref[2 * s + 1] = gather_back(odd, row_len).astype(out_ref.dtype)


def back(place, moves, mine, theirs, planes, row_len):
    rows, outs = moves.shape
    group = rows // 12
    cot_shape = mine[0].shape[:1] + (RING,) + mine[0].shape[1:2] + (2 * mine[0].shape[2],)
    cells = cot_shape[3] // (planes // 2 + 1)
    return pl.pallas_call(
        functools.partial(back_kernel, row_len),
        out_shape=jax.ShapeDtypeStruct((planes, group, cells), jnp.bfloat16),
        in_specs=[pl.BlockSpec(memory_space=pltpu.SMEM), IN_VMEM] + [IN_HBM] * (RING + 1),
        out_specs=IN_VMEM,
        scratch_shapes=[
            pltpu.VMEM(cot_shape, jnp.bfloat16),
            pltpu.SemaphoreType.DMA((2 * RING,)),
        ],
        compiler_params=GRANT,
        cost_estimate=pl.CostEstimate(
            flops=12 * group * outs * planes * cells, bytes_accessed=2**22, transcendentals=0
        ),
    )(place, moves, *mine, theirs)


def on_space(block, y_by=0, z_by=0, core_by=0):
    route = []
    for y in range(ROWS):
        for z in range(RING):
            for core in range(CORES):
                to = ((y + y_by) % ROWS, (z + z_by) % RING, (core + core_by) % CORES)
                route.append(((y * RING + z) * CORES + core, (to[0] * RING + to[1]) * CORES + to[2]))
    return lax.ppermute(block, "space", route)


CHIPS = [(y, z) for y in range(ROWS) for z in range(RING)]


def members(pick):
    groups = {}
    for y, z in CHIPS:
        for core in range(CORES):
            groups.setdefault(pick(y, z, core), []).append((y * RING + z) * CORES + core)
    return list(groups.values())


COLUMNS = members(lambda y, z, core: (z, core))
PILLARS = members(lambda y, z, core: z)
SLABS = members(lambda y, z, core: y)


def exchange(blocks, groups):
    return lax.all_to_all(
        blocks, "space", split_axis=0, concat_axis=0, axis_index_groups=groups, tiled=True
    )


def section(volume, w_first, w_second, cotangent):
    channels = volume.shape[1]
    cells = volume.shape[4]
    outs = w_first.shape[4]
    own = w_second.shape[3]
    row_len = WID // 4
    me = lax.axis_index("space")
    y, z, core = me // (RING * CORES), me // CORES % RING, me % CORES
    place = jnp.stack([y, z, core]).astype(jnp.int32)
    group = RING * CORES

    share = cotangent.shape[2] // ROWS
    local = jnp.pad(cotangent[0], ((0, 0), (0, 1), (0, 0)))
    parts = jnp.stack([local[:, at * share : (at + 1) * share + 1] for at in range(ROWS)])
    parts = parts.reshape(ROWS, -1, CORES, (share + 1) * cells // CORES).transpose(0, 2, 1, 3)
    first = exchange(parts.reshape((ROWS * CORES,) + parts.shape[2:]), PILLARS)
    first = first.reshape(ROWS, -1, first.shape[2])
    hops = {0: first}
    for step in (1, -1, 2, -2):
        hops[step] = on_space(first, z_by=-step)
    for step, come in ((3, 2), (-3, -2), (4, 2)):
        hops[step] = on_space(hops[come], z_by=come - step)
    mine = [hops[step] for step in (0, 1, 2, 3, 4, -3, -2, -1)]
    piled = pile(mine)
    theirs = on_space(piled, core_by=1)

    w_rel = [w_second.reshape(27 * own, C3)]
    for step in range(1, ROWS):
        w_rel.append(on_space(w_rel[0], y_by=-step))

    planes = volume[0].transpose(1, 2, 0, 3).reshape(2, 16 * channels, cells)
    w_rows = w_first.reshape(27 * channels, outs)
    ahead, part = conv(w_rows, planes, row_len)
    behind = from_behind(ahead, "space", 1)
    hidden = pointwise(activate, part, behind, group, jnp.bfloat16)
    slopes = pointwise(slope_of, part, behind, group, jnp.float32)
    by_plane = exchange(hidden, SLABS)

    moves = moves_of(place, w_rel)
    back_terms = back(place, moves, mine, theirs, group, row_len)
    hidden_grad = exchange(back_terms, SLABS)

    partial, *others = grad(place, by_plane, mine, theirs, row_len)
    for step, block in enumerate(others, 1):
        partial = partial + on_space(block, y_by=step).astype(jnp.float32)
    partial = partial.astype(jnp.bfloat16)
    sides = []
    for distance in (1, 2, 3):
        sides.append(from_side(partial, "dp", distance).astype(jnp.float32))
    grad_second = (partial.astype(jnp.float32) + sides[1]) + (sides[0] + sides[2])
    grad_second = grad_second.reshape(3, 3, 3, own, C3)

    pre_grad = (hidden_grad.astype(jnp.float32) * slopes).astype(jnp.bfloat16)
    pre_grad = pre_grad.reshape(group, 4, ROWS, own, cells).transpose(2, 0, 3, 1, 4)
    pre_grad = pre_grad.reshape(1, outs, 1, 4, cells)
    return (grad_second, pre_grad)


def solution(mesh):
    in_specs = (
        P("dp", None, "space", None, None),
        P(),
        P(None, None, None, "space", None),
        P("dp", "space", None, None),
    )
    out_specs = (P(None, None, None, "space", None), P("dp", None, "space", None, None))
    return jax.shard_map(
        section, mesh=mesh, in_specs=in_specs, out_specs=out_specs, check_vma=False
    )
```

```python
import functools

import jax
import jax.numpy as jnp
from jax import lax
from jax.experimental import pallas as pl
from jax.experimental.pallas import tpu as pltpu
from jax.sharding import PartitionSpec as P


C3 = 512
WID = 128


leak_slope = 0.3


def from_behind(block, axis, distance):
    devices = range(lax.axis_size(axis))
    route = [(i - distance, i) for i in devices if i - distance in devices]
    return lax.ppermute(block, axis, route)


def from_side(block, axis, distance):
    size = lax.axis_size(axis)
    return lax.ppermute(block, axis, [(i, (i + distance) % size) for i in range(size)])


def activate(values):
    return leak_slope * values + (1.0 - leak_slope) * values * jax.nn.sigmoid(values)


def slope_of(values):
    sigmoid_value = jax.nn.sigmoid(values)
    return leak_slope + (1.0 - leak_slope) * (
        sigmoid_value + values * sigmoid_value * (1.0 - sigmoid_value)
    )


ROWS, RING, CORES = 4, 8, 2
IN_VMEM = pl.BlockSpec(memory_space=pltpu.VMEM)
IN_HBM = pl.BlockSpec(memory_space=pltpu.HBM)
GRANT = pltpu.CompilerParams(vmem_limit_bytes=16 * 2**20)


def shifted(block, by_row, by_col, row_len):
    moved = block.astype(jnp.float32)
    lane = lax.broadcasted_iota(jnp.int32, moved.shape, 1)
    moved = pltpu.roll(moved, by_row * row_len + by_col, 1)
    keep = None
    if by_row:
        keep = lane >= row_len
    if by_col:
        inner = lane % row_len != 0
        keep = inner if keep is None else jnp.logical_and(keep, inner)
    return jnp.where(keep, moved, 0.0).astype(block.dtype)


def conv_kernel(row_len, w_from, volume_from, ahead_ref, part_ref, *scratch):
    cols_ref, w_ref, volume_ref, planes_ref, sems = scratch
    moves = [
        pltpu.make_async_copy(volume_from.at[:, at * 16 : at * 16 + 16], volume_ref.at[at], sems.at[at])
        for at in range(2)
    ]
    copy = pltpu.make_async_copy(w_from, w_ref, sems.at[2])
    for move in moves:
        move.start()
    copy.start()
    for at in range(2):
        moves[at].wait()
        for first in range(0, volume_ref.shape[1], 16):
            turned = jnp.swapaxes(volume_ref[at, first : first + 16], 0, 1)
            for phase in range(16):
                row = phase * volume_ref.shape[1] + first
                planes_ref[at, row : row + 16, :] = turned[phase]
    cells = planes_ref.shape[2]
    channels = planes_ref.shape[1] // 16
    tap_rows = 9 * channels
    for plane in range(2):
        for row in range(-1, 4):
            for col in range(-1, 4):
                source = ((row % 4) * 4 + col % 4) * channels
                block = planes_ref[plane, source : source + channels, :]
                if row < 0 or col < 0:
                    block = shifted(block, int(row < 0), int(col < 0), row_len)
                for row_phase in range(2):
                    row_tap = row + 1 - 2 * row_phase
                    if not 0 <= row_tap <= 2:
                        continue
                    for col_phase in range(2):
                        col_tap = col + 1 - 2 * col_phase
                        if not 0 <= col_tap <= 2:
                            continue
                        start = plane * tap_rows + (row_tap * 3 + col_tap) * channels
                        phase = row_phase * 2 + col_phase
                        put = slice(phase * cells, (phase + 1) * cells)
                        cols_ref[start : start + channels, put] = block
    copy.wait()
    over_rows = (((0,), (0,)), ((), ()))
    for out_ref, weights, cols in (
        (ahead_ref, w_ref[:tap_rows, :], cols_ref[tap_rows:, :]),
        (part_ref, w_ref[tap_rows:, :], cols_ref[...]),
    ):
        total = lax.dot_general(weights, cols, over_rows, preferred_element_type=jnp.float32)
        for phase in range(4):
            out_ref[phase] = total[:, phase * cells : (phase + 1) * cells].astype(out_ref.dtype)


def conv(w_rows, volume, row_len):
    depth, outs = w_rows.shape
    channels, _, cells = volume.shape
    return pl.pallas_call(
        functools.partial(conv_kernel, row_len),
        out_shape=(
            jax.ShapeDtypeStruct((4, outs, cells), jnp.bfloat16),
            jax.ShapeDtypeStruct((4, outs, cells), jnp.float32),
        ),
        in_specs=[IN_HBM] * 2,
        out_specs=(IN_VMEM,) * 2,
        scratch_shapes=[
            pltpu.VMEM((2 * depth // 3, 4 * cells), jnp.bfloat16),
            pltpu.VMEM(w_rows.shape, jnp.bfloat16),
            pltpu.VMEM((2, channels, 16, cells), jnp.bfloat16),
            pltpu.VMEM((2, 16 * channels, cells), jnp.bfloat16),
            pltpu.SemaphoreType.DMA((3,)),
        ],
        compiler_params=GRANT,
        cost_estimate=pl.CostEstimate(
            flops=8 * outs * depth * cells, bytes_accessed=4 * depth * cells, transcendentals=0
        ),
    )(w_rows, volume)


def regrouped(values, own, at):
    outs = values.shape[0]
    starts = range(at * own, outs, outs // ROWS)
    return jnp.concatenate([values[start : start + own] for start in starts], 0)


def pointwise_kernel(rule, part_ref, behind_ref, result_ref):
    groups, rows, _ = result_ref.shape
    unit = rows // 4
    for phase in range(4):
        values = rule(part_ref[phase] + behind_ref[phase].astype(jnp.float32))
        for at in range(groups):
            block = regrouped(values, unit // ROWS, at)
            result_ref[at, phase * unit : (phase + 1) * unit, :] = block.astype(result_ref.dtype)


def pointwise(rule, part, behind, groups, dtype):
    phases, outs, cells = part.shape
    return pl.pallas_call(
        functools.partial(pointwise_kernel, rule),
        out_shape=jax.ShapeDtypeStruct((groups, phases * outs // groups, cells), dtype),
        in_specs=[IN_VMEM] * 2,
        out_specs=IN_VMEM,
        compiler_params=GRANT,
        cost_estimate=pl.CostEstimate(
            flops=10 * part.size, bytes_accessed=8 * part.size, transcendentals=part.size
        ),
    )(part, behind)


def pile_kernel(*refs):
    blocks, out_ref, sems = refs[:-2], refs[-2], refs[-1]
    copies = [
        pltpu.make_async_copy(block, out_ref.at[at], sems.at[at]) for at, block in enumerate(blocks)
    ]
    for copy in copies:
        copy.start()
    for copy in copies:
        copy.wait()


def pile(blocks):
    shape = (len(blocks),) + blocks[0].shape
    return pl.pallas_call(
        pile_kernel,
        out_shape=jax.ShapeDtypeStruct(shape, blocks[0].dtype),
        in_specs=[IN_HBM] * len(blocks),
        out_specs=IN_VMEM,
        scratch_shapes=[pltpu.SemaphoreType.DMA((len(blocks),))],
        compiler_params=GRANT,
        cost_estimate=pl.CostEstimate(
            flops=0, bytes_accessed=4 * len(blocks) * blocks[0].size, transcendentals=0
        ),
    )(*blocks)


def spread(block, row_len):
    return jnp.concatenate(
        [block]
        + [shifted(block, by_row, by_col, row_len) for by_row, by_col in ((0, 1), (1, 0), (1, 1))],
        0,
    )


def gather_back(terms, row_len):
    rows = terms.shape[0] // 4
    lane = lax.broadcasted_iota(jnp.int32, (rows, terms.shape[1]), 1)
    cells = terms.shape[1]
    total = terms[:rows]
    for at, (by_row, by_col) in ((1, (0, 1)), (2, (1, 0)), (3, (1, 1))):
        moved = pltpu.roll(terms[at * rows : (at + 1) * rows], cells - by_row * row_len - by_col, 1)
        keep = lane < cells - row_len if by_row else None
        if by_col:
            inner = lane % row_len != row_len - 1
            keep = inner if keep is None else jnp.logical_and(keep, inner)
        total = total + jnp.where(keep, moved, 0.0)
    return total


def cot_copies(place_ref, mine, theirs_ref, cot_ref, sems):
    ring = len(mine)
    half = cot_ref.shape[3] // 2
    z, core = place_ref[1], place_ref[2]
    here = pl.ds(pl.multiple_of(core * half, 128), half)
    there = pl.ds(pl.multiple_of((1 - core) * half, 128), half)
    copies = []
    for k in range(ring):
        to = lax.rem(z + k, ring)
        for side, (source, part) in enumerate(((mine[k], here), (theirs_ref.at[k], there))):
            copies.append(
                pltpu.make_async_copy(source, cot_ref.at[:, to, :, part], sems.at[2 * k + side])
            )
    return copies


def grad_kernel(row_len, place_ref, hidden_ref, *refs):
    mine, theirs_ref, refs = refs[:RING], refs[RING], refs[RING + 1 :]
    outs_refs, (cot_ref, sems, even_ref, odd_ref, sum_ref) = refs[:-5], refs[-5:]
    copies = cot_copies(place_ref, mine, theirs_ref, cot_ref, sems)
    for copy in copies:
        copy.start()
    planes, group, cells = hidden_ref.shape
    steps = planes // 2
    own = group // 4
    unit = own // len(outs_refs)
    for s in range(steps):
        here = slice(s * cells, (s + 1) * cells)
        even_ref[:, here] = spread(hidden_ref[2 * s], row_len)
        odd_ref[:, here] = spread(hidden_ref[2 * s + 1], row_len)
    for copy in copies:
        copy.wait()
    over_cells = (((1,), (1,)), ((), ()))
    sources = ((odd_ref, cells), (even_ref, 0), (odd_ref, 0))
    for depth_tap, (rows_ref, start) in enumerate(sources):
        total = lax.dot_general(
            rows_ref[...],
            cot_ref[:, :, :, start : start + steps * cells].reshape(-1, steps * cells),
            over_cells,
            preferred_element_type=jnp.float32,
        )
        for row_tap in range(3):
            for col_tap in range(3):
                at = (2 * int(row_tap == 0) + int(col_tap == 0)) * group
                at += (2 * int(row_tap != 1) + int(col_tap != 1)) * own
                put = ((depth_tap * 3 + row_tap) * 3 + col_tap) * unit
                for y in range(len(outs_refs)):
                    first = at + y * unit
                    sum_ref[y, put : put + unit, :] = total[first : first + unit, :]
    for away, out_ref in enumerate(outs_refs):
        y = lax.rem(place_ref[0] + away, len(outs_refs))
        out_ref[...] = sum_ref[y].astype(out_ref.dtype)


def grad(place, hidden, mine, theirs, row_len):
    planes, group, cells = hidden.shape
    cot_shape = mine[0].shape[:1] + (RING,) + mine[0].shape[1:2] + (2 * mine[0].shape[2],)
    outs = cot_shape[0] * cot_shape[1] * cot_shape[2]
    rows = pltpu.VMEM((4 * group, planes // 2 * cells), jnp.bfloat16)
    size = 27 * group // (4 * ROWS)
    return pl.pallas_call(
        functools.partial(grad_kernel, row_len),
        out_shape=[
            jax.ShapeDtypeStruct((size, outs), jnp.bfloat16 if away else jnp.float32)
            for away in range(ROWS)
        ],
        in_specs=[pl.BlockSpec(memory_space=pltpu.SMEM), IN_VMEM] + [IN_HBM] * (RING + 1),
        out_specs=[IN_VMEM] * ROWS,
        scratch_shapes=[
            pltpu.VMEM(cot_shape, jnp.bfloat16),
            pltpu.SemaphoreType.DMA((2 * RING,)),
            rows,
            rows,
            pltpu.VMEM((ROWS, size, outs), jnp.float32),
        ],
        compiler_params=GRANT,
        cost_estimate=pl.CostEstimate(
            flops=12 * group * outs * planes * cells, bytes_accessed=2**22, transcendentals=0
        ),
    )(place, hidden, *mine, theirs)


def moves_kernel(place_ref, *refs):
    w_refs, (moves_ref, rows_ref) = refs[:-2], refs[-2:]
    for away, w_ref in enumerate(w_refs):
        rows_ref[lax.rem(place_ref[0] + away, ROWS)] = w_ref[...].astype(jnp.float32)
    own = w_refs[0].shape[0] // 27
    block = ROWS * own
    group = 4 * block
    moves_ref[...] = jnp.zeros_like(moves_ref)
    for tap in range(27):
        depth_tap, row_tap, col_tap = tap // 9, tap // 3 % 3, tap % 3
        at = (4 * depth_tap + 2 * int(row_tap == 0) + int(col_tap == 0)) * group
        at += (2 * int(row_tap != 1) + int(col_tap != 1)) * block
        pieces = [rows_ref[row, tap * own : (tap + 1) * own, :] for row in range(ROWS)]
        moves_ref[at : at + block, :] = jnp.concatenate(pieces, 0).astype(moves_ref.dtype)


def moves_of(place, w_rel):
    size, outs = w_rel[0].shape
    return pl.pallas_call(
        moves_kernel,
        out_shape=jax.ShapeDtypeStruct((48 * ROWS * size // 27, outs), jnp.bfloat16),
        in_specs=[pl.BlockSpec(memory_space=pltpu.SMEM)] + [IN_VMEM] * ROWS,
        out_specs=IN_VMEM,
        scratch_shapes=[pltpu.VMEM((ROWS, size, outs), jnp.float32)],
        compiler_params=GRANT,
        cost_estimate=pl.CostEstimate(flops=0, bytes_accessed=2**20, transcendentals=0),
    )(place, *w_rel)


def back_kernel(row_len, place_ref, moves_ref, *refs):
    mine, theirs_ref, (out_ref, cot_ref, sems) = refs[:RING], refs[RING], refs[RING + 1 :]
    planes, group, cells = out_ref.shape
    size = 4 * group
    copies = cot_copies(place_ref, mine, theirs_ref, cot_ref, sems)
    for copy in copies:
        copy.start()
    for copy in copies:
        copy.wait()

    def one(at, start):
        return jnp.dot(
            moves_ref[at * size : (at + 1) * size, :],
            cot_ref[:, :, :, start : start + cells].reshape(-1, cells),
            preferred_element_type=jnp.float32,
        )

    for s in range(planes // 2):
        start = s * cells
        out_ref[2 * s] = gather_back(one(1, start), row_len).astype(out_ref.dtype)
        odd = one(2, start) + one(0, start + cells)
        out_ref[2 * s + 1] = gather_back(odd, row_len).astype(out_ref.dtype)


def back(place, moves, mine, theirs, planes, row_len):
    rows, outs = moves.shape
    group = rows // 12
    cot_shape = mine[0].shape[:1] + (RING,) + mine[0].shape[1:2] + (2 * mine[0].shape[2],)
    cells = cot_shape[3] // (planes // 2 + 1)
    return pl.pallas_call(
        functools.partial(back_kernel, row_len),
        out_shape=jax.ShapeDtypeStruct((planes, group, cells), jnp.bfloat16),
        in_specs=[pl.BlockSpec(memory_space=pltpu.SMEM), IN_VMEM] + [IN_HBM] * (RING + 1),
        out_specs=IN_VMEM,
        scratch_shapes=[
            pltpu.VMEM(cot_shape, jnp.bfloat16),
            pltpu.SemaphoreType.DMA((2 * RING,)),
        ],
        compiler_params=GRANT,
        cost_estimate=pl.CostEstimate(
            flops=12 * group * outs * planes * cells, bytes_accessed=2**22, transcendentals=0
        ),
    )(place, moves, *mine, theirs)


def parts_kernel(cot_ref, out_ref):
    channels, depth, cells = cot_ref.shape
    share = depth // ROWS
    half = out_ref.shape[2]
    turned = jnp.swapaxes(cot_ref[...].astype(jnp.float32), 0, 1)
    for row in range(ROWS):
        for at in range(share + 1):
            s = row * share + at
            for lane in range(0, cells, 128):
                put = at * cells + lane
                if s < depth:
                    block = turned[s, :, lane : lane + 128].astype(out_ref.dtype)
                else:
                    block = jnp.zeros((channels, 128), out_ref.dtype)
                out_ref[row * CORES + put // half, :, put % half : put % half + 128] = block


def parts_of(cot):
    channels, depth, cells = cot.shape
    half = (depth // ROWS + 1) * cells // CORES
    return pl.pallas_call(
        parts_kernel,
        out_shape=jax.ShapeDtypeStruct((ROWS * CORES, channels, half), cot.dtype),
        in_specs=[IN_VMEM],
        out_specs=IN_VMEM,
        compiler_params=GRANT,
        cost_estimate=pl.CostEstimate(flops=0, bytes_accessed=4 * cot.size, transcendentals=0),
    )(cot)


def total_kernel(own_ref, left_ref, opposite_ref, right_ref, out_ref):
    f32 = jnp.float32
    across = own_ref[...].astype(f32) + opposite_ref[...].astype(f32)
    total = across + (left_ref[...].astype(f32) + right_ref[...].astype(f32))
    taps, own, _ = out_ref.shape
    for tap in range(taps):
        out_ref[tap] = total[tap * own : (tap + 1) * own, :]


def total_of(own, left, opposite, right):
    rows, outs = own.shape
    return pl.pallas_call(
        total_kernel,
        out_shape=jax.ShapeDtypeStruct((27, rows // 27, outs), jnp.float32),
        in_specs=[IN_VMEM] * 4,
        out_specs=IN_VMEM,
        compiler_params=GRANT,
        cost_estimate=pl.CostEstimate(
            flops=3 * own.size, bytes_accessed=12 * own.size, transcendentals=0
        ),
    )(own, left, opposite, right)


def on_space(block, y_by=0, z_by=0, core_by=0):
    route = []
    for y in range(ROWS):
        for z in range(RING):
            for core in range(CORES):
                to = ((y + y_by) % ROWS, (z + z_by) % RING, (core + core_by) % CORES)
                route.append(((y * RING + z) * CORES + core, (to[0] * RING + to[1]) * CORES + to[2]))
    return lax.ppermute(block, "space", route)


CHIPS = [(y, z) for y in range(ROWS) for z in range(RING)]


def members(pick):
    groups = {}
    for y, z in CHIPS:
        for core in range(CORES):
            groups.setdefault(pick(y, z, core), []).append((y * RING + z) * CORES + core)
    return list(groups.values())


COLUMNS = members(lambda y, z, core: (z, core))
PILLARS = members(lambda y, z, core: z)
SLABS = members(lambda y, z, core: y)


def exchange(blocks, groups):
    return lax.all_to_all(
        blocks, "space", split_axis=0, concat_axis=0, axis_index_groups=groups, tiled=True
    )


def section(volume, w_first, w_second, cotangent):
    channels = volume.shape[1]
    cells = volume.shape[4]
    outs = w_first.shape[4]
    own = w_second.shape[3]
    row_len = WID // 4
    me = lax.axis_index("space")
    y, z, core = me // (RING * CORES), me // CORES % RING, me % CORES
    place = jnp.stack([y, z, core]).astype(jnp.int32)
    group = RING * CORES

    parts = parts_of(cotangent[0])
    first = exchange(parts, PILLARS)
    first = first.reshape(ROWS, -1, first.shape[2])
    hops = {0: first}
    for step in (1, -1, 2, -2):
        hops[step] = on_space(first, z_by=-step)
    for step, come in ((3, 2), (-3, -2), (4, 2)):
        hops[step] = on_space(hops[come], z_by=come - step)
    mine = [hops[step] for step in (0, 1, 2, 3, 4, -3, -2, -1)]
    piled = pile(mine)
    theirs = on_space(piled, core_by=1)

    w_rel = [w_second.reshape(27 * own, C3)]
    for step in range(1, ROWS):
        w_rel.append(on_space(w_rel[0], y_by=-step))

    w_rows = w_first.reshape(27 * channels, outs)
    ahead, part = conv(w_rows, volume[0].reshape(channels, 32, cells), row_len)
    behind = from_behind(ahead, "space", 1)
    hidden = pointwise(activate, part, behind, group, jnp.bfloat16)
    slopes = pointwise(slope_of, part, behind, group, jnp.float32)
    by_plane = exchange(hidden, SLABS)

    moves = moves_of(place, w_rel)
    back_terms = back(place, moves, mine, theirs, group, row_len)
    hidden_grad = exchange(back_terms, SLABS)

    partial, *others = grad(place, by_plane, mine, theirs, row_len)
    for step, block in enumerate(others, 1):
        partial = partial + on_space(block, y_by=step).astype(jnp.float32)
    partial = partial.astype(jnp.bfloat16)
    sides = []
    for distance in (1, 2, 3):
        sides.append(from_side(partial, "dp", distance))
    grad_second = total_of(partial, *sides)
    grad_second = grad_second.reshape(3, 3, 3, own, C3)

    pre_grad = (hidden_grad.astype(jnp.float32) * slopes).astype(jnp.bfloat16)
    pre_grad = pre_grad.reshape(group, 4, ROWS, own, cells).transpose(2, 0, 3, 1, 4)
    pre_grad = pre_grad.reshape(1, outs, 1, 4, cells)
    return (grad_second, pre_grad)


def solution(mesh):
    in_specs = (
        P("dp", None, "space", None, None),
        P(),
        P(None, None, None, "space", None),
        P("dp", "space", None, None),
    )
    out_specs = (P(None, None, None, "space", None), P("dp", None, "space", None, None))
    return jax.shard_map(
        section, mesh=mesh, in_specs=in_specs, out_specs=out_specs, check_vma=False
    )
```

```python
import functools

import jax
import jax.numpy as jnp
from jax import lax
from jax.experimental import pallas as pl
from jax.experimental.pallas import tpu as pltpu
from jax.sharding import PartitionSpec as P


C3 = 512
WID = 128


leak_slope = 0.3


def from_behind(block, axis, distance):
    devices = range(lax.axis_size(axis))
    route = [(i - distance, i) for i in devices if i - distance in devices]
    return lax.ppermute(block, axis, route)


def from_side(block, axis, distance):
    size = lax.axis_size(axis)
    return lax.ppermute(block, axis, [(i, (i + distance) % size) for i in range(size)])


def activate(values):
    return leak_slope * values + (1.0 - leak_slope) * values * jax.nn.sigmoid(values)


def slope_of(values):
    sigmoid_value = jax.nn.sigmoid(values)
    return leak_slope + (1.0 - leak_slope) * (
        sigmoid_value + values * sigmoid_value * (1.0 - sigmoid_value)
    )


ROWS, RING, CORES = 4, 8, 2
IN_VMEM = pl.BlockSpec(memory_space=pltpu.VMEM)
IN_HBM = pl.BlockSpec(memory_space=pltpu.HBM)
WIDE = pltpu.CompilerParams(vmem_limit_bytes=64900000)
GRANT = pltpu.CompilerParams(vmem_limit_bytes=16 * 2**20)


def shifted(block, by_row, by_col, row_len):
    moved = block.astype(jnp.float32)
    lane = lax.broadcasted_iota(jnp.int32, moved.shape, 1)
    moved = pltpu.roll(moved, by_row * row_len + by_col, 1)
    keep = None
    if by_row:
        keep = lane >= row_len
    if by_col:
        inner = lane % row_len != 0
        keep = inner if keep is None else jnp.logical_and(keep, inner)
    return jnp.where(keep, moved, 0.0).astype(block.dtype)


def conv_kernel(row_len, w_from, volume_from, ahead_ref, part_ref, *scratch):
    cols_ref, w_ref, volume_ref, planes_ref, sems = scratch
    moves = [
        pltpu.make_async_copy(volume_from.at[:, at * 16 : at * 16 + 16], volume_ref.at[at], sems.at[at])
        for at in range(2)
    ]
    copy = pltpu.make_async_copy(w_from, w_ref, sems.at[2])
    for move in moves:
        move.start()
    copy.start()
    for at in range(2):
        moves[at].wait()
        for first in range(0, volume_ref.shape[1], 16):
            turned = jnp.swapaxes(volume_ref[at, first : first + 16], 0, 1)
            for phase in range(16):
                row = phase * volume_ref.shape[1] + first
                planes_ref[at, row : row + 16, :] = turned[phase]
    cells = planes_ref.shape[2]
    channels = planes_ref.shape[1] // 16
    tap_rows = 9 * channels
    for plane in range(2):
        for row in range(-1, 4):
            for col in range(-1, 4):
                source = ((row % 4) * 4 + col % 4) * channels
                block = planes_ref[plane, source : source + channels, :]
                if row < 0 or col < 0:
                    block = shifted(block, int(row < 0), int(col < 0), row_len)
                for row_phase in range(2):
                    row_tap = row + 1 - 2 * row_phase
                    if not 0 <= row_tap <= 2:
                        continue
                    for col_phase in range(2):
                        col_tap = col + 1 - 2 * col_phase
                        if not 0 <= col_tap <= 2:
                            continue
                        start = plane * tap_rows + (row_tap * 3 + col_tap) * channels
                        phase = row_phase * 2 + col_phase
                        put = slice(phase * cells, (phase + 1) * cells)
                        cols_ref[start : start + channels, put] = block
    copy.wait()
    over_rows = (((0,), (0,)), ((), ()))
    for out_ref, weights, cols in (
        (ahead_ref, w_ref[:tap_rows, :], cols_ref[tap_rows:, :]),
        (part_ref, w_ref[tap_rows:, :], cols_ref[...]),
    ):
        total = lax.dot_general(weights, cols, over_rows, preferred_element_type=jnp.float32)
        for phase in range(4):
            out_ref[phase] = total[:, phase * cells : (phase + 1) * cells].astype(out_ref.dtype)


def conv(w_rows, volume, row_len):
    depth, outs = w_rows.shape
    channels, _, cells = volume.shape
    return pl.pallas_call(
        functools.partial(conv_kernel, row_len),
        out_shape=(
            jax.ShapeDtypeStruct((4, outs, cells), jnp.bfloat16),
            jax.ShapeDtypeStruct((4, outs, cells), jnp.float32),
        ),
        in_specs=[IN_HBM] * 2,
        out_specs=(IN_VMEM,) * 2,
        scratch_shapes=[
            pltpu.VMEM((2 * depth // 3, 4 * cells), jnp.bfloat16),
            pltpu.VMEM(w_rows.shape, jnp.bfloat16),
            pltpu.VMEM((2, channels, 16, cells), jnp.bfloat16),
            pltpu.VMEM((2, 16 * channels, cells), jnp.bfloat16),
            pltpu.SemaphoreType.DMA((3,)),
        ],
        compiler_params=WIDE,
        cost_estimate=pl.CostEstimate(
            flops=8 * outs * depth * cells, bytes_accessed=4 * depth * cells, transcendentals=0
        ),
    )(w_rows, volume)


def regrouped(values, own, at):
    outs = values.shape[0]
    starts = range(at * own, outs, outs // ROWS)
    return jnp.concatenate([values[start : start + own] for start in starts], 0)


def pointwise_kernel(rule, part_from, behind_ref, result_ref, part_ref, sems):
    groups, rows, _ = result_ref.shape
    unit = rows // 4
    copies = [
        pltpu.make_async_copy(part_from.at[phase], part_ref.at[phase], sems.at[phase])
        for phase in range(4)
    ]
    for copy in copies:
        copy.start()
    for phase in range(4):
        copies[phase].wait()
        values = rule(part_ref[phase] + behind_ref[phase].astype(jnp.float32))
        for at in range(groups):
            block = regrouped(values, unit // ROWS, at)
            result_ref[at, phase * unit : (phase + 1) * unit, :] = block.astype(result_ref.dtype)


def pointwise(rule, part, behind, groups, dtype):
    phases, outs, cells = part.shape
    return pl.pallas_call(
        functools.partial(pointwise_kernel, rule),
        out_shape=jax.ShapeDtypeStruct((groups, phases * outs // groups, cells), dtype),
        in_specs=[IN_HBM, IN_VMEM],
        out_specs=IN_VMEM,
        scratch_shapes=[pltpu.VMEM(part.shape, part.dtype), pltpu.SemaphoreType.DMA((4,))],
        compiler_params=pltpu.CompilerParams(vmem_limit_bytes=65_800_000),
        cost_estimate=pl.CostEstimate(
            flops=10 * part.size, bytes_accessed=8 * part.size, transcendentals=part.size
        ),
    )(part, behind)


def pile_kernel(*refs):
    blocks, out_ref, sems = refs[:-2], refs[-2], refs[-1]
    copies = [
        pltpu.make_async_copy(block, out_ref.at[at], sems.at[at]) for at, block in enumerate(blocks)
    ]
    for copy in copies:
        copy.start()
    for copy in copies:
        copy.wait()


def pile(blocks):
    shape = (len(blocks),) + blocks[0].shape
    return pl.pallas_call(
        pile_kernel,
        out_shape=jax.ShapeDtypeStruct(shape, blocks[0].dtype),
        in_specs=[IN_HBM] * len(blocks),
        out_specs=IN_VMEM,
        scratch_shapes=[pltpu.SemaphoreType.DMA((len(blocks),))],
        compiler_params=GRANT,
        cost_estimate=pl.CostEstimate(
            flops=0, bytes_accessed=4 * len(blocks) * blocks[0].size, transcendentals=0
        ),
    )(*blocks)


def spread(block, row_len):
    return jnp.concatenate(
        [block]
        + [shifted(block, by_row, by_col, row_len) for by_row, by_col in ((0, 1), (1, 0), (1, 1))],
        0,
    )


def gather_back(terms, row_len):
    rows = terms.shape[0] // 4
    lane = lax.broadcasted_iota(jnp.int32, (rows, terms.shape[1]), 1)
    cells = terms.shape[1]
    total = terms[:rows]
    for at, (by_row, by_col) in ((1, (0, 1)), (2, (1, 0)), (3, (1, 1))):
        moved = pltpu.roll(terms[at * rows : (at + 1) * rows], cells - by_row * row_len - by_col, 1)
        keep = lane < cells - row_len if by_row else None
        if by_col:
            inner = lane % row_len != row_len - 1
            keep = inner if keep is None else jnp.logical_and(keep, inner)
        total = total + jnp.where(keep, moved, 0.0)
    return total


def cot_copies(place_ref, mine, theirs_ref, cot_ref, sems):
    ring = len(mine)
    half = cot_ref.shape[3] // 2
    z, core = place_ref[1], place_ref[2]
    here = pl.ds(pl.multiple_of(core * half, 128), half)
    there = pl.ds(pl.multiple_of((1 - core) * half, 128), half)
    copies = []
    for k in range(ring):
        to = lax.rem(z + k, ring)
        for side, (source, part) in enumerate(((mine[k], here), (theirs_ref.at[k], there))):
            copies.append(
                pltpu.make_async_copy(source, cot_ref.at[:, to, :, part], sems.at[2 * k + side])
            )
    return copies


def grad_kernel(row_len, place_ref, hidden_ref, *refs):
    mine, theirs_ref, refs = refs[:RING], refs[RING], refs[RING + 1 :]
    outs_refs, (cot_ref, sems, even_ref, odd_ref, sum_ref) = refs[:-5], refs[-5:]
    copies = cot_copies(place_ref, mine, theirs_ref, cot_ref, sems)
    for copy in copies:
        copy.start()
    planes, group, cells = hidden_ref.shape
    steps = planes // 2
    own = group // 4
    unit = own // len(outs_refs)
    for s in range(steps):
        here = slice(s * cells, (s + 1) * cells)
        even_ref[:, here] = spread(hidden_ref[2 * s], row_len)
        odd_ref[:, here] = spread(hidden_ref[2 * s + 1], row_len)
    for copy in copies:
        copy.wait()
    over_cells = (((1,), (1,)), ((), ()))
    sources = ((odd_ref, cells), (even_ref, 0), (odd_ref, 0))
    for depth_tap, (rows_ref, start) in enumerate(sources):
        total = lax.dot_general(
            rows_ref[...],
            cot_ref[:, :, :, start : start + steps * cells].reshape(-1, steps * cells),
            over_cells,
            preferred_element_type=jnp.float32,
        )
        for row_tap in range(3):
            for col_tap in range(3):
                at = (2 * int(row_tap == 0) + int(col_tap == 0)) * group
                at += (2 * int(row_tap != 1) + int(col_tap != 1)) * own
                put = ((depth_tap * 3 + row_tap) * 3 + col_tap) * unit
                for y in range(len(outs_refs)):
                    first = at + y * unit
                    sum_ref[y, put : put + unit, :] = total[first : first + unit, :]
    for away, out_ref in enumerate(outs_refs):
        y = lax.rem(place_ref[0] + away, len(outs_refs))
        out_ref[...] = sum_ref[y].astype(out_ref.dtype)


def grad(place, hidden, mine, theirs, row_len):
    planes, group, cells = hidden.shape
    cot_shape = mine[0].shape[:1] + (RING,) + mine[0].shape[1:2] + (2 * mine[0].shape[2],)
    outs = cot_shape[0] * cot_shape[1] * cot_shape[2]
    rows = pltpu.VMEM((4 * group, planes // 2 * cells), jnp.bfloat16)
    size = 27 * group // (4 * ROWS)
    return pl.pallas_call(
        functools.partial(grad_kernel, row_len),
        out_shape=[
            jax.ShapeDtypeStruct((size, outs), jnp.bfloat16 if away else jnp.float32)
            for away in range(ROWS)
        ],
        in_specs=[pl.BlockSpec(memory_space=pltpu.SMEM), IN_VMEM] + [IN_HBM] * (RING + 1),
        out_specs=[IN_VMEM] * ROWS,
        scratch_shapes=[
            pltpu.VMEM(cot_shape, jnp.bfloat16),
            pltpu.SemaphoreType.DMA((2 * RING,)),
            rows,
            rows,
            pltpu.VMEM((ROWS, size, outs), jnp.float32),
        ],
        compiler_params=GRANT,
        cost_estimate=pl.CostEstimate(
            flops=12 * group * outs * planes * cells, bytes_accessed=2**22, transcendentals=0
        ),
    )(place, hidden, *mine, theirs)


def moves_kernel(place_ref, *refs):
    w_refs, (moves_ref, rows_ref) = refs[:-2], refs[-2:]
    for away, w_ref in enumerate(w_refs):
        rows_ref[lax.rem(place_ref[0] + away, ROWS)] = w_ref[...].astype(jnp.float32)
    own = w_refs[0].shape[0] // 27
    block = ROWS * own
    group = 4 * block
    moves_ref[...] = jnp.zeros_like(moves_ref)
    for tap in range(27):
        depth_tap, row_tap, col_tap = tap // 9, tap // 3 % 3, tap % 3
        at = (4 * depth_tap + 2 * int(row_tap == 0) + int(col_tap == 0)) * group
        at += (2 * int(row_tap != 1) + int(col_tap != 1)) * block
        pieces = [rows_ref[row, tap * own : (tap + 1) * own, :] for row in range(ROWS)]
        moves_ref[at : at + block, :] = jnp.concatenate(pieces, 0).astype(moves_ref.dtype)


def moves_of(place, w_rel):
    size, outs = w_rel[0].shape
    return pl.pallas_call(
        moves_kernel,
        out_shape=jax.ShapeDtypeStruct((48 * ROWS * size // 27, outs), jnp.bfloat16),
        in_specs=[pl.BlockSpec(memory_space=pltpu.SMEM)] + [IN_VMEM] * ROWS,
        out_specs=IN_VMEM,
        scratch_shapes=[pltpu.VMEM((ROWS, size, outs), jnp.float32)],
        compiler_params=GRANT,
        cost_estimate=pl.CostEstimate(flops=0, bytes_accessed=2**20, transcendentals=0),
    )(place, *w_rel)


def back_kernel(row_len, place_ref, moves_ref, *refs):
    mine, theirs_ref, (out_ref, cot_ref, sems) = refs[:RING], refs[RING], refs[RING + 1 :]
    planes, group, cells = out_ref.shape
    size = 4 * group
    copies = cot_copies(place_ref, mine, theirs_ref, cot_ref, sems)
    for copy in copies:
        copy.start()
    for copy in copies:
        copy.wait()

    def one(at, start):
        return jnp.dot(
            moves_ref[at * size : (at + 1) * size, :],
            cot_ref[:, :, :, start : start + cells].reshape(-1, cells),
            preferred_element_type=jnp.float32,
        )

    for s in range(planes // 2):
        start = s * cells
        out_ref[2 * s] = gather_back(one(1, start), row_len).astype(out_ref.dtype)
        odd = one(2, start) + one(0, start + cells)
        out_ref[2 * s + 1] = gather_back(odd, row_len).astype(out_ref.dtype)


def back(place, moves, mine, theirs, planes, row_len):
    rows, outs = moves.shape
    group = rows // 12
    cot_shape = mine[0].shape[:1] + (RING,) + mine[0].shape[1:2] + (2 * mine[0].shape[2],)
    cells = cot_shape[3] // (planes // 2 + 1)
    return pl.pallas_call(
        functools.partial(back_kernel, row_len),
        out_shape=jax.ShapeDtypeStruct((planes, group, cells), jnp.bfloat16),
        in_specs=[pl.BlockSpec(memory_space=pltpu.SMEM), IN_VMEM] + [IN_HBM] * (RING + 1),
        out_specs=IN_VMEM,
        scratch_shapes=[
            pltpu.VMEM(cot_shape, jnp.bfloat16),
            pltpu.SemaphoreType.DMA((2 * RING,)),
        ],
        compiler_params=GRANT,
        cost_estimate=pl.CostEstimate(
            flops=12 * group * outs * planes * cells, bytes_accessed=2**22, transcendentals=0
        ),
    )(place, moves, *mine, theirs)


def parts_kernel(cot_ref, out_ref):
    channels, depth, cells = cot_ref.shape
    share = depth // ROWS
    half = out_ref.shape[2]
    turned = jnp.swapaxes(cot_ref[...].astype(jnp.float32), 0, 1)
    for row in range(ROWS):
        for at in range(share + 1):
            s = row * share + at
            for lane in range(0, cells, 128):
                put = at * cells + lane
                if s < depth:
                    block = turned[s, :, lane : lane + 128].astype(out_ref.dtype)
                else:
                    block = jnp.zeros((channels, 128), out_ref.dtype)
                out_ref[row * CORES + put // half, :, put % half : put % half + 128] = block


def parts_of(cot):
    channels, depth, cells = cot.shape
    half = (depth // ROWS + 1) * cells // CORES
    return pl.pallas_call(
        parts_kernel,
        out_shape=jax.ShapeDtypeStruct((ROWS * CORES, channels, half), cot.dtype),
        in_specs=[IN_VMEM],
        out_specs=IN_VMEM,
        compiler_params=GRANT,
        cost_estimate=pl.CostEstimate(flops=0, bytes_accessed=4 * cot.size, transcendentals=0),
    )(cot)


def total_kernel(own_ref, left_ref, opposite_ref, right_ref, out_ref):
    f32 = jnp.float32
    across = own_ref[...].astype(f32) + opposite_ref[...].astype(f32)
    total = across + (left_ref[...].astype(f32) + right_ref[...].astype(f32))
    taps, own, _ = out_ref.shape
    for tap in range(taps):
        out_ref[tap] = total[tap * own : (tap + 1) * own, :]


def total_of(own, left, opposite, right):
    rows, outs = own.shape
    return pl.pallas_call(
        total_kernel,
        out_shape=jax.ShapeDtypeStruct((27, rows // 27, outs), jnp.float32),
        in_specs=[IN_VMEM] * 4,
        out_specs=IN_VMEM,
        compiler_params=GRANT,
        cost_estimate=pl.CostEstimate(
            flops=3 * own.size, bytes_accessed=12 * own.size, transcendentals=0
        ),
    )(own, left, opposite, right)


def on_space(block, y_by=0, z_by=0, core_by=0):
    route = []
    for y in range(ROWS):
        for z in range(RING):
            for core in range(CORES):
                to = ((y + y_by) % ROWS, (z + z_by) % RING, (core + core_by) % CORES)
                route.append(((y * RING + z) * CORES + core, (to[0] * RING + to[1]) * CORES + to[2]))
    return lax.ppermute(block, "space", route)


CHIPS = [(y, z) for y in range(ROWS) for z in range(RING)]


def members(pick):
    groups = {}
    for y, z in CHIPS:
        for core in range(CORES):
            groups.setdefault(pick(y, z, core), []).append((y * RING + z) * CORES + core)
    return list(groups.values())


COLUMNS = members(lambda y, z, core: (z, core))
PILLARS = members(lambda y, z, core: z)
SLABS = members(lambda y, z, core: y)


def exchange(blocks, groups):
    return lax.all_to_all(
        blocks, "space", split_axis=0, concat_axis=0, axis_index_groups=groups, tiled=True
    )


def section(volume, w_first, w_second, cotangent):
    channels = volume.shape[1]
    cells = volume.shape[4]
    outs = w_first.shape[4]
    own = w_second.shape[3]
    row_len = WID // 4
    me = lax.axis_index("space")
    y, z, core = me // (RING * CORES), me // CORES % RING, me % CORES
    place = jnp.stack([y, z, core]).astype(jnp.int32)
    group = RING * CORES

    parts = parts_of(cotangent[0])
    first = exchange(parts, PILLARS)
    first = first.reshape(ROWS, -1, first.shape[2])
    hops = {0: first}
    for step in (1, -1, 2, -2):
        hops[step] = on_space(first, z_by=-step)
    for step, come in ((3, 2), (-3, -2), (4, 2)):
        hops[step] = on_space(hops[come], z_by=come - step)
    mine = [hops[step] for step in (0, 1, 2, 3, 4, -3, -2, -1)]
    piled = pile(mine)
    theirs = on_space(piled, core_by=1)

    w_rel = [w_second.reshape(27 * own, C3)]
    for step in range(1, ROWS):
        w_rel.append(on_space(w_rel[0], y_by=-step))

    w_rows = w_first.reshape(27 * channels, outs)
    ahead, part = conv(w_rows, volume[0].reshape(channels, 32, cells), row_len)
    behind = from_behind(ahead, "space", 1)
    hidden = pointwise(activate, part, behind, group, jnp.bfloat16)
    slopes = pointwise(slope_of, part, behind, group, jnp.float32)
    by_plane = exchange(hidden, SLABS)

    moves = moves_of(place, w_rel)
    back_terms = back(place, moves, mine, theirs, group, row_len)
    hidden_grad = exchange(back_terms, SLABS)

    partial, *others = grad(place, by_plane, mine, theirs, row_len)
    for step, block in enumerate(others, 1):
        partial = partial + on_space(block, y_by=step).astype(jnp.float32)
    partial = partial.astype(jnp.bfloat16)
    sides = []
    for distance in (1, 2, 3):
        sides.append(from_side(partial, "dp", distance))
    grad_second = total_of(partial, *sides)
    grad_second = grad_second.reshape(3, 3, 3, own, C3)

    pre_grad = (hidden_grad.astype(jnp.float32) * slopes).astype(jnp.bfloat16)
    pre_grad = pre_grad.reshape(group, 4, ROWS, own, cells).transpose(2, 0, 3, 1, 4)
    pre_grad = pre_grad.reshape(1, outs, 1, 4, cells)
    return (grad_second, pre_grad)


def solution(mesh):
    in_specs = (
        P("dp", None, "space", None, None),
        P(),
        P(None, None, None, "space", None),
        P("dp", "space", None, None),
    )
    out_specs = (P(None, None, None, "space", None), P("dp", None, "space", None, None))
    return jax.shard_map(
        section, mesh=mesh, in_specs=in_specs, out_specs=out_specs, check_vma=False
    )
```

```python
import functools

import jax
import jax.numpy as jnp
from jax import lax
from jax.experimental import pallas as pl
from jax.experimental.pallas import tpu as pltpu
from jax.sharding import PartitionSpec as P


C3 = 512
WID = 128


leak_slope = 0.3


def from_behind(block, axis, distance):
    devices = range(lax.axis_size(axis))
    route = [(i - distance, i) for i in devices if i - distance in devices]
    return lax.ppermute(block, axis, route)


def from_side(block, axis, distance):
    size = lax.axis_size(axis)
    return lax.ppermute(block, axis, [(i, (i + distance) % size) for i in range(size)])


def activate(values):
    return leak_slope * values + (1.0 - leak_slope) * values * jax.nn.sigmoid(values)


def slope_of(values):
    sigmoid_value = jax.nn.sigmoid(values)
    return leak_slope + (1.0 - leak_slope) * (
        sigmoid_value + values * sigmoid_value * (1.0 - sigmoid_value)
    )


ROWS, RING, CORES = 4, 8, 2
IN_VMEM = pl.BlockSpec(memory_space=pltpu.VMEM)
IN_HBM = pl.BlockSpec(memory_space=pltpu.HBM)
GRANT = pltpu.CompilerParams(vmem_limit_bytes=16 * 2**20)


def shifted(block, by_row, by_col, row_len):
    moved = block.astype(jnp.float32)
    lane = lax.broadcasted_iota(jnp.int32, moved.shape, 1)
    moved = pltpu.roll(moved, by_row * row_len + by_col, 1)
    keep = None
    if by_row:
        keep = lane >= row_len
    if by_col:
        inner = lane % row_len != 0
        keep = inner if keep is None else jnp.logical_and(keep, inner)
    return jnp.where(keep, moved, 0.0).astype(block.dtype)


def conv_kernel(row_len, w_from, planes_ref, ahead_ref, part_ref, cols_ref, w_ref, sem):
    copy = pltpu.make_async_copy(w_from, w_ref, sem)
    copy.start()
    cells = planes_ref.shape[2]
    channels = planes_ref.shape[1] // 16
    tap_rows = 9 * channels
    for plane in range(2):
        for row in range(-1, 4):
            for col in range(-1, 4):
                source = ((row % 4) * 4 + col % 4) * channels
                block = planes_ref[plane, source : source + channels, :]
                if row < 0 or col < 0:
                    block = shifted(block, int(row < 0), int(col < 0), row_len)
                for row_phase in range(2):
                    row_tap = row + 1 - 2 * row_phase
                    if not 0 <= row_tap <= 2:
                        continue
                    for col_phase in range(2):
                        col_tap = col + 1 - 2 * col_phase
                        if not 0 <= col_tap <= 2:
                            continue
                        start = plane * tap_rows + (row_tap * 3 + col_tap) * channels
                        phase = row_phase * 2 + col_phase
                        put = slice(phase * cells, (phase + 1) * cells)
                        cols_ref[start : start + channels, put] = block
    copy.wait()
    over_rows = (((0,), (0,)), ((), ()))
    for out_ref, weights, cols in (
        (ahead_ref, w_ref[:tap_rows, :], cols_ref[tap_rows:, :]),
        (part_ref, w_ref[tap_rows:, :], cols_ref[...]),
    ):
        total = lax.dot_general(weights, cols, over_rows, preferred_element_type=jnp.float32)
        for phase in range(4):
            out_ref[phase] = total[:, phase * cells : (phase + 1) * cells].astype(out_ref.dtype)


def conv(w_rows, planes, row_len):
    depth, outs = w_rows.shape
    cells = planes.shape[2]
    return pl.pallas_call(
        functools.partial(conv_kernel, row_len),
        out_shape=(
            jax.ShapeDtypeStruct((4, outs, cells), jnp.bfloat16),
            jax.ShapeDtypeStruct((4, outs, cells), jnp.float32),
        ),
        in_specs=[IN_HBM, IN_VMEM],
        out_specs=(IN_VMEM,) * 2,
        scratch_shapes=[
            pltpu.VMEM((2 * depth // 3, 4 * cells), jnp.bfloat16),
            pltpu.VMEM(w_rows.shape, jnp.bfloat16),
            pltpu.SemaphoreType.DMA(()),
        ],
        compiler_params=GRANT,
        cost_estimate=pl.CostEstimate(
            flops=8 * outs * depth * cells, bytes_accessed=4 * depth * cells, transcendentals=0
        ),
    )(w_rows, planes)


def regrouped(values, own, at):
    outs = values.shape[0]
    starts = range(at * own, outs, outs // ROWS)
    return jnp.concatenate([values[start : start + own] for start in starts], 0)


def pointwise_kernel(rule, part_ref, behind_ref, result_ref):
    groups, rows, _ = result_ref.shape
    unit = rows // 4
    for phase in range(4):
        values = rule(part_ref[phase] + behind_ref[phase].astype(jnp.float32))
        for at in range(groups):
            block = regrouped(values, unit // ROWS, at)
            result_ref[at, phase * unit : (phase + 1) * unit, :] = block.astype(result_ref.dtype)


def pointwise(rule, part, behind, groups, dtype):
    phases, outs, cells = part.shape
    return pl.pallas_call(
        functools.partial(pointwise_kernel, rule),
        out_shape=jax.ShapeDtypeStruct((groups, phases * outs // groups, cells), dtype),
        in_specs=[IN_VMEM] * 2,
        out_specs=IN_VMEM,
        compiler_params=GRANT,
        cost_estimate=pl.CostEstimate(
            flops=10 * part.size, bytes_accessed=8 * part.size, transcendentals=part.size
        ),
    )(part, behind)


def pile_kernel(*refs):
    blocks, out_ref, sems = refs[:-2], refs[-2], refs[-1]
    copies = [
        pltpu.make_async_copy(block, out_ref.at[at], sems.at[at]) for at, block in enumerate(blocks)
    ]
    for copy in copies:
        copy.start()
    for copy in copies:
        copy.wait()


def pile(blocks):
    shape = (len(blocks),) + blocks[0].shape
    return pl.pallas_call(
        pile_kernel,
        out_shape=jax.ShapeDtypeStruct(shape, blocks[0].dtype),
        in_specs=[IN_HBM] * len(blocks),
        out_specs=IN_VMEM,
        scratch_shapes=[pltpu.SemaphoreType.DMA((len(blocks),))],
        compiler_params=GRANT,
        cost_estimate=pl.CostEstimate(
            flops=0, bytes_accessed=4 * len(blocks) * blocks[0].size, transcendentals=0
        ),
    )(*blocks)


def spread(block, row_len):
    return jnp.concatenate(
        [block]
        + [shifted(block, by_row, by_col, row_len) for by_row, by_col in ((0, 1), (1, 0), (1, 1))],
        0,
    )


def gather_back(terms, row_len):
    rows = terms.shape[0] // 4
    lane = lax.broadcasted_iota(jnp.int32, (rows, terms.shape[1]), 1)
    cells = terms.shape[1]
    total = terms[:rows]
    for at, (by_row, by_col) in ((1, (0, 1)), (2, (1, 0)), (3, (1, 1))):
        moved = pltpu.roll(terms[at * rows : (at + 1) * rows], cells - by_row * row_len - by_col, 1)
        keep = lane < cells - row_len if by_row else None
        if by_col:
            inner = lane % row_len != row_len - 1
            keep = inner if keep is None else jnp.logical_and(keep, inner)
        total = total + jnp.where(keep, moved, 0.0)
    return total


def cot_copies(place_ref, mine, theirs_ref, cot_ref, sems):
    ring = len(mine)
    half = cot_ref.shape[3] // 2
    z, core = place_ref[1], place_ref[2]
    here = pl.ds(pl.multiple_of(core * half, 128), half)
    there = pl.ds(pl.multiple_of((1 - core) * half, 128), half)
    copies = []
    for k in range(ring):
        to = lax.rem(z + k, ring)
        for side, (source, part) in enumerate(((mine[k], here), (theirs_ref.at[k], there))):
            copies.append(
                pltpu.make_async_copy(source, cot_ref.at[:, to, :, part], sems.at[2 * k + side])
            )
    return copies


def grad_kernel(row_len, place_ref, hidden_ref, *refs):
    mine, theirs_ref, refs = refs[:RING], refs[RING], refs[RING + 1 :]
    outs_refs, (cot_ref, sems, even_ref, odd_ref, sum_ref) = refs[:-5], refs[-5:]
    copies = cot_copies(place_ref, mine, theirs_ref, cot_ref, sems)
    for copy in copies:
        copy.start()
    planes, group, cells = hidden_ref.shape
    steps = planes // 2
    own = group // 4
    unit = own // len(outs_refs)
    for s in range(steps):
        here = slice(s * cells, (s + 1) * cells)
        even_ref[:, here] = spread(hidden_ref[2 * s], row_len)
        odd_ref[:, here] = spread(hidden_ref[2 * s + 1], row_len)
    for copy in copies:
        copy.wait()
    over_cells = (((1,), (1,)), ((), ()))
    sources = ((odd_ref, cells), (even_ref, 0), (odd_ref, 0))
    for depth_tap, (rows_ref, start) in enumerate(sources):
        total = lax.dot_general(
            rows_ref[...],
            cot_ref[:, :, :, start : start + steps * cells].reshape(-1, steps * cells),
            over_cells,
            preferred_element_type=jnp.float32,
        )
        for row_tap in range(3):
            for col_tap in range(3):
                at = (2 * int(row_tap == 0) + int(col_tap == 0)) * group
                at += (2 * int(row_tap != 1) + int(col_tap != 1)) * own
                put = ((depth_tap * 3 + row_tap) * 3 + col_tap) * unit
                for y in range(len(outs_refs)):
                    first = at + y * unit
                    sum_ref[y, put : put + unit, :] = total[first : first + unit, :]
    for away, out_ref in enumerate(outs_refs):
        y = lax.rem(place_ref[0] + away, len(outs_refs))
        out_ref[...] = sum_ref[y].astype(out_ref.dtype)


def grad(place, hidden, mine, theirs, row_len):
    planes, group, cells = hidden.shape
    cot_shape = mine[0].shape[:1] + (RING,) + mine[0].shape[1:2] + (2 * mine[0].shape[2],)
    outs = cot_shape[0] * cot_shape[1] * cot_shape[2]
    rows = pltpu.VMEM((4 * group, planes // 2 * cells), jnp.bfloat16)
    size = 27 * group // (4 * ROWS)
    return pl.pallas_call(
        functools.partial(grad_kernel, row_len),
        out_shape=[
            jax.ShapeDtypeStruct((size, outs), jnp.bfloat16 if away else jnp.float32)
            for away in range(ROWS)
        ],
        in_specs=[pl.BlockSpec(memory_space=pltpu.SMEM), IN_VMEM] + [IN_HBM] * (RING + 1),
        out_specs=[IN_VMEM] * ROWS,
        scratch_shapes=[
            pltpu.VMEM(cot_shape, jnp.bfloat16),
            pltpu.SemaphoreType.DMA((2 * RING,)),
            rows,
            rows,
            pltpu.VMEM((ROWS, size, outs), jnp.float32),
        ],
        compiler_params=GRANT,
        cost_estimate=pl.CostEstimate(
            flops=12 * group * outs * planes * cells, bytes_accessed=2**22, transcendentals=0
        ),
    )(place, hidden, *mine, theirs)


def moves_kernel(place_ref, *refs):
    w_refs, (moves_ref, rows_ref) = refs[:-2], refs[-2:]
    for away, w_ref in enumerate(w_refs):
        rows_ref[lax.rem(place_ref[0] + away, ROWS)] = w_ref[...].astype(jnp.float32)
    own = w_refs[0].shape[0] // 27
    block = ROWS * own
    group = 4 * block
    moves_ref[...] = jnp.zeros_like(moves_ref)
    for tap in range(27):
        depth_tap, row_tap, col_tap = tap // 9, tap // 3 % 3, tap % 3
        at = (4 * depth_tap + 2 * int(row_tap == 0) + int(col_tap == 0)) * group
        at += (2 * int(row_tap != 1) + int(col_tap != 1)) * block
        pieces = [rows_ref[row, tap * own : (tap + 1) * own, :] for row in range(ROWS)]
        moves_ref[at : at + block, :] = jnp.concatenate(pieces, 0).astype(moves_ref.dtype)


def moves_of(place, w_rel):
    size, outs = w_rel[0].shape
    return pl.pallas_call(
        moves_kernel,
        out_shape=jax.ShapeDtypeStruct((48 * ROWS * size // 27, outs), jnp.bfloat16),
        in_specs=[pl.BlockSpec(memory_space=pltpu.SMEM)] + [IN_VMEM] * ROWS,
        out_specs=IN_VMEM,
        scratch_shapes=[pltpu.VMEM((ROWS, size, outs), jnp.float32)],
        compiler_params=GRANT,
        cost_estimate=pl.CostEstimate(flops=0, bytes_accessed=2**20, transcendentals=0),
    )(place, *w_rel)


def back_kernel(row_len, place_ref, moves_ref, *refs):
    mine, theirs_ref, (out_ref, cot_ref, sems) = refs[:RING], refs[RING], refs[RING + 1 :]
    planes, group, cells = out_ref.shape
    size = 4 * group
    copies = cot_copies(place_ref, mine, theirs_ref, cot_ref, sems)
    for copy in copies:
        copy.start()
    for copy in copies:
        copy.wait()

    def one(at, start):
        return jnp.dot(
            moves_ref[at * size : (at + 1) * size, :],
            cot_ref[:, :, :, start : start + cells].reshape(-1, cells),
            preferred_element_type=jnp.float32,
        )

    for s in range(planes // 2):
        start = s * cells
        out_ref[2 * s] = gather_back(one(1, start), row_len).astype(out_ref.dtype)
        odd = one(2, start) + one(0, start + cells)
        out_ref[2 * s + 1] = gather_back(odd, row_len).astype(out_ref.dtype)


def back(place, moves, mine, theirs, planes, row_len):
    rows, outs = moves.shape
    group = rows // 12
    cot_shape = mine[0].shape[:1] + (RING,) + mine[0].shape[1:2] + (2 * mine[0].shape[2],)
    cells = cot_shape[3] // (planes // 2 + 1)
    return pl.pallas_call(
        functools.partial(back_kernel, row_len),
        out_shape=jax.ShapeDtypeStruct((planes, group, cells), jnp.bfloat16),
        in_specs=[pl.BlockSpec(memory_space=pltpu.SMEM), IN_VMEM] + [IN_HBM] * (RING + 1),
        out_specs=IN_VMEM,
        scratch_shapes=[
            pltpu.VMEM(cot_shape, jnp.bfloat16),
            pltpu.SemaphoreType.DMA((2 * RING,)),
        ],
        compiler_params=GRANT,
        cost_estimate=pl.CostEstimate(
            flops=12 * group * outs * planes * cells, bytes_accessed=2**22, transcendentals=0
        ),
    )(place, moves, *mine, theirs)


def parts_kernel(cot_ref, out_ref):
    channels, depth, cells = cot_ref.shape
    share = depth // ROWS
    half = out_ref.shape[2]
    turned = jnp.swapaxes(cot_ref[...].astype(jnp.float32), 0, 1)
    for row in range(ROWS):
        for at in range(share + 1):
            s = row * share + at
            for lane in range(0, cells, 128):
                put = at * cells + lane
                if s < depth:
                    block = turned[s, :, lane : lane + 128].astype(out_ref.dtype)
                else:
                    block = jnp.zeros((channels, 128), out_ref.dtype)
                out_ref[row * CORES + put // half, :, put % half : put % half + 128] = block


def parts_of(cot):
    channels, depth, cells = cot.shape
    half = (depth // ROWS + 1) * cells // CORES
    return pl.pallas_call(
        parts_kernel,
        out_shape=jax.ShapeDtypeStruct((ROWS * CORES, channels, half), cot.dtype),
        in_specs=[IN_VMEM],
        out_specs=IN_VMEM,
        compiler_params=GRANT,
        cost_estimate=pl.CostEstimate(flops=0, bytes_accessed=4 * cot.size, transcendentals=0),
    )(cot)


def total_kernel(own_ref, left_ref, opposite_ref, right_ref, out_ref):
    f32 = jnp.float32
    across = own_ref[...].astype(f32) + opposite_ref[...].astype(f32)
    total = across + (left_ref[...].astype(f32) + right_ref[...].astype(f32))
    taps, own, _ = out_ref.shape
    for tap in range(taps):
        out_ref[tap] = total[tap * own : (tap + 1) * own, :]


def total_of(own, left, opposite, right):
    rows, outs = own.shape
    return pl.pallas_call(
        total_kernel,
        out_shape=jax.ShapeDtypeStruct((27, rows // 27, outs), jnp.float32),
        in_specs=[IN_VMEM] * 4,
        out_specs=IN_VMEM,
        compiler_params=GRANT,
        cost_estimate=pl.CostEstimate(
            flops=3 * own.size, bytes_accessed=12 * own.size, transcendentals=0
        ),
    )(own, left, opposite, right)


def on_space(block, y_by=0, z_by=0, core_by=0):
    route = []
    for y in range(ROWS):
        for z in range(RING):
            for core in range(CORES):
                to = ((y + y_by) % ROWS, (z + z_by) % RING, (core + core_by) % CORES)
                route.append(((y * RING + z) * CORES + core, (to[0] * RING + to[1]) * CORES + to[2]))
    return lax.ppermute(block, "space", route)


CHIPS = [(y, z) for y in range(ROWS) for z in range(RING)]


def members(pick):
    groups = {}
    for y, z in CHIPS:
        for core in range(CORES):
            groups.setdefault(pick(y, z, core), []).append((y * RING + z) * CORES + core)
    return list(groups.values())


COLUMNS = members(lambda y, z, core: (z, core))
PILLARS = members(lambda y, z, core: z)
SLABS = members(lambda y, z, core: y)


def exchange(blocks, groups):
    return lax.all_to_all(
        blocks, "space", split_axis=0, concat_axis=0, axis_index_groups=groups, tiled=True
    )


def section(volume, w_first, w_second, cotangent):
    channels = volume.shape[1]
    cells = volume.shape[4]
    outs = w_first.shape[4]
    own = w_second.shape[3]
    row_len = WID // 4
    me = lax.axis_index("space")
    y, z, core = me // (RING * CORES), me // CORES % RING, me % CORES
    place = jnp.stack([y, z, core]).astype(jnp.int32)
    group = RING * CORES

    parts = parts_of(cotangent[0])
    first = exchange(parts, PILLARS)
    first = first.reshape(ROWS, -1, first.shape[2])
    hops = {0: first}
    for step in (1, -1, 2, -2):
        hops[step] = on_space(first, z_by=-step)
    for step, come in ((3, 2), (-3, -2), (4, 2)):
        hops[step] = on_space(hops[come], z_by=come - step)
    mine = [hops[step] for step in (0, 1, 2, 3, 4, -3, -2, -1)]
    piled = pile(mine)
    theirs = on_space(piled, core_by=1)

    w_rel = [w_second.reshape(27 * own, C3)]
    for step in range(1, ROWS):
        w_rel.append(on_space(w_rel[0], y_by=-step))

    planes = volume[0].transpose(1, 2, 0, 3).reshape(2, 16 * channels, cells)
    w_rows = w_first.reshape(27 * channels, outs)
    ahead, part = conv(w_rows, planes, row_len)
    behind = from_behind(ahead, "space", 1)
    hidden = pointwise(activate, part, behind, group, jnp.bfloat16)
    slopes = pointwise(slope_of, part, behind, group, jnp.float32)
    by_plane = exchange(hidden, SLABS)

    moves = moves_of(place, w_rel)
    back_terms = back(place, moves, mine, theirs, group, row_len)
    hidden_grad = exchange(back_terms, SLABS)

    partial, *others = grad(place, by_plane, mine, theirs, row_len)
    for step, block in enumerate(others, 1):
        partial = partial + on_space(block, y_by=step).astype(jnp.float32)
    partial = partial.astype(jnp.bfloat16)
    sides = []
    for distance in (1, 2, 3):
        sides.append(from_side(partial, "dp", distance))
    grad_second = total_of(partial, *sides)
    grad_second = grad_second.reshape(3, 3, 3, own, C3)

    pre_grad = (hidden_grad.astype(jnp.float32) * slopes).astype(jnp.bfloat16)
    pre_grad = pre_grad.reshape(group, 4, ROWS, own, cells).transpose(2, 0, 3, 1, 4)
    pre_grad = pre_grad.reshape(1, outs, 1, 4, cells)
    return (grad_second, pre_grad)


def solution(mesh):
    in_specs = (
        P("dp", None, "space", None, None),
        P(),
        P(None, None, None, "space", None),
        P("dp", "space", None, None),
    )
    out_specs = (P(None, None, None, "space", None), P("dp", None, "space", None, None))
    return jax.shard_map(
        section, mesh=mesh, in_specs=in_specs, out_specs=out_specs, check_vma=False
    )
```
